256 devices in a mesh: span: 32 (over y, z), sector: 8 (over x, core).
Axes of the slice: x: 4, y: 4, z: 8, core: 2. Of those that a mesh axis runs over, the one named last changes fastest.
Arguments:
- velocity: float32 [3, 128, 48, 4096], P(None, 'sector', None, 'span'), may hold values from -6 to 6
- current_speed: float32 [16], replicated, may hold values from 0.25 to 1.5
- current_bin: int32 [4096], P('span'), may hold values from 0 to 15
- face_index: int32 [192], P('sector'), may hold values from 0 to 15, as said below
- quad_weight: float32 [192], P('sector'), may hold values from 0.05 to 0.25
- tension: float32 [4096], P('span'), may hold values from 0.25 to 4
- displacement: float32 [2, 4096], P(None, 'span'), may hold values from -12 to 12
- beam_rate: float32 [2, 4096], P(None, 'span'), may hold values from -12 to 12
Outputs:
- fresh_velocity: float32 [3, 128, 48, 4096], P(None, 'sector', None, 'span')
- sectional_force: float32 [2, 4096], P(None, 'span')
- deflection: float32 [2, 4096], P(None, 'span')
The draws below stay inside these ranges and needn't reach their ends.
Inputs may be any that keep to these rules, and one draw needn't show every extreme that they name: `face_index`: a wall face of the quadrature point's own sector, counted within that sector's 16 faces; in every sector some point lies on the first face and some on the last.
All inputs are finite; a program needn't handle non-finite values.
Results may differ from the reference program's by a relative error of at most 0.0075.
Values sent between devices are 32-bit elements; how exact they have to be, the bound alone decides.
A program may use at most 192 MiB of HBM per device.

```python
import math
import jax
import jax.numpy as jnp
from jax import lax

SEC_DEV = 128
CT = 16
NR = 48
QPD = 24
NBIN = 16
NSEC = 4096
NTH = 128
N_SECTOR = 8


def draw_face_index(key, part):
    values = jax.random.randint(jax.random.fold_in(key, 11), (N_SECTOR, QPD), 0, CT, dtype=jnp.int32)
    values = values.at[:, 0].set(CT - 1)
    values = values.at[:, 1].set(0)
    return values.reshape((N_SECTOR * QPD,))


def set_ends(drawn, stream_key, least, top_value):
    longest = drawn.shape.index(max(drawn.shape))
    spots = []
    for shift in (0, 1):
        where = [jax.random.randint(jax.random.fold_in(stream_key, axis), (), 0, length) for axis, length in enumerate(drawn.shape)]
        where[longest] = (where[longest] + shift) % drawn.shape[longest]
        spots.append(tuple(where))
    return drawn.at[spots[0]].set(least).at[spots[1]].set(top_value)


def block_scale(own_key, dims, shards, least, top_value):
    def one(dim, blocks):
        draws = jax.random.uniform(jax.random.fold_in(jax.random.fold_in(own_key, 6), dim), (blocks,), jnp.float32, least / len(shards), top_value / len(shards))
        return jnp.repeat(jnp.exp(draws), dims[dim] // blocks).reshape((-1,) + (1,) * (len(dims) - dim - 1))

    gain = one(*shards[0])
    for cut in shards[1:]:
        gain = gain * one(*cut)
    return gain


def scatter_about(stream_key, shape, deviation, limit, shards=(), kind=jnp.bfloat16):
    drawn = jax.random.normal(stream_key, shape, jnp.float32) * deviation
    if len(shards) > 0:
        drawn = block_scale(stream_key, shape, shards, -0.22, 0.18) * drawn
    return jnp.clip(drawn, min=-limit, max=limit).astype(kind)


def setup_inputs(seed: int = 0) -> dict:
    streams_of = jax.random.split(jax.random.key(seed), 9)
    return {
        "velocity": scatter_about(streams_of[0], (3, NTH, NR, NSEC), 1.0, 6.0, ((1, 8), (3, 32)), jnp.float32),
        "current_speed": jnp.clip(jnp.exp(jax.random.uniform(streams_of[1], (NBIN,), jnp.float32, math.log(0.25), math.log(1.5))), 0.25, 1.5),
        "current_bin": set_ends(jax.random.randint(streams_of[2], (NSEC,), 0, NBIN), jax.random.fold_in(streams_of[2], 1), 0, NBIN - 1).astype(jnp.int32),
        "face_index": draw_face_index(jax.random.fold_in(streams_of[8], 71), 0),
        "quad_weight": jnp.clip(jnp.exp(math.log(0.25) - 1.609438 * jax.random.uniform(streams_of[4], (QPD * N_SECTOR,), jnp.float32) ** block_scale(streams_of[4], (QPD * N_SECTOR,), ((0, 8),), -0.2, 0.2)), 0.05, 0.25),
        "tension": jnp.clip(jnp.exp(math.log(4.0) - 2.7725887 * jax.random.uniform(streams_of[5], (NSEC,), jnp.float32) ** block_scale(streams_of[5], (NSEC,), ((0, 32),), -0.2, 0.2)), 0.25, 4.0),
        "displacement": scatter_about(streams_of[6], (2, NSEC), 3.0, 12.0, ((1, 32),), jnp.float32),
        "beam_rate": scatter_about(streams_of[7], (2, NSEC), 3.0, 12.0, ((1, 32),), jnp.float32),
    }


NU_DT = 0.15
ADV_DT = 0.1
WALL_NU = 0.5
BEAM_EI = 0.5
BEAM_MASS = 0.4


def pair_block(a, b, c, d):
    return jnp.stack([jnp.stack([a, b], -1), jnp.stack([c, d], -1)], -2)


def block_product(a, b):
    return a[..., :, 0:1] * b[..., 0:1, :] + a[..., :, 1:2] * b[..., 1:2, :]


def invert_block(a):
    determinant = a[..., 0, 0] * a[..., 1, 1] - a[..., 0, 1] * a[..., 1, 0]
    return pair_block(a[..., 1, 1], -a[..., 0, 1], -a[..., 1, 0], a[..., 0, 0]) / determinant[..., None, None]


def element_blocks(tension_values):
    geo_part = tension_values / 30.0
    stiff_aa = pair_block(12.0 * BEAM_EI + 36.0 * geo_part, 6.0 * BEAM_EI + 3.0 * geo_part, 6.0 * BEAM_EI + 3.0 * geo_part, 4.0 * BEAM_EI + 4.0 * geo_part)
    stiff_ab = pair_block(-12.0 * BEAM_EI - 36.0 * geo_part, 6.0 * BEAM_EI + 3.0 * geo_part, -6.0 * BEAM_EI - 3.0 * geo_part, 2.0 * BEAM_EI - geo_part)
    stiff_ba = pair_block(-12.0 * BEAM_EI - 36.0 * geo_part, -6.0 * BEAM_EI - 3.0 * geo_part, 6.0 * BEAM_EI + 3.0 * geo_part, 2.0 * BEAM_EI - geo_part)
    stiff_bb = pair_block(12.0 * BEAM_EI + 36.0 * geo_part, -6.0 * BEAM_EI - 3.0 * geo_part, -6.0 * BEAM_EI - 3.0 * geo_part, 4.0 * BEAM_EI + 4.0 * geo_part)
    return stiff_aa, stiff_ab, stiff_ba, stiff_bb


def block_thomas(diag_block, lower_block, upper_block, load_columns):
    def forward(carried, entries):
        couple_prev, solved_prev = carried
        d, l, u, f = entries
        pivot_block = d - block_product(l, couple_prev)
        inverse = invert_block(pivot_block)
        solved = block_product(inverse, f - block_product(l, solved_prev))
        couple = block_product(inverse, u)
        return (couple, solved), (couple, solved)

    start = (jnp.zeros((2, 2), jnp.float32), jnp.zeros(load_columns.shape[1:], jnp.float32))
    unused, (couples, solveds) = lax.scan(forward, start, (diag_block, lower_block, upper_block, load_columns))

    def backward(later_value, entries):
        couple, solved = entries
        top_here = solved - block_product(couple, later_value)
        return top_here, top_here

    unused_last, solution = lax.scan(backward, jnp.zeros(load_columns.shape[1:], jnp.float32), (couples, solveds), reverse=True)
    return solution


def far_field(angles, current_at):
    along = -current_at[None, :] * jnp.sin(angles)[:, None]
    across = current_at[None, :] * jnp.cos(angles)[:, None]
    return jnp.stack([along, across, jnp.zeros_like(along)], 0)[:, :, None, :]


def widen_radial(field, outer_row):
    return jnp.concatenate([-field[:, :, :1], field, outer_row], axis=2)


def segment_rates(padded):
    centre = padded[:, 1:-1, 1:-1, 1:-1]
    theta_up = padded[:, 2:, 1:-1, 1:-1]
    theta_down = padded[:, :-2, 1:-1, 1:-1]
    radial_up = padded[:, 1:-1, 2:, 1:-1]
    radial_down = padded[:, 1:-1, :-2, 1:-1]
    span_up = padded[:, 1:-1, 1:-1, 2:]
    span_down = padded[:, 1:-1, 1:-1, :-2]
    laplace = (theta_up + theta_down - 2.0 * centre) + (radial_up + radial_down - 2.0 * centre) + (span_up + span_down - 2.0 * centre)
    advect = centre[0:1] * (theta_up - theta_down) + centre[1:2] * (radial_up - radial_down) + centre[2:3] * (span_up - span_down)
    return NU_DT * laplace - 0.5 * ADV_DT * advect


def wall_traction(wall_cells, angles):
    cosine = jnp.cos(angles)[:, None]
    sine = jnp.sin(angles)[:, None]
    along = wall_cells[0]
    normal = wall_cells[1]
    force_x = 2.0 * WALL_NU * (normal * cosine - along * sine)
    force_y = 2.0 * WALL_NU * (normal * sine + along * cosine)
    return jnp.stack([force_x, force_y], 0)


def reference(velocity, current_speed, current_bin, face_index, quad_weight, tension, displacement, beam_rate):
    angles = 2.0 * math.pi * (jnp.arange(NTH, dtype=jnp.int32).astype(jnp.float32) + 0.5) / NTH
    choose = (current_bin[:, None] == jnp.arange(NBIN, dtype=jnp.int32)[None, :]).astype(jnp.float32)
    current_at = jnp.sum(choose * current_speed[None, :], axis=1)
    outer_row = far_field(angles, current_at)

    def rates_of(field):
        radial = widen_radial(field, outer_row)
        beside_all = jnp.concatenate([radial[:, -1:], radial, radial[:, :1]], axis=1)
        padded = jnp.concatenate([beside_all[..., :1], beside_all, beside_all[..., -1:]], axis=3)
        return segment_rates(padded)

    first_rates = rates_of(velocity)
    second_rates = rates_of(velocity + first_rates)
    fresh_velocity = velocity + 0.5 * (first_rates + second_rates)

    traction = wall_traction(fresh_velocity[:, :, 0, :], angles)
    owner = jnp.arange(QPD * N_SECTOR, dtype=jnp.int32) // QPD
    faces = owner * CT + face_index
    quad_table = (faces[:, None] == jnp.arange(NTH, dtype=jnp.int32)[None, :]).astype(jnp.float32) * quad_weight[:, None]
    sectional_force = jnp.einsum("qf,cfk->ck", quad_table, traction, precision=lax.Precision.HIGHEST)

    mass_value = BEAM_MASS / SEC_DEV ** 2
    mass_block = jnp.array([[mass_value, 0.0], [0.0, 0.0]], jnp.float32)
    next_tension = jnp.concatenate([tension[1:], jnp.zeros((1,), jnp.float32)])
    exists = (jnp.arange(NSEC, dtype=jnp.int32) < NSEC - 1).astype(jnp.float32)[:, None, None]
    own_aa, own_ab, own_ba, own_bb = element_blocks(tension)
    next_aa, next_ab, next_ba, next_bb = element_blocks(next_tension)
    diag_block = own_bb + next_aa * exists + mass_block
    upper_block = next_ab * exists
    deflect_load = sectional_force.T * SEC_DEV ** -1.5 + mass_value * (displacement + beam_rate).T
    load_columns = jnp.stack([deflect_load, jnp.zeros_like(deflect_load)], axis=1)
    solution = block_thomas(diag_block, own_ba, upper_block, load_columns)
    deflection = solution[:, 0, :].T
    return fresh_velocity, sectional_force, deflection
```

```python
import math

import jax
import jax.numpy as jnp
from jax import lax
from jax.experimental import pallas as pl
from jax.experimental.pallas import tpu as pltpu
from jax.sharding import PartitionSpec as P

MESH = pl.DeviceIdType.MESH
NU_DT = 0.15
ADV_DT = 0.1
WALL_NU = 0.5
BEAM_EI = 0.5
BEAM_MASS = 0.4
LANES = 128


def roll(x, shift, axis=1):
    size = x.shape[axis]
    return pltpu.roll(x, shift % size if isinstance(shift, int) else shift, axis)


def lane_iota(rows):
    return lax.broadcasted_iota(jnp.int32, (rows, LANES), 1)


def row_iota(rows):
    return lax.broadcasted_iota(jnp.int32, (rows, LANES), 0)


def reduce_chain(A, D, F, rho_of, strides):
    A00, A01, A10, A11 = A
    D00, D01, D11 = D
    Fw, Fs = F
    steps = []
    for s in strides:
        inv = 1.0 / (D00 * D11 - D01 * D01)
        I00, I01, I11 = D11 * inv, -D01 * inv, D00 * inv
        P00 = I00 * A00 + I01 * A10
        P01 = I00 * A01 + I01 * A11
        P10 = I01 * A00 + I11 * A10
        P11 = I01 * A01 + I11 * A11
        E11 = A01 * P01 + A11 * P11
        I00m, I01m, I11m = roll(I00, s), roll(I01, s), roll(I11, s)
        al00 = A00 * I00m + A01 * I01m
        al01 = A00 * I01m + A01 * I11m
        al10 = A10 * I00m + A11 * I01m
        al11 = A10 * I01m + A11 * I11m
        ga00, ga01, ga10, ga11 = roll(P00, -s), roll(P10, -s), roll(P01, -s), roll(P11, -s)
        steps.append((al00, al01, al10, al11, ga00, ga01, ga10, ga11))
        P00m, P01m, P10m, P11m = roll(P00, s), roll(P01, s), roll(P10, s), roll(P11, s)
        D11 = D11 - (al10 * A10 + al11 * A11) - roll(E11, -s)
        Fw, Fs = reduce_load(steps[-1], Fw, Fs, s)
        A00, A01, A10, A11 = (
            -(A00 * P00m + A01 * P10m),
            -(A00 * P01m + A01 * P11m),
            -(A10 * P00m + A11 * P10m),
            -(A10 * P01m + A11 * P11m),
        )
        rw, rs = rho_of(Fw, Fs)
        D00 = rw - A00 - roll(A00, -2 * s)
        D01 = rs - A10 - roll(A01, -2 * s)
    inv = 1.0 / (D00 * D11 - D01 * D01)
    last = (D11 * inv, -D01 * inv, D00 * inv)
    return last[0] * Fw + last[1] * Fs, last[1] * Fw + last[2] * Fs, steps, last


def reduce_load(step, Fw, Fs, s):
    al00, al01, al10, al11, ga00, ga01, ga10, ga11 = step
    Fwm, Fsm, Fwp, Fsp = roll(Fw, s), roll(Fs, s), roll(Fw, -s), roll(Fs, -s)
    return (
        Fw - (al00 * Fwm + al01 * Fsm) - (ga00 * Fwp + ga01 * Fsp),
        Fs - (al10 * Fwm + al11 * Fsm) - (ga10 * Fwp + ga11 * Fsp),
    )


def slab_system(t, mass):
    lane = lane_iota(1)
    g = t / 30.0
    gn = roll(g, -1)
    a00, a01, a10, a11 = (
        -12.0 * BEAM_EI - 36.0 * g,
        -6.0 * BEAM_EI - 3.0 * g,
        6.0 * BEAM_EI + 3.0 * g,
        2.0 * BEAM_EI - g,
    )
    n00, n01, n10, n11 = roll(a00, -1), roll(a01, -1), roll(a10, -1), roll(a11, -1)
    d00 = (12.0 * BEAM_EI + 36.0 * g) + (12.0 * BEAM_EI + 36.0 * gn) + mass
    d01 = (-6.0 * BEAM_EI - 3.0 * g) + (6.0 * BEAM_EI + 3.0 * gn)
    d11 = (4.0 * BEAM_EI + 4.0 * g) + (4.0 * BEAM_EI + 4.0 * gn)
    inside = lane < LANES - 1
    rho_w = jnp.where(inside, (d00 - jnp.maximum(-a00, -n00)) - jnp.minimum(-a00, -n00), 0.0)
    rho_s = jnp.where(inside, (d01 + a10) + n01, 0.0)
    first, last, end = lane == 0, lane == LANES - 2, lane == LANES - 1
    zero = jnp.zeros_like(t)
    row = row_iota(8)

    def stack(rows):
        out = jnp.zeros((8, LANES), jnp.float32)
        for index, value in enumerate(rows):
            out = jnp.where(row == index, value, out)
        return out

    Fw = stack(
        [
            rho_w,
            jnp.where(first, -a00, zero),
            jnp.where(first, -a01, zero),
            jnp.where(last, -n00, jnp.where(end, 1.0, zero)),
            jnp.where(last, -n10, zero),
        ]
    )
    Fs = stack(
        [
            rho_s,
            jnp.where(first, -a10, zero),
            jnp.where(first, -a11, zero),
            jnp.where(last, -n01, zero),
            jnp.where(last, -n11, jnp.where(end, 1.0, zero)),
        ]
    )
    coupled = jnp.logical_and(lane > 0, inside)
    A = tuple(jnp.where(coupled, x, 0.0) for x in (a00, a01, a10, a11))
    D = (jnp.where(inside, d00, 1.0), jnp.where(inside, d01, 0.0), jnp.where(inside, d11, 1.0))

    def rho_of(Fw, Fs):
        return Fw[0:1] + Fw[1:2] + Fw[3:4], Fs[0:1] + Fs[1:2] + Fs[3:4]

    Zw, Zs, steps, inverse = reduce_chain(A, D, (Fw, Fs), rho_of, [1 << b for b in range(7)])
    yw, ys = Zw[0:1], Zs[0:1]
    xa1w, xa1s = Zw[2:3], Zs[2:3]
    xb0w, xb0s, xb1w, xb1s = Zw[3:4], Zs[3:4], Zw[4:5], Zs[4:5]
    numbers = [
        (0, xb0w * a00 + xb0s * a10),
        (0, xb0w * a01 + xb0s * a11),
        (0, xb1w * a00 + xb1s * a10),
        (0, xb1w * a01 + xb1s * a11),
        (0, -(a00 * yw + a10 * ys)),
        (0, -(a01 * yw + a11 * ys)),
        (0, (4.0 * BEAM_EI + 4.0 * g) + (a01 * xa1w + a11 * xa1s)),
        (LANES - 2, -(n00 * yw + n01 * ys)),
        (LANES - 2, -(n10 * yw + n11 * ys)),
        (LANES - 2, (4.0 * BEAM_EI + 4.0 * gn) + (n10 * xb1w + n11 * xb1s)),
    ]
    row16 = row_iota(16)
    table = jnp.zeros((16, LANES), jnp.float32)
    for index, (spot, value) in enumerate(numbers):
        table = jnp.where((row16 == index) & (lane == spot), value, table)
    column = jnp.sum(table, axis=1, keepdims=True)
    message = jnp.sum(jnp.where(lane_iota(16) == row16, column, 0.0), axis=0, keepdims=True)
    answers = jnp.zeros((8, LANES), jnp.float32)
    for u in range(4):
        answers = jnp.where(row // 2 == u, Zw[u + 1 : u + 2], answers)
    return message, answers, steps, inverse


def chain_response(numbers, count, place, mass):
    lane = lane_iota(1)
    valid = lane < count
    row = row_iota(8)
    pick = lambda n: jnp.where(valid, numbers[n : n + 1], 0.0)
    a00, a01, a10, a11 = pick(0), pick(1), pick(2), pick(3)
    raw, ras, ka11, rbw, rbs, kb11 = [pick(n) for n in range(4, 10)]
    above = lambda x: jnp.where(lane < count - 1, roll(x, -1), 0.0)
    first = lane == 0
    rw = rbw + above(raw) + mass - jnp.where(first, a00, 0.0)
    rs = rbs + above(ras) - jnp.where(first, a10, 0.0)
    rw = jnp.where(valid, rw, 1.0)
    rs = jnp.where(valid, rs, 0.0)
    d11 = jnp.where(valid, kb11 + above(ka11), 1.0)
    A = tuple(jnp.where(first, 0.0, x) for x in (a00, a01, a10, a11))
    d00 = rw - A[0] - roll(A[0], -1)
    d01 = rs - A[2] - roll(A[1], -1)
    lane8 = lane_iota(8)
    mine = lane8 == place
    before = lane8 == place - 1
    Fw = jnp.where((before & (row == 0)) | (mine & (row == 2)), 1.0, 0.0)
    Fs = jnp.where((before & (row == 1)) | (mine & (row == 3)), 1.0, 0.0)
    Fw = jnp.where(row == 4, rw, Fw)
    Fs = jnp.where(row == 4, rs, Fs)
    strides = []
    while (1 << len(strides)) < count:
        strides.append(1 << len(strides))
    Gw, Gs, _, _ = reduce_chain(
        A, (d00, d01, d11), (Fw, Fs), lambda w, s: (w[4:5], s[4:5]), strides
    )
    Hw, Hs = roll(Gw, 1), roll(Gs, 1)
    blocks = []
    for u in range(4):
        block = jnp.where(row // 2 == 0, Hw[u : u + 1], 0.0)
        block = jnp.where(row // 2 == 1, Hs[u : u + 1], block)
        block = jnp.where(row // 2 == 2, Gw[u : u + 1], block)
        blocks.append(jnp.where(row // 2 == 3, Gs[u : u + 1], block))
    return blocks


def wide_loads(load):
    row = row_iota(8)
    return jnp.where(row % 2 == 0, load[0:1], load[1:2])


def end_loads(answers, load8):
    total = jnp.sum(answers * load8, axis=1, keepdims=True)
    lane = lane_iota(8)
    keep = (lane % 8 == row_iota(8)) & (lane < 32)
    return jnp.sum(jnp.where(keep, total, 0.0), axis=0, keepdims=True)


def ends_solved(response, loads):
    total = jnp.sum(response * loads, axis=0, keepdims=True)
    lane, row = lane_iota(8), row_iota(8)
    keep = (lane // 8 == row // 2) & (lane % 2 == row % 2) & (lane < 32)
    return jnp.sum(jnp.where(keep, total, 0.0), axis=1, keepdims=True)


def inner_deflection(steps, inverse, load8):
    inside = lane_iota(8) < LANES - 1
    Fw, Fs = jnp.where(inside, load8, 0.0), jnp.zeros((8, LANES), jnp.float32)
    for b in range(7):
        Fw, Fs = reduce_load(steps[b], Fw, Fs, 1 << b)
    return inverse[0] * Fw + inverse[1] * Fs


def kernel(
    count,
    ring,
    vel,
    speed,
    cbin,
    face,
    weight,
    tens,
    disp,
    rate,
    out,
    force_out,
    defl_out,
    V,
    U,
    W,
    TR,
    TL,
    near,
    full,
    PG,
    UG,
    FB,
    KB,
    RB,
    coef,
    OV,
    own_sem,
    send_sem,
    theta_sem,
    near_sem,
    full_sem,
    force_sem,
    stiff_sem,
    load_sem,
    out_sem,
):
    cells, rows = vel.shape[1], vel.shape[2]
    tiles = rows // 8
    base = 8
    k = lax.axis_index("span")
    s = lax.axis_index("sector")
    left, right = lax.rem(k + count - 1, count), lax.rem(k + 1, count)
    lower, upper = lax.rem(s + ring - 1, ring), lax.rem(s + 1, ring)
    low_end = jnp.where(k == 0, 1, 0)
    high_end = jnp.where(k == count - 1, 1, 0)
    mass = BEAM_MASS / LANES**2
    stride = cells + 2
    group = 2 * stride

    own_wall = pltpu.make_async_copy(
        vel.at[:, :, pl.ds(0, 8), :],
        V.at[:, pl.ds(2, cells), pl.ds(base, 8), :],
        own_sem.at[0],
    )
    own_bulk = pltpu.make_async_copy(
        vel.at[:, :, pl.ds(8, rows - 8), :],
        V.at[:, pl.ds(2, cells), pl.ds(base + 8, rows - 8), :],
        own_sem.at[1],
    )
    own_wall.start()
    own_bulk.start()

    barrier = pltpu.get_barrier_semaphore()

    def greet(span, sector):
        pl.semaphore_signal(
            barrier, inc=1, device_id={"span": span, "sector": sector}, device_id_type=MESH
        )

    for side in (left, right):
        for turn in (lower, upper):
            greet(side, turn)

    @pl.loop(1, ring)
    def _(d):
        greet(k, lax.rem(s + d, ring))

    @pl.loop(1, count)
    def _(d):
        greet(lax.rem(k + d, count), s)

    lane = lane_iota(1)
    row8 = row_iota(8)
    current = jnp.zeros((1, LANES), jnp.float32)
    for b in range(speed.shape[0]):
        current = current + jnp.where(cbin[...] == b, speed[b], 0.0)
    total_cells = cells * ring

    def angle_of(index):
        whole = lax.rem(s * cells + index + total_cells, total_cells)
        return 2.0 * math.pi * (whole.astype(jnp.float32) + 0.5) / total_cells

    ring_angle = angle_of(row_iota(24) - 1)
    ring_sin, ring_cos = jnp.sin(ring_angle), jnp.cos(ring_angle)
    face_row = row_iota(24) - 1
    face_weight = jnp.zeros((24, LANES), jnp.float32)
    for q in range(weight.shape[0]):
        face_weight = face_weight + jnp.where(face_row == face[q], weight[q], 0.0)
    coef[0] = face_weight * ring_cos
    coef[1] = face_weight * ring_sin
    coef[2] = -current * ring_sin
    coef[3] = current * ring_cos
    lane_cell = lax.rem(lane, group) // 2 - 1
    lane_angle = angle_of(lane_cell)
    lane_sin, lane_cos = jnp.sin(lane_angle), jnp.cos(lane_angle)

    message, answers, steps, inverse = slab_system(tens[...], mass)
    KB[pl.ds(k, 1), 0, :] = message
    wide = lane_iota(rows)
    even = wide % 2 == 0

    own_wall.wait()
    own_bulk.wait()
    cur_high = jnp.sum(jnp.where(lane == LANES - 1, current, 0.0), axis=1, keepdims=True)
    cur_low = jnp.sum(jnp.where(lane == 0, current, 0.0), axis=1, keepdims=True)

    TR[...] = jnp.where(wide == 3 * group + 1, cur_high, 0.0)
    TL[...] = jnp.where(wide == 3 * group + 2, cur_low, 0.0)

    @pl.loop(0, cells)
    def _(i):
        high, low = TR[...], TL[...]
        for c in range(3):
            spot = c * group + 2 * (i + 1)
            turned = roll(V[c, i + 2, pl.ds(base, rows), :], spot + 2)
            high = jnp.where(wide // 2 == spot // 2, turned, high)
            low = jnp.where(wide // 2 == spot // 2 + 1, turned, low)
        TR[...] = high
        TL[...] = low

    TL[...] = roll(TL[...], -2)

    pl.semaphore_wait(barrier, 4 + (ring - 1) + (count - 1))

    def remote(src, dst, sent, arrived, span, sector):
        return pltpu.make_async_remote_copy(
            src_ref=src,
            dst_ref=dst,
            send_sem=sent,
            recv_sem=arrived,
            device_id={"span": span, "sector": sector},
            device_id_type=MESH,
        )

    spread = [
        (TR, 0, right, s),
        (TL, 1, left, s),
        (TR, 2, right, upper),
        (TL, 3, left, upper),
        (TR, 4, right, lower),
        (TL, 5, left, lower),
    ]
    near_copies = [
        remote(
            src.at[pl.ds(0, 8), :], near.at[slot], send_sem.at[slot], near_sem.at[slot], span, sector
        )
        for src, slot, span, sector in spread
    ]
    full_copies = [
        remote(src, full.at[slot], send_sem.at[6 + slot], full_sem.at[slot], span, sector)
        for src, slot, span, sector in spread
    ]
    theta_copies = []
    for part, (start, size) in enumerate(((0, 8), (8, rows - 8))):
        theta_copies.append(
            remote(
                vel.at[:, pl.ds(0, 2), pl.ds(start, size), :],
                V.at[:, pl.ds(cells + 2, 2), pl.ds(base + start, size), :],
                send_sem.at[12 + 2 * part],
                theta_sem.at[2 * part],
                k,
                lower,
            )
        )
        theta_copies.append(
            remote(
                vel.at[:, pl.ds(cells - 2, 2), pl.ds(start, size), :],
                V.at[:, pl.ds(0, 2), pl.ds(base + start, size), :],
                send_sem.at[13 + 2 * part],
                theta_sem.at[1 + 2 * part],
                k,
                upper,
            )
        )
    for copy in near_copies[2:] + near_copies[:2] + theta_copies[:2]:
        copy.start()
    for copy in theta_copies[2:] + full_copies:
        copy.start()

    @pl.loop(1, count)
    def _(d):
        remote(
            KB.at[k], KB.at[k], send_sem.at[16], stiff_sem, lax.rem(k + d, count), s
        ).start()

    def ghosts(boxes, high, low, depth, store):
        here = lane_iota(depth)
        evens = here % 2 == 0
        at_low = here * 0 + low_end == 1
        at_high = here * 0 + high_end == 1
        ahead = lambda x: roll(x, -1)
        behind = lambda x: roll(x, 1)
        centre = jnp.where(
            evens,
            jnp.where(at_low, low, ahead(boxes[0])),
            jnp.where(at_high, high, behind(boxes[1])),
        )
        outer = jnp.where(
            evens, jnp.where(at_low, low, boxes[0]), jnp.where(at_high, high, boxes[1])
        )
        inner = jnp.where(
            evens, jnp.where(at_low, ahead(low), low), jnp.where(at_high, behind(high), high)
        )
        down = roll(jnp.where(evens, ahead(boxes[2]), behind(boxes[3])), -2 * cells)
        up = roll(jnp.where(evens, ahead(boxes[4]), behind(boxes[5])), 2 * cells)
        own_down, own_up = jnp.zeros_like(down), jnp.zeros_like(up)
        for c in range(3):
            spot = c * group
            turned = roll(V[c, 1, pl.ds(base, depth), :], spot + 1)
            own_down = jnp.where(here // 2 == spot // 2, turned, own_down)
            spot = c * group + 2 * (cells + 1)
            turned = roll(V[c, cells + 2, pl.ds(base, depth), :], spot + 1)
            own_up = jnp.where(here // 2 == spot // 2, turned, own_up)
        own = own_down + own_up
        own = jnp.where(evens, ahead(own), behind(own))
        mirrored = jnp.where(evens, low_end, high_end) == 1
        cell = lax.rem(here, group) // 2 - 1
        in_fields = here < 3 * group
        centre = jnp.where(
            in_fields & (cell == -1),
            jnp.where(mirrored, own, down),
            jnp.where(in_fields & (cell == cells), jnp.where(mirrored, own, up), centre),
        )
        return centre, outer, inner

    def ghost_rates(centre, outer, inner, depth, top):
        here = lane_iota(depth)
        evens = here % 2 == 0
        which = here // group
        ups = {n: roll(centre, n * group) for n in (-2, -1, 1, 2)}
        of = lambda d: jnp.where(
            which == d,
            centre,
            jnp.where(
                which == (d + 1) % 3,
                ups[1] if d < 2 else ups[-2],
                ups[2] if d == 0 else ups[-1],
            ),
        )
        c0, c1, c2 = of(0), of(1), of(2)
        tu, td = roll(centre, -2), roll(centre, 2)
        sub = row_iota(depth)
        ru, rd = roll(centre, -1, 0), roll(centre, 1, 0)
        rd = jnp.where(sub == 0, -centre, rd)
        if top is not None:
            ru = jnp.where(sub == depth - 1, top, ru)
        su, sd = jnp.where(evens, inner, outer), jnp.where(evens, outer, inner)
        return combine(centre, c0, c1, c2, tu, td, ru, rd, su, sd)

    def combine(centre, c0, c1, c2, tu, td, ru, rd, su, sd):
        laplace = (tu + td) + (ru + rd) + (su + sd) - 6.0 * centre
        advect = c0 * (tu - td) + c1 * (ru - rd) + c2 * (su - sd)
        return NU_DT * laplace - (0.5 * ADV_DT) * advect

    def beside(centre, edge, at):
        left_end, right_end = lane_iota(8) == 0, lane_iota(8) == LANES - 1
        turned = roll(edge, lax.rem(2 * LANES - 1 - at, LANES))
        up = roll(jnp.where(left_end, turned, centre), -1)
        down = roll(jnp.where(right_end, turned, centre), 1)
        return up, down

    for copy in near_copies + theta_copies[:2]:
        copy.wait_recv()
    high8, low8 = TR[pl.ds(0, 8), :], TL[pl.ds(0, 8), :]
    centre, outer, inner = ghosts([near[n] for n in range(6)], high8, low8, 8, None)
    edge1 = centre
    edge2 = centre + ghost_rates(centre, outer, inner, 8, None)

    def wall_rates(field, lift, i, edge, fields):
        here = [field(c, i) for c in range(3)]
        rates = []
        for c in range(fields):
            centre = here[c]
            su, sd = beside(centre, edge, c * group + 2 * (i + 1))
            ru = roll(centre, -1, 0)
            rd = jnp.where(row8 == 0, -centre, roll(centre, 1, 0))
            rates.append(
                combine(
                    centre, here[0], here[1], here[2], field(c, i + 1), field(c, i - 1), ru, rd, su, sd
                )
            )
        return here, rates

    @pl.loop(0, cells + 2)
    def _(n):
        here, rates = wall_rates(
            lambda c, i: V[c, i + 2, pl.ds(base, 8), :], None, n - 1, edge1, 3
        )
        for c in range(3):
            W[c, n] = here[c] + rates[c]

    def wall_sum(i, sums):
        x, y = sums
        here, rates = wall_rates(lambda c, i: W[c, i + 1], None, i, edge2, 2)
        fresh = [
            0.5 * (V[c, i + 2, pl.ds(base, 8), :] + here[c] + rates[c]) for c in range(2)
        ]
        wc, ws = coef[0, pl.ds(i + 1, 1), :], coef[1, pl.ds(i + 1, 1), :]
        return (
            x + 2.0 * WALL_NU * (fresh[1] * wc - fresh[0] * ws),
            y + 2.0 * WALL_NU * (fresh[1] * ws + fresh[0] * wc),
        )

    zero8 = jnp.zeros((8, LANES), jnp.float32)
    fx, fy = lax.fori_loop(0, cells, wall_sum, (zero8, zero8))
    FB[s] = jnp.concatenate([fx[0:1], fy[0:1]], axis=0)

    @pl.loop(1, ring)
    def _(d):
        remote(FB.at[s], FB.at[s], send_sem.at[17], force_sem, k, lax.rem(s + d, ring)).start()

    for copy in full_copies + theta_copies[2:]:
        copy.wait_recv()
    centre, outer, inner = ghosts([full[n] for n in range(6)], TR[...], TL[...], rows, None)
    PG[...] = centre
    cur_lo = jnp.sum(
        jnp.where(lane == 3 * group, centre[0:1], 0.0), axis=1, keepdims=True
    )
    cur_hi = jnp.sum(
        jnp.where(lane == 3 * group + 1, centre[0:1], 0.0), axis=1, keepdims=True
    )
    cur_side = jnp.where(lane % 2 == 0, cur_lo, cur_hi)
    top = jnp.where(
        lane // group == 0,
        -cur_side * lane_sin,
        jnp.where(lane // group == 1, cur_side * lane_cos, 0.0),
    )
    UG[...] = centre + ghost_rates(centre, outer, inner, rows, top)

    def outer_rows(i):
        return coef[2, pl.ds(i + 1, 1), :], coef[3, pl.ds(i + 1, 1), :], jnp.zeros((1, LANES), jnp.float32)

    @pl.loop(0, cells + 2)
    def _(n):
        for c, value in enumerate(outer_rows(n - 1)):
            V[c, n + 1, pl.ds(base + rows, 1), :] = value
            V[c, n + 1, pl.ds(base - 1, 1), :] = -V[c, n + 1, pl.ds(base, 1), :]

    def bulk_rates(field, edge, i, t):
        start = base + 8 * t
        here = [field(c, i, start) for c in range(3)]
        rates = []
        for c in range(3):
            su, sd = beside(here[c], edge[pl.ds(8 * t, 8), :], c * group + 2 * (i + 1))
            rates.append(
                combine(
                    here[c],
                    here[0],
                    here[1],
                    here[2],
                    field(c, i + 1, start),
                    field(c, i - 1, start),
                    field(c, i, start + 1),
                    field(c, i, start - 1),
                    su,
                    sd,
                )
            )
        return here, rates

    @pl.loop(0, cells + 2)
    def _(n):
        for t in range(tiles):
            here, rates = bulk_rates(
                lambda c, i, start: V[c, i + 2, pl.ds(start, 8), :], PG, n - 1, t
            )
            for c in range(3):
                fresh = here[c] + rates[c]
                U[c, n, pl.ds(base + 8 * t, 8), :] = fresh
                if t == 0:
                    U[c, n, pl.ds(base - 1, 1), :] = -fresh[0:1]
        for c, value in enumerate(outer_rows(n - 1)):
            U[c, n, pl.ds(base + rows, 1), :] = value

    arrivals = ring - 1
    pltpu.make_async_copy(
        FB.at[pl.ds(0, arrivals)], FB.at[pl.ds(0, arrivals)], force_sem
    ).wait()
    force = FB[0]
    for n in range(1, ring):
        force = force + FB[n]
    force_out[...] = force
    load = force * LANES ** (-1.5) + mass * (disp[...] + rate[...])
    load8 = wide_loads(load)
    RB[pl.ds(k, 1), 0, :] = end_loads(answers, load8)

    @pl.loop(1, count)
    def _(d):
        remote(
            RB.at[k], RB.at[k], send_sem.at[18], load_sem, lax.rem(k + d, count), s
        ).start()

    others = count - 1
    pltpu.make_async_copy(KB.at[pl.ds(0, others)], KB.at[pl.ds(0, others)], stiff_sem).wait()
    spare = jnp.zeros((LANES - count, LANES), jnp.float32)
    numbers = jnp.concatenate([KB[:, 0, :], spare], axis=0).T
    blocks = chain_response(numbers, count, k, mass)
    blocks.append(jnp.zeros((LANES - 32, LANES), jnp.float32))
    response = jnp.concatenate(blocks, axis=0).T[0:count]
    rest = inner_deflection(steps, inverse, load8)

    chunks = 4
    each = cells // chunks
    out_copies = []
    for part in range(chunks):

        @pl.loop(part * each, (part + 1) * each)
        def _(i):
            for t in range(tiles):
                here, rates = bulk_rates(
                    lambda c, i, start: U[c, i + 1, pl.ds(start, 8), :], UG, i, t
                )
                for c in range(3):
                    OV[c, i, pl.ds(8 * t, 8), :] = 0.5 * (
                        V[c, i + 2, pl.ds(base + 8 * t, 8), :] + here[c] + rates[c]
                    )

        copy = pltpu.make_async_copy(
            OV.at[:, pl.ds(part * each, each)],
            out.at[:, pl.ds(part * each, each)],
            out_sem.at[part],
        )
        copy.start()
        out_copies.append(copy)

    pltpu.make_async_copy(RB.at[pl.ds(0, others)], RB.at[pl.ds(0, others)], load_sem).wait()
    ends = ends_solved(response, RB[:, 0, :])
    moved = ends * answers
    for direction in range(2):
        mine = jnp.sum(jnp.where(row8 % 2 == direction, moved, 0.0), axis=0, keepdims=True)
        defl_out[pl.ds(direction, 1), :] = rest[direction : direction + 1] + mine

    for copy in near_copies + full_copies + theta_copies:
        copy.wait_send()
    for sent, size, buffer in ((16, others, KB), (17, arrivals, FB), (18, others, RB)):
        pltpu.make_async_copy(
            buffer.at[pl.ds(0, size)], buffer.at[pl.ds(0, size)], send_sem.at[sent]
        ).wait()
    for copy in out_copies:
        copy.wait()


def solution(mesh):
    count, ring = mesh.shape["span"], mesh.shape["sector"]

    def local(velocity, speed, cbin, face, weight, tension, displacement, beam_rate):
        cells, rows, sections = velocity.shape[1:]
        anywhere = pl.BlockSpec(memory_space=pl.ANY)
        vmem = pl.BlockSpec(memory_space=pltpu.VMEM)
        smem = pl.BlockSpec(memory_space=pltpu.SMEM)
        tall = rows + 16
        f32 = jnp.float32
        return pl.pallas_call(
            lambda *refs: kernel(count, ring, *refs),
            out_shape=(
                jax.ShapeDtypeStruct(velocity.shape, f32),
                jax.ShapeDtypeStruct((2, sections), f32),
                jax.ShapeDtypeStruct((2, sections), f32),
            ),
            in_specs=[anywhere, smem, vmem, smem, smem, vmem, vmem, vmem],
            out_specs=(anywhere, vmem, vmem),
            scratch_shapes=[
                pltpu.VMEM((3, cells + 4, tall, LANES), f32),
                pltpu.VMEM((3, cells + 2, tall, LANES), f32),
                pltpu.VMEM((3, cells + 2, 8, LANES), f32),
                pltpu.VMEM((rows, LANES), f32),
                pltpu.VMEM((rows, LANES), f32),
                pltpu.VMEM((6, 8, LANES), f32),
                pltpu.VMEM((6, rows, LANES), f32),
                pltpu.VMEM((rows, LANES), f32),
                pltpu.VMEM((rows, LANES), f32),
                pltpu.VMEM((ring, 2, LANES), f32),
                pltpu.VMEM((count, 1, LANES), f32),
                pltpu.VMEM((count, 1, LANES), f32),
                pltpu.VMEM((4, 24, LANES), f32),
                pltpu.VMEM((3, cells, rows, LANES), f32),
                pltpu.SemaphoreType.DMA((2,)),
                pltpu.SemaphoreType.DMA((19,)),
                pltpu.SemaphoreType.DMA((4,)),
                pltpu.SemaphoreType.DMA((6,)),
                pltpu.SemaphoreType.DMA((6,)),
                pltpu.SemaphoreType.DMA,
                pltpu.SemaphoreType.DMA,
                pltpu.SemaphoreType.DMA,
                pltpu.SemaphoreType.DMA((4,)),
            ],
            compiler_params=pltpu.CompilerParams(
                collective_id=0, has_side_effects=True, vmem_limit_bytes=48 << 20
            ),
            name="riser",
        )(
            velocity,
            speed,
            cbin.reshape(1, sections),
            face,
            weight,
            tension.reshape(1, sections),
            displacement,
            beam_rate,
        )

    return jax.shard_map(
        local,
        mesh=mesh,
        in_specs=(
            P(None, "sector", None, "span"),
            P(),
            P("span"),
            P("sector"),
            P("sector"),
            P("span"),
            P(None, "span"),
            P(None, "span"),
        ),
        out_specs=(P(None, "sector", None, "span"), P(None, "span"), P(None, "span")),
        check_vma=False,
    )
```

```python
import math

import jax
import jax.numpy as jnp
from jax import lax
from jax.experimental import pallas as pl
from jax.experimental.pallas import tpu as pltpu
from jax.sharding import PartitionSpec as P

MESH = pl.DeviceIdType.MESH
NU_DT = 0.15
ADV_DT = 0.1
WALL_NU = 0.5
BEAM_EI = 0.5
BEAM_MASS = 0.4
LANES = 128


def roll(x, shift, axis=1):
    size = x.shape[axis]
    return pltpu.roll(x, shift % size if isinstance(shift, int) else shift, axis)


def lane_iota(rows):
    return lax.broadcasted_iota(jnp.int32, (rows, LANES), 1)


def row_iota(rows):
    return lax.broadcasted_iota(jnp.int32, (rows, LANES), 0)


def reduce_chain(A, D, F, rho_of, strides):
    A00, A01, A10, A11 = A
    D00, D01, D11 = D
    Fw, Fs = F
    steps = []
    for s in strides:
        inv = 1.0 / (D00 * D11 - D01 * D01)
        I00, I01, I11 = D11 * inv, -D01 * inv, D00 * inv
        P00 = I00 * A00 + I01 * A10
        P01 = I00 * A01 + I01 * A11
        P10 = I01 * A00 + I11 * A10
        P11 = I01 * A01 + I11 * A11
        E11 = A01 * P01 + A11 * P11
        I00m, I01m, I11m = roll(I00, s), roll(I01, s), roll(I11, s)
        al00 = A00 * I00m + A01 * I01m
        al01 = A00 * I01m + A01 * I11m
        al10 = A10 * I00m + A11 * I01m
        al11 = A10 * I01m + A11 * I11m
        ga00, ga01, ga10, ga11 = roll(P00, -s), roll(P10, -s), roll(P01, -s), roll(P11, -s)
        steps.append((al00, al01, al10, al11, ga00, ga01, ga10, ga11))
        P00m, P01m, P10m, P11m = roll(P00, s), roll(P01, s), roll(P10, s), roll(P11, s)
        D11 = D11 - (al10 * A10 + al11 * A11) - roll(E11, -s)
        Fw, Fs = reduce_load(steps[-1], Fw, Fs, s)
        A00, A01, A10, A11 = (
            -(A00 * P00m + A01 * P10m),
            -(A00 * P01m + A01 * P11m),
            -(A10 * P00m + A11 * P10m),
            -(A10 * P01m + A11 * P11m),
        )
        rw, rs = rho_of(Fw, Fs)
        D00 = rw - A00 - roll(A00, -2 * s)
        D01 = rs - A10 - roll(A01, -2 * s)
    inv = 1.0 / (D00 * D11 - D01 * D01)
    last = (D11 * inv, -D01 * inv, D00 * inv)
    return last[0] * Fw + last[1] * Fs, last[1] * Fw + last[2] * Fs, steps, last


def reduce_load(step, Fw, Fs, s):
    al00, al01, al10, al11, ga00, ga01, ga10, ga11 = step
    Fwm, Fsm, Fwp, Fsp = roll(Fw, s), roll(Fs, s), roll(Fw, -s), roll(Fs, -s)
    return (
        Fw - (al00 * Fwm + al01 * Fsm) - (ga00 * Fwp + ga01 * Fsp),
        Fs - (al10 * Fwm + al11 * Fsm) - (ga10 * Fwp + ga11 * Fsp),
    )


def slab_system(t, mass):
    lane = lane_iota(1)
    g = t / 30.0
    gn = roll(g, -1)
    a00, a01, a10, a11 = (
        -12.0 * BEAM_EI - 36.0 * g,
        -6.0 * BEAM_EI - 3.0 * g,
        6.0 * BEAM_EI + 3.0 * g,
        2.0 * BEAM_EI - g,
    )
    n00, n01, n10, n11 = roll(a00, -1), roll(a01, -1), roll(a10, -1), roll(a11, -1)
    d00 = (12.0 * BEAM_EI + 36.0 * g) + (12.0 * BEAM_EI + 36.0 * gn) + mass
    d01 = (-6.0 * BEAM_EI - 3.0 * g) + (6.0 * BEAM_EI + 3.0 * gn)
    d11 = (4.0 * BEAM_EI + 4.0 * g) + (4.0 * BEAM_EI + 4.0 * gn)
    inside = lane < LANES - 1
    rho_w = jnp.where(inside, (d00 - jnp.maximum(-a00, -n00)) - jnp.minimum(-a00, -n00), 0.0)
    rho_s = jnp.where(inside, (d01 + a10) + n01, 0.0)
    first, last, end = lane == 0, lane == LANES - 2, lane == LANES - 1
    zero = jnp.zeros_like(t)
    row = row_iota(8)

    def stack(rows):
        out = jnp.zeros((8, LANES), jnp.float32)
        for index, value in enumerate(rows):
            out = jnp.where(row == index, value, out)
        return out

    Fw = stack(
        [
            rho_w,
            jnp.where(first, -a00, zero),
            jnp.where(first, -a01, zero),
            jnp.where(last, -n00, jnp.where(end, 1.0, zero)),
            jnp.where(last, -n10, zero),
        ]
    )
    Fs = stack(
        [
            rho_s,
            jnp.where(first, -a10, zero),
            jnp.where(first, -a11, zero),
            jnp.where(last, -n01, zero),
            jnp.where(last, -n11, jnp.where(end, 1.0, zero)),
        ]
    )
    coupled = jnp.logical_and(lane > 0, inside)
    A = tuple(jnp.where(coupled, x, 0.0) for x in (a00, a01, a10, a11))
    D = (jnp.where(inside, d00, 1.0), jnp.where(inside, d01, 0.0), jnp.where(inside, d11, 1.0))

    def rho_of(Fw, Fs):
        return Fw[0:1] + Fw[1:2] + Fw[3:4], Fs[0:1] + Fs[1:2] + Fs[3:4]

    Zw, Zs, steps, inverse = reduce_chain(A, D, (Fw, Fs), rho_of, [1 << b for b in range(7)])
    yw, ys = Zw[0:1], Zs[0:1]
    xa1w, xa1s = Zw[2:3], Zs[2:3]
    xb0w, xb0s, xb1w, xb1s = Zw[3:4], Zs[3:4], Zw[4:5], Zs[4:5]
    numbers = [
        (0, xb0w * a00 + xb0s * a10),
        (0, xb0w * a01 + xb0s * a11),
        (0, xb1w * a00 + xb1s * a10),
        (0, xb1w * a01 + xb1s * a11),
        (0, -(a00 * yw + a10 * ys)),
        (0, -(a01 * yw + a11 * ys)),
        (0, (4.0 * BEAM_EI + 4.0 * g) + (a01 * xa1w + a11 * xa1s)),
        (LANES - 2, -(n00 * yw + n01 * ys)),
        (LANES - 2, -(n10 * yw + n11 * ys)),
        (LANES - 2, (4.0 * BEAM_EI + 4.0 * gn) + (n10 * xb1w + n11 * xb1s)),
    ]
    row16 = row_iota(16)
    table = jnp.zeros((16, LANES), jnp.float32)
    for index, (spot, value) in enumerate(numbers):
        table = jnp.where((row16 == index) & (lane == spot), value, table)
    column = jnp.sum(table, axis=1, keepdims=True)
    message = jnp.sum(jnp.where(lane_iota(16) == row16, column, 0.0), axis=0, keepdims=True)
    answers = jnp.zeros((8, LANES), jnp.float32)
    for u in range(4):
        answers = jnp.where(row // 2 == u, Zw[u + 1 : u + 2], answers)
    return message, answers, steps, inverse


def chain_response(numbers, count, place, mass):
    lane = lane_iota(1)
    valid = lane < count
    row = row_iota(8)
    pick = lambda n: jnp.where(valid, numbers[n : n + 1], 0.0)
    a00, a01, a10, a11 = pick(0), pick(1), pick(2), pick(3)
    raw, ras, ka11, rbw, rbs, kb11 = [pick(n) for n in range(4, 10)]
    above = lambda x: jnp.where(lane < count - 1, roll(x, -1), 0.0)
    first = lane == 0
    rw = rbw + above(raw) + mass - jnp.where(first, a00, 0.0)
    rs = rbs + above(ras) - jnp.where(first, a10, 0.0)
    rw = jnp.where(valid, rw, 1.0)
    rs = jnp.where(valid, rs, 0.0)
    d11 = jnp.where(valid, kb11 + above(ka11), 1.0)
    A = tuple(jnp.where(first, 0.0, x) for x in (a00, a01, a10, a11))
    d00 = rw - A[0] - roll(A[0], -1)
    d01 = rs - A[2] - roll(A[1], -1)
    lane8 = lane_iota(8)
    mine = lane8 == place
    before = lane8 == place - 1
    Fw = jnp.where((before & (row == 0)) | (mine & (row == 2)), 1.0, 0.0)
    Fs = jnp.where((before & (row == 1)) | (mine & (row == 3)), 1.0, 0.0)
    Fw = jnp.where(row == 4, rw, Fw)
    Fs = jnp.where(row == 4, rs, Fs)
    strides = []
    while (1 << len(strides)) < count:
        strides.append(1 << len(strides))
    Gw, Gs, _, _ = reduce_chain(
        A, (d00, d01, d11), (Fw, Fs), lambda w, s: (w[4:5], s[4:5]), strides
    )
    Hw, Hs = roll(Gw, 1), roll(Gs, 1)
    blocks = []
    for u in range(4):
        block = jnp.where(row // 2 == 0, Hw[u : u + 1], 0.0)
        block = jnp.where(row // 2 == 1, Hs[u : u + 1], block)
        block = jnp.where(row // 2 == 2, Gw[u : u + 1], block)
        blocks.append(jnp.where(row // 2 == 3, Gs[u : u + 1], block))
    return blocks


def wide_loads(load):
    row = row_iota(8)
    return jnp.where(row % 2 == 0, load[0:1], load[1:2])


def end_loads(answers, load8):
    total = jnp.sum(answers * load8, axis=1, keepdims=True)
    lane = lane_iota(8)
    keep = (lane % 8 == row_iota(8)) & (lane < 32)
    return jnp.sum(jnp.where(keep, total, 0.0), axis=0, keepdims=True)


def ends_solved(response, loads):
    total = jnp.sum(response * loads, axis=0, keepdims=True)
    lane, row = lane_iota(8), row_iota(8)
    keep = (lane // 8 == row // 2) & (lane % 2 == row % 2) & (lane < 32)
    return jnp.sum(jnp.where(keep, total, 0.0), axis=1, keepdims=True)


def inner_deflection(steps, inverse, load8):
    inside = lane_iota(8) < LANES - 1
    Fw, Fs = jnp.where(inside, load8, 0.0), jnp.zeros((8, LANES), jnp.float32)
    for b in range(7):
        Fw, Fs = reduce_load(steps[b], Fw, Fs, 1 << b)
    return inverse[0] * Fw + inverse[1] * Fs


def kernel(
    count,
    ring,
    vel_hbm,
    speed_hbm,
    cbin_hbm,
    face_hbm,
    weight_hbm,
    tens_hbm,
    disp_hbm,
    rate_hbm,
    out,
    force_out,
    defl_out,
    V,
    U,
    W,
    TR,
    TL,
    TRw,
    TLw,
    near,
    full,
    PG,
    UG,
    FB,
    KB,
    RB,
    coef,
    speed,
    cbin,
    face,
    weight,
    tens,
    disp,
    rate,
    own_sem,
    small_sem,
    send_sem,
    theta_sem,
    near_sem,
    full_sem,
    force_sem,
    stiff_sem,
    load_sem,
    round_sem,
):
    vel = vel_hbm
    cells, rows = vel.shape[1], vel.shape[2]
    tiles = rows // 8
    base = 8
    k = lax.axis_index("span")
    s = lax.axis_index("sector")
    left, right = lax.rem(k + count - 1, count), lax.rem(k + 1, count)
    turn = lambda d: lax.rem(s + d + ring, ring)
    lower, upper = turn(-1), turn(1)
    ny = 4 if count >= 32 else 2
    nz = count // ny
    y, z = k // nz, lax.rem(k, nz)

    def torus(dy, dz):
        return lax.rem(y + dy + ny, ny) * nz + lax.rem(z + dz + nz, nz)

    low_end = jnp.where(k == 0, 1, 0)
    high_end = jnp.where(k == count - 1, 1, 0)
    mass = BEAM_MASS / LANES**2
    stride = cells + 2
    group = 2 * stride

    barrier = pltpu.get_barrier_semaphore()

    def signal(semaphore, span, sector):
        pl.semaphore_signal(
            semaphore, inc=1, device_id={"span": span, "sector": sector}, device_id_type=MESH
        )

    close = [(side, way) for side in (left, right) for way in (lower, upper)]
    close += [(k, lower), (k, upper), (left, s), (right, s)]
    close += [(torus(1, 0), s), (torus(-1, 0), s), (torus(0, 1), s), (torus(0, -1), s)]
    for span, sector in close:
        signal(barrier, span, sector)

    own_wall = pltpu.make_async_copy(
        vel.at[:, :, pl.ds(0, 8), :],
        V.at[:, pl.ds(2, cells), pl.ds(base, 8), :],
        own_sem.at[0],
    )
    own_bulk = pltpu.make_async_copy(
        vel.at[:, :, pl.ds(8, rows - 8), :],
        V.at[:, pl.ds(2, cells), pl.ds(base + 8, rows - 8), :],
        own_sem.at[1],
    )
    small = [
        pltpu.make_async_copy(src, dst, small_sem.at[n])
        for n, (src, dst) in enumerate(
            (
                (speed_hbm, speed),
                (cbin_hbm, cbin),
                (face_hbm, face),
                (weight_hbm, weight),
                (tens_hbm, tens),
                (disp_hbm, disp),
                (rate_hbm, rate),
            )
        )
    ]
    own_wall.start()
    for copy in small:
        copy.start()
    own_bulk.start()

    rounds = []
    known = 1
    while known < max(ring // 2, nz // 2):
        steps_out = []
        if known < ring // 2:
            steps_out += [(k, turn(known)), (k, turn(-known))]
        if known < nz // 2:
            steps_out += [(torus(0, known), s), (torus(0, -known), s)]
        rounds.append(steps_out)
        known *= 2
    rows_out = [(torus(1, 0), s), (torus(-1, 0), s)]
    ring_rounds = len(rounds)
    rounds += [rows_out, rows_out]

    def begin(n):
        for span, sector in rounds[n]:
            signal(round_sem.at[n], span, sector)

    def finish(n):
        pl.semaphore_wait(round_sem.at[n], len(rounds[n]))

    lane = lane_iota(1)
    row8 = row_iota(8)
    total_cells = cells * ring

    def angle_of(index):
        whole = lax.rem(s * cells + index + total_cells, total_cells)
        return 2.0 * math.pi * (whole.astype(jnp.float32) + 0.5) / total_cells

    ring_angle = angle_of(row_iota(24) - 1)
    ring_sin, ring_cos = jnp.sin(ring_angle), jnp.cos(ring_angle)
    lane_cell = lax.rem(lane, group) // 2 - 1
    lane_angle = angle_of(lane_cell)
    lane_sin, lane_cos = jnp.sin(lane_angle), jnp.cos(lane_angle)

    own_wall.wait()
    lane8 = lane_iota(8)
    highs, lows = [], []
    for c in range(3):
        high = jnp.zeros((8, LANES), jnp.float32)
        low = high
        for i in range(cells):
            spot = c * group + 2 * (i + 1)
            turned = roll(V[c, i + 2, pl.ds(base, 8), :], spot + 2)
            high = jnp.where(lane8 // 2 == spot // 2, turned, high)
            low = jnp.where(lane8 // 2 == spot // 2 + 1, turned, low)
        highs.append(high)
        lows.append(low)
    high8 = highs[0] + highs[1] + highs[2]
    low8 = roll(lows[0] + lows[1] + lows[2], -2)
    TRw[...] = high8
    TLw[...] = low8

    def remote(src, dst, sent, arrived, span, sector):
        return pltpu.make_async_remote_copy(
            src_ref=src,
            dst_ref=dst,
            send_sem=sent,
            recv_sem=arrived,
            device_id={"span": span, "sector": sector},
            device_id_type=MESH,
        )

    spread = [
        (0, 0, right, s),
        (1, 1, left, s),
        (0, 2, right, upper),
        (1, 3, left, upper),
        (0, 4, right, lower),
        (1, 5, left, lower),
    ]
    near_copies = [
        remote(
            (TRw, TLw)[which], near.at[slot], send_sem.at[slot], near_sem.at[slot], span, sector
        )
        for which, slot, span, sector in spread
    ]
    full_copies = [
        remote(
            (TR, TL)[which], full.at[slot], send_sem.at[6 + slot], full_sem.at[slot], span, sector
        )
        for which, slot, span, sector in spread
    ]
    theta_copies = []
    for part, (start, size) in enumerate(((0, 8), (8, rows - 8))):
        theta_copies.append(
            remote(
                vel.at[:, pl.ds(0, 2), pl.ds(start, size), :],
                V.at[:, pl.ds(cells + 2, 2), pl.ds(base + start, size), :],
                send_sem.at[12 + 2 * part],
                theta_sem.at[2 * part],
                k,
                lower,
            )
        )
        theta_copies.append(
            remote(
                vel.at[:, pl.ds(cells - 2, 2), pl.ds(start, size), :],
                V.at[:, pl.ds(0, 2), pl.ds(base + start, size), :],
                send_sem.at[13 + 2 * part],
                theta_sem.at[1 + 2 * part],
                k,
                upper,
            )
        )

    pl.semaphore_wait(barrier, len(close))
    for copy in near_copies[2:] + near_copies[:2] + theta_copies[:2]:
        copy.start()
    begin(0)
    for copy in theta_copies[2:]:
        copy.start()

    for copy in small:
        copy.wait()
    current = jnp.zeros((1, LANES), jnp.float32)
    for b in range(speed.shape[0]):
        current = current + jnp.where(cbin[...] == b, speed[b], 0.0)
    face_row = row_iota(24) - 1
    face_weight = jnp.zeros((24, LANES), jnp.float32)
    for q in range(weight.shape[0]):
        face_weight = face_weight + jnp.where(face_row == face[q], weight[q], 0.0)
    coef[0] = face_weight * ring_cos
    coef[1] = face_weight * ring_sin
    coef[2] = -current * ring_sin
    coef[3] = current * ring_cos
    cur_high = jnp.sum(jnp.where(lane == LANES - 1, current, 0.0), axis=1, keepdims=True)
    cur_low = jnp.sum(jnp.where(lane == 0, current, 0.0), axis=1, keepdims=True)
    wide = lane_iota(rows)
    TR[...] = jnp.where(wide == 3 * group + 1, cur_high, 0.0)
    TL[...] = jnp.where(wide == 3 * group + 2, cur_low, 0.0)
    own_bulk.wait()

    @pl.loop(0, cells)
    def _(i):
        high, low = TR[...], TL[...]
        for c in range(3):
            spot = c * group + 2 * (i + 1)
            turned = roll(V[c, i + 2, pl.ds(base, rows), :], spot + 2)
            high = jnp.where(wide // 2 == spot // 2, turned, high)
            low = jnp.where(wide // 2 == spot // 2 + 1, turned, low)
        TR[...] = high
        TL[...] = low

    TL[...] = roll(TL[...], -2)
    for copy in full_copies:
        copy.start()
    for n in range(ring_rounds):
        finish(n)
        begin(n + 1)
        if n == 0:
            message, answers, steps, inverse = slab_system(tens[...], mass)
            KB[pl.ds(k, 1), 0, :] = message

    def everyone(buffer, sent, arrived):
        far = [(dy, dz) for dy in range(ny) for dz in range(nz) if (dy, dz) != (0, 0)]
        far.sort(key=lambda d: -(min(d[0], ny - d[0]) + min(d[1], nz - d[1])))
        for dy, dz in far:
            remote(buffer.at[k], buffer.at[k], sent, arrived, torus(dy, dz), s).start()

    def ghosts(boxes, high, low, depth, store):
        here = lane_iota(depth)
        evens = here % 2 == 0
        at_low = here * 0 + low_end == 1
        at_high = here * 0 + high_end == 1
        ahead = lambda x: roll(x, -1)
        behind = lambda x: roll(x, 1)
        centre = jnp.where(
            evens,
            jnp.where(at_low, low, ahead(boxes[0])),
            jnp.where(at_high, high, behind(boxes[1])),
        )
        outer = jnp.where(
            evens, jnp.where(at_low, low, boxes[0]), jnp.where(at_high, high, boxes[1])
        )
        inner = jnp.where(
            evens, jnp.where(at_low, ahead(low), low), jnp.where(at_high, behind(high), high)
        )
        down = roll(jnp.where(evens, ahead(boxes[2]), behind(boxes[3])), -2 * cells)
        up = roll(jnp.where(evens, ahead(boxes[4]), behind(boxes[5])), 2 * cells)
        own_down, own_up = jnp.zeros_like(down), jnp.zeros_like(up)
        for c in range(3):
            spot = c * group
            turned = roll(V[c, 1, pl.ds(base, depth), :], spot + 1)
            own_down = jnp.where(here // 2 == spot // 2, turned, own_down)
            spot = c * group + 2 * (cells + 1)
            turned = roll(V[c, cells + 2, pl.ds(base, depth), :], spot + 1)
            own_up = jnp.where(here // 2 == spot // 2, turned, own_up)
        own = own_down + own_up
        own = jnp.where(evens, ahead(own), behind(own))
        mirrored = jnp.where(evens, low_end, high_end) == 1
        cell = lax.rem(here, group) // 2 - 1
        in_fields = here < 3 * group
        centre = jnp.where(
            in_fields & (cell == -1),
            jnp.where(mirrored, own, down),
            jnp.where(in_fields & (cell == cells), jnp.where(mirrored, own, up), centre),
        )
        return centre, outer, inner

    def ghost_rates(centre, outer, inner, depth, top):
        here = lane_iota(depth)
        evens = here % 2 == 0
        which = here // group
        ups = {n: roll(centre, n * group) for n in (-2, -1, 1, 2)}
        of = lambda d: jnp.where(
            which == d,
            centre,
            jnp.where(
                which == (d + 1) % 3,
                ups[1] if d < 2 else ups[-2],
                ups[2] if d == 0 else ups[-1],
            ),
        )
        c0, c1, c2 = of(0), of(1), of(2)
        tu, td = roll(centre, -2), roll(centre, 2)
        sub = row_iota(depth)
        ru, rd = roll(centre, -1, 0), roll(centre, 1, 0)
        rd = jnp.where(sub == 0, -centre, rd)
        if top is not None:
            ru = jnp.where(sub == depth - 1, top, ru)
        su, sd = jnp.where(evens, inner, outer), jnp.where(evens, outer, inner)
        return combine(centre, c0, c1, c2, tu, td, ru, rd, su, sd)

    def combine(centre, c0, c1, c2, tu, td, ru, rd, su, sd):
        laplace = (tu + td) + (ru + rd) + (su + sd) - 6.0 * centre
        advect = c0 * (tu - td) + c1 * (ru - rd) + c2 * (su - sd)
        return NU_DT * laplace - (0.5 * ADV_DT) * advect

    def beside(centre, edge, at):
        left_end, right_end = lane_iota(8) == 0, lane_iota(8) == LANES - 1
        turned = roll(edge, lax.rem(2 * LANES - 1 - at, LANES))
        up = roll(jnp.where(left_end, turned, centre), -1)
        down = roll(jnp.where(right_end, turned, centre), 1)
        return up, down

    for copy in near_copies + theta_copies[:2]:
        copy.wait_recv()
    centre, outer, inner = ghosts([near[n] for n in range(6)], high8, low8, 8, None)
    edge1 = centre
    edge2 = centre + ghost_rates(centre, outer, inner, 8, None)

    def wall_rates(field, lift, i, edge, fields):
        here = [field(c, i) for c in range(3)]
        rates = []
        for c in range(fields):
            centre = here[c]
            su, sd = beside(centre, edge, c * group + 2 * (i + 1))
            ru = roll(centre, -1, 0)
            rd = jnp.where(row8 == 0, -centre, roll(centre, 1, 0))
            rates.append(
                combine(
                    centre, here[0], here[1], here[2], field(c, i + 1), field(c, i - 1), ru, rd, su, sd
                )
            )
        return here, rates

    @pl.loop(0, (cells + 2) // 6)
    def _(block):
        for n in range(6):
            n = block * 6 + n
            here, rates = wall_rates(
                lambda c, i: V[c, i + 2, pl.ds(base, 8), :], None, n - 1, edge1, 3
            )
            for c in range(3):
                W[c, n] = here[c] + rates[c]

    def wall_block(block, sums):
        for n in range(8):
            sums = wall_sum(block * 8 + n, sums)
        return sums

    def wall_sum(i, sums):
        x, y = sums
        here, rates = wall_rates(lambda c, i: W[c, i + 1], None, i, edge2, 2)
        fresh = [
            0.5 * (V[c, i + 2, pl.ds(base, 8), :] + here[c] + rates[c]) for c in range(2)
        ]
        wc, ws = coef[0, pl.ds(i + 1, 1), :], coef[1, pl.ds(i + 1, 1), :]
        return (
            x + 2.0 * WALL_NU * (fresh[1] * wc - fresh[0] * ws),
            y + 2.0 * WALL_NU * (fresh[1] * ws + fresh[0] * wc),
        )

    zero8 = jnp.zeros((8, LANES), jnp.float32)
    fx, fy = lax.fori_loop(0, cells // 8, wall_block, (zero8, zero8))
    FB[s] = jnp.concatenate([fx[0:1], fy[0:1]], axis=0)

    @pl.loop(1, ring)
    def _(d):
        remote(FB.at[s], FB.at[s], send_sem.at[17], force_sem, k, lax.rem(s + d, ring)).start()

    finish(ring_rounds)
    begin(ring_rounds + 1)

    for copy in full_copies + theta_copies[2:]:
        copy.wait_recv()
    centre, outer, inner = ghosts([full[n] for n in range(6)], TR[...], TL[...], rows, None)
    PG[...] = centre
    cur_lo = jnp.sum(
        jnp.where(lane == 3 * group, centre[0:1], 0.0), axis=1, keepdims=True
    )
    cur_hi = jnp.sum(
        jnp.where(lane == 3 * group + 1, centre[0:1], 0.0), axis=1, keepdims=True
    )
    cur_side = jnp.where(lane % 2 == 0, cur_lo, cur_hi)
    top = jnp.where(
        lane // group == 0,
        -cur_side * lane_sin,
        jnp.where(lane // group == 1, cur_side * lane_cos, 0.0),
    )
    UG[...] = centre + ghost_rates(centre, outer, inner, rows, top)

    def outer_rows(i):
        return coef[2, pl.ds(i + 1, 1), :], coef[3, pl.ds(i + 1, 1), :], jnp.zeros((1, LANES), jnp.float32)

    @pl.loop(0, cells + 2)
    def _(n):
        for c, value in enumerate(outer_rows(n - 1)):
            V[c, n + 1, pl.ds(base + rows, 1), :] = value
            V[c, n + 1, pl.ds(base - 1, 1), :] = -V[c, n + 1, pl.ds(base, 1), :]

    def bulk_rates(field, edge, i, t):
        start = base + 8 * t
        here = [field(c, i, start) for c in range(3)]
        rates = []
        for c in range(3):
            su, sd = beside(here[c], edge[pl.ds(8 * t, 8), :], c * group + 2 * (i + 1))
            rates.append(
                combine(
                    here[c],
                    here[0],
                    here[1],
                    here[2],
                    field(c, i + 1, start),
                    field(c, i - 1, start),
                    field(c, i, start + 1),
                    field(c, i, start - 1),
                    su,
                    sd,
                )
            )
        return here, rates

    @pl.loop(0, cells + 2)
    def _(n):
        for t in range(tiles):
            here, rates = bulk_rates(
                lambda c, i, start: V[c, i + 2, pl.ds(start, 8), :], PG, n - 1, t
            )
            for c in range(3):
                fresh = here[c] + rates[c]
                U[c, n, pl.ds(base + 8 * t, 8), :] = fresh
                if t == 0:
                    U[c, n, pl.ds(base - 1, 1), :] = -fresh[0:1]
        for c, value in enumerate(outer_rows(n - 1)):
            U[c, n, pl.ds(base + rows, 1), :] = value

    finish(ring_rounds + 1)
    everyone(KB, send_sem.at[16], stiff_sem)

    arrivals = ring - 1
    pltpu.make_async_copy(
        FB.at[pl.ds(0, arrivals)], FB.at[pl.ds(0, arrivals)], force_sem
    ).wait()
    force = FB[0]
    for n in range(1, ring):
        force = force + FB[n]
    force_out[...] = force
    load = force * LANES ** (-1.5) + mass * (disp[...] + rate[...])
    load8 = wide_loads(load)
    RB[pl.ds(k, 1), 0, :] = end_loads(answers, load8)

    everyone(RB, send_sem.at[18], load_sem)

    others = count - 1
    pltpu.make_async_copy(KB.at[pl.ds(0, others)], KB.at[pl.ds(0, others)], stiff_sem).wait()
    spare = jnp.zeros((LANES - count, LANES), jnp.float32)
    numbers = jnp.concatenate([KB[:, 0, :], spare], axis=0).T
    blocks = chain_response(numbers, count, k, mass)
    blocks.append(jnp.zeros((LANES - 32, LANES), jnp.float32))
    response = jnp.concatenate(blocks, axis=0).T[0:count]
    rest = inner_deflection(steps, inverse, load8)

    @pl.loop(0, cells)
    def _(i):
        for t in range(tiles):
            here, rates = bulk_rates(
                lambda c, i, start: U[c, i + 1, pl.ds(start, 8), :], UG, i, t
            )
            for c in range(3):
                out[c, i, pl.ds(8 * t, 8), :] = 0.5 * (
                    V[c, i + 2, pl.ds(base + 8 * t, 8), :] + here[c] + rates[c]
                )

    pltpu.make_async_copy(RB.at[pl.ds(0, others)], RB.at[pl.ds(0, others)], load_sem).wait()
    ends = ends_solved(response, RB[:, 0, :])
    moved = ends * answers
    for direction in range(2):
        mine = jnp.sum(jnp.where(row8 % 2 == direction, moved, 0.0), axis=0, keepdims=True)
        defl_out[pl.ds(direction, 1), :] = rest[direction : direction + 1] + mine

    for copy in near_copies + full_copies + theta_copies:
        copy.wait_send()
    for sent, size, buffer in ((16, others, KB), (17, arrivals, FB), (18, others, RB)):
        pltpu.make_async_copy(
            buffer.at[pl.ds(0, size)], buffer.at[pl.ds(0, size)], send_sem.at[sent]
        ).wait()


def hand_over(fresh, force, defl, fresh_out, force_out, defl_out, sem):
    copies = [
        pltpu.make_async_copy(src, dst, sem.at[n])
        for n, (src, dst) in enumerate(
            ((fresh, fresh_out), (force, force_out), (defl, defl_out))
        )
    ]
    for copy in copies:
        copy.start()
    for copy in copies:
        copy.wait()


def solution(mesh):
    count, ring = mesh.shape["span"], mesh.shape["sector"]

    def local(velocity, speed, cbin, face, weight, tension, displacement, beam_rate):
        cells, rows, sections = velocity.shape[1:]
        far = pl.BlockSpec(memory_space=pltpu.HBM)
        vmem = pl.BlockSpec(memory_space=pltpu.VMEM)
        tall = rows + 16
        f32 = jnp.float32
        shapes = (
            jax.ShapeDtypeStruct(velocity.shape, f32),
            jax.ShapeDtypeStruct((2, sections), f32),
            jax.ShapeDtypeStruct((2, sections), f32),
        )
        results = pl.pallas_call(
            lambda *refs: kernel(count, ring, *refs),
            out_shape=shapes,
            in_specs=[far] * 8,
            out_specs=(vmem,) * 3,
            scratch_shapes=[
                pltpu.VMEM((3, cells + 4, tall, LANES), f32),
                pltpu.VMEM((3, cells + 2, tall, LANES), f32),
                pltpu.VMEM((3, cells + 2, 8, LANES), f32),
                pltpu.VMEM((rows, LANES), f32),
                pltpu.VMEM((rows, LANES), f32),
                pltpu.VMEM((8, LANES), f32),
                pltpu.VMEM((8, LANES), f32),
                pltpu.VMEM((6, 8, LANES), f32),
                pltpu.VMEM((6, rows, LANES), f32),
                pltpu.VMEM((rows, LANES), f32),
                pltpu.VMEM((rows, LANES), f32),
                pltpu.VMEM((ring, 2, LANES), f32),
                pltpu.VMEM((count, 1, LANES), f32),
                pltpu.VMEM((count, 1, LANES), f32),
                pltpu.VMEM((4, 24, LANES), f32),
                pltpu.SMEM(speed.shape, f32),
                pltpu.VMEM((1, sections), jnp.int32),
                pltpu.SMEM(face.shape, jnp.int32),
                pltpu.SMEM(weight.shape, f32),
                pltpu.VMEM((1, sections), f32),
                pltpu.VMEM((2, sections), f32),
                pltpu.VMEM((2, sections), f32),
                pltpu.SemaphoreType.DMA((2,)),
                pltpu.SemaphoreType.DMA((7,)),
                pltpu.SemaphoreType.DMA((19,)),
                pltpu.SemaphoreType.DMA((4,)),
                pltpu.SemaphoreType.DMA((6,)),
                pltpu.SemaphoreType.DMA((6,)),
                pltpu.SemaphoreType.DMA,
                pltpu.SemaphoreType.DMA,
                pltpu.SemaphoreType.DMA,
                pltpu.SemaphoreType.REGULAR((6,)),
            ],
            compiler_params=pltpu.CompilerParams(
                collective_id=0, has_side_effects=True, vmem_limit_bytes=24 << 20
            ),
            name="riser",
        )(
            *[pltpu.with_memory_space_constraint(x, pltpu.HBM) for x in (velocity,
            speed,
            cbin.reshape(1, sections),
            face,
            weight,
            tension.reshape(1, sections),
            displacement,
            beam_rate)],
        )
        return pl.pallas_call(
            hand_over,
            out_shape=shapes,
            in_specs=[vmem] * 3,
            out_specs=(far,) * 3,
            scratch_shapes=[pltpu.SemaphoreType.DMA((3,))],
            name="results",
        )(*[pltpu.with_memory_space_constraint(x, pltpu.VMEM) for x in results])

    return jax.shard_map(
        local,
        mesh=mesh,
        in_specs=(
            P(None, "sector", None, "span"),
            P(),
            P("span"),
            P("sector"),
            P("sector"),
            P("span"),
            P(None, "span"),
            P(None, "span"),
        ),
        out_specs=(P(None, "sector", None, "span"), P(None, "span"), P(None, "span")),
        check_vma=False,
    )
```

```python
import math

import jax
import jax.numpy as jnp
from jax import lax
from jax.experimental import pallas as pl
from jax.experimental.pallas import tpu as pltpu
from jax.sharding import PartitionSpec as P

MESH = pl.DeviceIdType.MESH
NU_DT = 0.15
ADV_DT = 0.1
WALL_NU = 0.5
BEAM_EI = 0.5
BEAM_MASS = 0.4
LANES = 128


def roll(x, shift, axis=1):
    size = x.shape[axis]
    return pltpu.roll(x, shift % size if isinstance(shift, int) else shift, axis)


def lane_iota(rows):
    return lax.broadcasted_iota(jnp.int32, (rows, LANES), 1)


def row_iota(rows):
    return lax.broadcasted_iota(jnp.int32, (rows, LANES), 0)


def reduce_chain(A, D, F, rho_of, strides):
    A00, A01, A10, A11 = A
    D00, D01, D11 = D
    Fw, Fs = F
    steps = []
    for s in strides:
        inv = 1.0 / (D00 * D11 - D01 * D01)
        I00, I01, I11 = D11 * inv, -D01 * inv, D00 * inv
        P00 = I00 * A00 + I01 * A10
        P01 = I00 * A01 + I01 * A11
        P10 = I01 * A00 + I11 * A10
        P11 = I01 * A01 + I11 * A11
        E11 = A01 * P01 + A11 * P11
        I00m, I01m, I11m = roll(I00, s), roll(I01, s), roll(I11, s)
        al00 = A00 * I00m + A01 * I01m
        al01 = A00 * I01m + A01 * I11m
        al10 = A10 * I00m + A11 * I01m
        al11 = A10 * I01m + A11 * I11m
        ga00, ga01, ga10, ga11 = roll(P00, -s), roll(P10, -s), roll(P01, -s), roll(P11, -s)
        steps.append((al00, al01, al10, al11, ga00, ga01, ga10, ga11))
        P00m, P01m, P10m, P11m = roll(P00, s), roll(P01, s), roll(P10, s), roll(P11, s)
        D11 = D11 - (al10 * A10 + al11 * A11) - roll(E11, -s)
        Fw, Fs = reduce_load(steps[-1], Fw, Fs, s)
        A00, A01, A10, A11 = (
            -(A00 * P00m + A01 * P10m),
            -(A00 * P01m + A01 * P11m),
            -(A10 * P00m + A11 * P10m),
            -(A10 * P01m + A11 * P11m),
        )
        rw, rs = rho_of(Fw, Fs)
        D00 = rw - A00 - roll(A00, -2 * s)
        D01 = rs - A10 - roll(A01, -2 * s)
    inv = 1.0 / (D00 * D11 - D01 * D01)
    last = (D11 * inv, -D01 * inv, D00 * inv)
    return last[0] * Fw + last[1] * Fs, last[1] * Fw + last[2] * Fs, steps, last


def reduce_load(step, Fw, Fs, s):
    al00, al01, al10, al11, ga00, ga01, ga10, ga11 = step
    Fwm, Fsm, Fwp, Fsp = roll(Fw, s), roll(Fs, s), roll(Fw, -s), roll(Fs, -s)
    return (
        Fw - (al00 * Fwm + al01 * Fsm) - (ga00 * Fwp + ga01 * Fsp),
        Fs - (al10 * Fwm + al11 * Fsm) - (ga10 * Fwp + ga11 * Fsp),
    )


def slab_system(t, mass):
    lane = lane_iota(1)
    g = t / 30.0
    gn = roll(g, -1)
    a00, a01, a10, a11 = (
        -12.0 * BEAM_EI - 36.0 * g,
        -6.0 * BEAM_EI - 3.0 * g,
        6.0 * BEAM_EI + 3.0 * g,
        2.0 * BEAM_EI - g,
    )
    n00, n01, n10, n11 = roll(a00, -1), roll(a01, -1), roll(a10, -1), roll(a11, -1)
    d00 = (12.0 * BEAM_EI + 36.0 * g) + (12.0 * BEAM_EI + 36.0 * gn) + mass
    d01 = (-6.0 * BEAM_EI - 3.0 * g) + (6.0 * BEAM_EI + 3.0 * gn)
    d11 = (4.0 * BEAM_EI + 4.0 * g) + (4.0 * BEAM_EI + 4.0 * gn)
    inside = lane < LANES - 1
    rho_w = jnp.where(inside, (d00 - jnp.maximum(-a00, -n00)) - jnp.minimum(-a00, -n00), 0.0)
    rho_s = jnp.where(inside, (d01 + a10) + n01, 0.0)
    first, last, end = lane == 0, lane == LANES - 2, lane == LANES - 1
    zero = jnp.zeros_like(t)
    row = row_iota(8)

    def stack(rows):
        out = jnp.zeros((8, LANES), jnp.float32)
        for index, value in enumerate(rows):
            out = jnp.where(row == index, value, out)
        return out

    Fw = stack(
        [
            rho_w,
            jnp.where(first, -a00, zero),
            jnp.where(first, -a01, zero),
            jnp.where(last, -n00, jnp.where(end, 1.0, zero)),
            jnp.where(last, -n10, zero),
        ]
    )
    Fs = stack(
        [
            rho_s,
            jnp.where(first, -a10, zero),
            jnp.where(first, -a11, zero),
            jnp.where(last, -n01, zero),
            jnp.where(last, -n11, jnp.where(end, 1.0, zero)),
        ]
    )
    coupled = jnp.logical_and(lane > 0, inside)
    A = tuple(jnp.where(coupled, x, 0.0) for x in (a00, a01, a10, a11))
    D = (jnp.where(inside, d00, 1.0), jnp.where(inside, d01, 0.0), jnp.where(inside, d11, 1.0))

    def rho_of(Fw, Fs):
        return Fw[0:1] + Fw[1:2] + Fw[3:4], Fs[0:1] + Fs[1:2] + Fs[3:4]

    Zw, Zs, steps, inverse = reduce_chain(A, D, (Fw, Fs), rho_of, [1 << b for b in range(7)])
    yw, ys = Zw[0:1], Zs[0:1]
    xa1w, xa1s = Zw[2:3], Zs[2:3]
    xb0w, xb0s, xb1w, xb1s = Zw[3:4], Zs[3:4], Zw[4:5], Zs[4:5]
    numbers = [
        (0, xb0w * a00 + xb0s * a10),
        (0, xb0w * a01 + xb0s * a11),
        (0, xb1w * a00 + xb1s * a10),
        (0, xb1w * a01 + xb1s * a11),
        (0, -(a00 * yw + a10 * ys)),
        (0, -(a01 * yw + a11 * ys)),
        (0, (4.0 * BEAM_EI + 4.0 * g) + (a01 * xa1w + a11 * xa1s)),
        (LANES - 2, -(n00 * yw + n01 * ys)),
        (LANES - 2, -(n10 * yw + n11 * ys)),
        (LANES - 2, (4.0 * BEAM_EI + 4.0 * gn) + (n10 * xb1w + n11 * xb1s)),
    ]
    row16 = row_iota(16)
    table = jnp.zeros((16, LANES), jnp.float32)
    for index, (spot, value) in enumerate(numbers):
        table = jnp.where((row16 == index) & (lane == spot), value, table)
    column = jnp.sum(table, axis=1, keepdims=True)
    message = jnp.sum(jnp.where(lane_iota(16) == row16, column, 0.0), axis=0, keepdims=True)
    answers = jnp.zeros((8, LANES), jnp.float32)
    for u in range(4):
        answers = jnp.where(row // 2 == u, Zw[u + 1 : u + 2], answers)
    return message, answers, steps, inverse


def chain_response(numbers, count, place, mass):
    lane = lane_iota(1)
    valid = lane < count
    row = row_iota(8)
    pick = lambda n: jnp.where(valid, numbers[n : n + 1], 0.0)
    a00, a01, a10, a11 = pick(0), pick(1), pick(2), pick(3)
    raw, ras, ka11, rbw, rbs, kb11 = [pick(n) for n in range(4, 10)]
    above = lambda x: jnp.where(lane < count - 1, roll(x, -1), 0.0)
    first = lane == 0
    rw = rbw + above(raw) + mass - jnp.where(first, a00, 0.0)
    rs = rbs + above(ras) - jnp.where(first, a10, 0.0)
    rw = jnp.where(valid, rw, 1.0)
    rs = jnp.where(valid, rs, 0.0)
    d11 = jnp.where(valid, kb11 + above(ka11), 1.0)
    A = tuple(jnp.where(first, 0.0, x) for x in (a00, a01, a10, a11))
    d00 = rw - A[0] - roll(A[0], -1)
    d01 = rs - A[2] - roll(A[1], -1)
    lane8 = lane_iota(8)
    mine = lane8 == place
    before = lane8 == place - 1
    Fw = jnp.where((before & (row == 0)) | (mine & (row == 2)), 1.0, 0.0)
    Fs = jnp.where((before & (row == 1)) | (mine & (row == 3)), 1.0, 0.0)
    Fw = jnp.where(row == 4, rw, Fw)
    Fs = jnp.where(row == 4, rs, Fs)
    strides = []
    while (1 << len(strides)) < count:
        strides.append(1 << len(strides))
    Gw, Gs, _, _ = reduce_chain(
        A, (d00, d01, d11), (Fw, Fs), lambda w, s: (w[4:5], s[4:5]), strides
    )
    Hw, Hs = roll(Gw, 1), roll(Gs, 1)
    blocks = []
    for u in range(4):
        block = jnp.where(row // 2 == 0, Hw[u : u + 1], 0.0)
        block = jnp.where(row // 2 == 1, Hs[u : u + 1], block)
        block = jnp.where(row // 2 == 2, Gw[u : u + 1], block)
        blocks.append(jnp.where(row // 2 == 3, Gs[u : u + 1], block))
    return blocks


def wide_loads(load):
    row = row_iota(8)
    return jnp.where(row % 2 == 0, load[0:1], load[1:2])


def end_loads(answers, load8):
    total = jnp.sum(answers * load8, axis=1, keepdims=True)
    lane = lane_iota(8)
    keep = (lane % 8 == row_iota(8)) & (lane < 32)
    return jnp.sum(jnp.where(keep, total, 0.0), axis=0, keepdims=True)


def ends_solved(response, loads):
    total = jnp.sum(response * loads, axis=0, keepdims=True)
    lane, row = lane_iota(8), row_iota(8)
    keep = (lane // 8 == row // 2) & (lane % 2 == row % 2) & (lane < 32)
    return jnp.sum(jnp.where(keep, total, 0.0), axis=1, keepdims=True)


def inner_deflection(steps, inverse, load8):
    inside = lane_iota(8) < LANES - 1
    Fw, Fs = jnp.where(inside, load8, 0.0), jnp.zeros((8, LANES), jnp.float32)
    for b in range(7):
        Fw, Fs = reduce_load(steps[b], Fw, Fs, 1 << b)
    return inverse[0] * Fw + inverse[1] * Fs


def kernel(
    count,
    ring,
    vel_hbm,
    speed_hbm,
    cbin_hbm,
    face_hbm,
    weight_hbm,
    tens_hbm,
    disp_hbm,
    rate_hbm,
    out,
    force_out,
    defl_out,
    V,
    U,
    W,
    TR,
    TL,
    TRw,
    TLw,
    near,
    full,
    PG,
    UG,
    FB,
    KB,
    RB,
    coef,
    speed,
    cbin,
    face,
    weight,
    tens,
    disp,
    rate,
    own_sem,
    small_sem,
    send_sem,
    theta_sem,
    near_sem,
    full_sem,
    force_sem,
    stiff_sem,
    load_sem,
    round_sem,
):
    vel = vel_hbm
    cells, rows = vel.shape[1], vel.shape[2]
    tiles = rows // 8
    base = 8
    k = lax.axis_index("span")
    s = lax.axis_index("sector")
    left, right = lax.rem(k + count - 1, count), lax.rem(k + 1, count)
    turn = lambda d: lax.rem(s + d + ring, ring)
    lower, upper = turn(-1), turn(1)
    ny = 4 if count >= 32 else 2
    nz = count // ny
    y, z = k // nz, lax.rem(k, nz)

    def torus(dy, dz):
        return lax.rem(y + dy + ny, ny) * nz + lax.rem(z + dz + nz, nz)

    low_end = jnp.where(k == 0, 1, 0)
    high_end = jnp.where(k == count - 1, 1, 0)
    mass = BEAM_MASS / LANES**2
    stride = cells + 2
    group = 2 * stride

    barrier = pltpu.get_barrier_semaphore()

    def signal(semaphore, span, sector):
        pl.semaphore_signal(
            semaphore, inc=1, device_id={"span": span, "sector": sector}, device_id_type=MESH
        )

    close = [(side, way) for side in (left, right) for way in (lower, upper)]
    close += [(k, lower), (k, upper), (left, s), (right, s)]
    close += [(torus(1, 0), s), (torus(-1, 0), s), (torus(0, 1), s), (torus(0, -1), s)]
    own_wall = pltpu.make_async_copy(
        vel.at[:, :, pl.ds(0, 8), :],
        V.at[:, pl.ds(2, cells), pl.ds(base, 8), :],
        own_sem.at[0],
    )
    own_bulk = pltpu.make_async_copy(
        vel.at[:, :, pl.ds(8, rows - 8), :],
        V.at[:, pl.ds(2, cells), pl.ds(base + 8, rows - 8), :],
        own_sem.at[1],
    )
    small = [
        pltpu.make_async_copy(src, dst, small_sem.at[n])
        for n, (src, dst) in enumerate(
            (
                (speed_hbm, speed),
                (cbin_hbm, cbin),
                (face_hbm, face),
                (weight_hbm, weight),
                (tens_hbm, tens),
                (disp_hbm, disp),
                (rate_hbm, rate),
            )
        )
    ]
    own_wall.start()
    for copy in small:
        copy.start()
    own_bulk.start()

    for span, sector in close:
        signal(barrier, span, sector)

    rounds = []
    known = 1
    while known < max(ring // 2, nz // 2):
        steps_out = []
        if known < ring // 2:
            steps_out += [(k, turn(known)), (k, turn(-known))]
        if known < nz // 2:
            steps_out += [(torus(0, known), s), (torus(0, -known), s)]
        rounds.append(steps_out)
        known *= 2
    rows_out = [(torus(1, 0), s), (torus(-1, 0), s)]
    ring_rounds = len(rounds)
    rounds += [rows_out, rows_out]

    def begin(n):
        for span, sector in rounds[n]:
            signal(round_sem.at[n], span, sector)

    def finish(n):
        pl.semaphore_wait(round_sem.at[n], len(rounds[n]))

    lane = lane_iota(1)
    row8 = row_iota(8)
    total_cells = cells * ring

    def angle_of(index):
        whole = lax.rem(s * cells + index + total_cells, total_cells)
        return 2.0 * math.pi * (whole.astype(jnp.float32) + 0.5) / total_cells

    ring_angle = angle_of(row_iota(24) - 1)
    ring_sin, ring_cos = jnp.sin(ring_angle), jnp.cos(ring_angle)
    lane_cell = lax.rem(lane, group) // 2 - 1
    lane_angle = angle_of(lane_cell)
    lane_sin, lane_cos = jnp.sin(lane_angle), jnp.cos(lane_angle)

    own_wall.wait()
    lane8 = lane_iota(8)
    highs, lows = [], []
    for c in range(3):
        high = jnp.zeros((8, LANES), jnp.float32)
        low = high
        for i in range(cells):
            spot = c * group + 2 * (i + 1)
            turned = roll(V[c, i + 2, pl.ds(base, 8), :], spot + 2)
            high = jnp.where(lane8 // 2 == spot // 2, turned, high)
            low = jnp.where(lane8 // 2 == spot // 2 + 1, turned, low)
        highs.append(high)
        lows.append(low)
    high8 = highs[0] + highs[1] + highs[2]
    low8 = roll(lows[0] + lows[1] + lows[2], -2)
    TRw[...] = high8
    TLw[...] = low8

    def remote(src, dst, sent, arrived, span, sector):
        return pltpu.make_async_remote_copy(
            src_ref=src,
            dst_ref=dst,
            send_sem=sent,
            recv_sem=arrived,
            device_id={"span": span, "sector": sector},
            device_id_type=MESH,
        )

    spread = [
        (0, 0, right, s),
        (1, 1, left, s),
        (0, 2, right, upper),
        (1, 3, left, upper),
        (0, 4, right, lower),
        (1, 5, left, lower),
    ]
    near_copies = [
        remote(
            (TRw, TLw)[which], near.at[slot], send_sem.at[slot], near_sem.at[slot], span, sector
        )
        for which, slot, span, sector in spread
    ]
    full_copies = [
        remote(
            (TR, TL)[which], full.at[slot], send_sem.at[6 + slot], full_sem.at[slot], span, sector
        )
        for which, slot, span, sector in spread
    ]
    theta_copies = []
    for part, (start, size) in enumerate(((0, 8), (8, rows - 8))):
        theta_copies.append(
            remote(
                vel.at[:, pl.ds(0, 2), pl.ds(start, size), :],
                V.at[:, pl.ds(cells + 2, 2), pl.ds(base + start, size), :],
                send_sem.at[12 + 2 * part],
                theta_sem.at[2 * part],
                k,
                lower,
            )
        )
        theta_copies.append(
            remote(
                vel.at[:, pl.ds(cells - 2, 2), pl.ds(start, size), :],
                V.at[:, pl.ds(0, 2), pl.ds(base + start, size), :],
                send_sem.at[13 + 2 * part],
                theta_sem.at[1 + 2 * part],
                k,
                upper,
            )
        )

    for copy in small:
        copy.wait()
    current = jnp.zeros((1, LANES), jnp.float32)
    for b in range(speed.shape[0]):
        current = current + jnp.where(cbin[...] == b, speed[b], 0.0)
    face_row = row_iota(24) - 1
    face_weight = jnp.zeros((24, LANES), jnp.float32)
    for q in range(weight.shape[0]):
        face_weight = face_weight + jnp.where(face_row == face[q], weight[q], 0.0)
    coef[0] = face_weight * ring_cos
    coef[1] = face_weight * ring_sin
    coef[2] = -current * ring_sin
    coef[3] = current * ring_cos
    cur_high = jnp.sum(jnp.where(lane == LANES - 1, current, 0.0), axis=1, keepdims=True)
    cur_low = jnp.sum(jnp.where(lane == 0, current, 0.0), axis=1, keepdims=True)
    wide = lane_iota(rows)
    TR[...] = jnp.where(wide == 3 * group + 1, cur_high, 0.0)
    TL[...] = jnp.where(wide == 3 * group + 2, cur_low, 0.0)
    own_bulk.wait()

    @pl.loop(0, cells)
    def _(i):
        high, low = TR[...], TL[...]
        for c in range(3):
            spot = c * group + 2 * (i + 1)
            turned = roll(V[c, i + 2, pl.ds(base, rows), :], spot + 2)
            high = jnp.where(wide // 2 == spot // 2, turned, high)
            low = jnp.where(wide // 2 == spot // 2 + 1, turned, low)
        TR[...] = high
        TL[...] = low

    TL[...] = roll(TL[...], -2)
    pl.semaphore_wait(barrier, len(close))
    for copy in near_copies[2:] + near_copies[:2] + theta_copies[:2]:
        copy.start()
    begin(0)
    for copy in full_copies[2:] + full_copies[:2] + theta_copies[2:]:
        copy.start()

    message, answers, steps, inverse = slab_system(tens[...], mass)
    KB[pl.ds(k, 1), 0, :] = message
    for n in range(ring_rounds):
        finish(n)
        begin(n + 1)

    def everyone(buffer, sent, arrived):
        far = [(dy, dz) for dy in range(ny) for dz in range(nz) if (dy, dz) != (0, 0)]
        far.sort(key=lambda d: -(min(d[0], ny - d[0]) + min(d[1], nz - d[1])))
        for dy, dz in far:
            remote(buffer.at[k], buffer.at[k], sent, arrived, torus(dy, dz), s).start()

    def ghosts(boxes, high, low, depth, store):
        here = lane_iota(depth)
        evens = here % 2 == 0
        at_low = here * 0 + low_end == 1
        at_high = here * 0 + high_end == 1
        ahead = lambda x: roll(x, -1)
        behind = lambda x: roll(x, 1)
        centre = jnp.where(
            evens,
            jnp.where(at_low, low, ahead(boxes[0])),
            jnp.where(at_high, high, behind(boxes[1])),
        )
        outer = jnp.where(
            evens, jnp.where(at_low, low, boxes[0]), jnp.where(at_high, high, boxes[1])
        )
        inner = jnp.where(
            evens, jnp.where(at_low, ahead(low), low), jnp.where(at_high, behind(high), high)
        )
        down = roll(jnp.where(evens, ahead(boxes[2]), behind(boxes[3])), -2 * cells)
        up = roll(jnp.where(evens, ahead(boxes[4]), behind(boxes[5])), 2 * cells)
        own_down, own_up = jnp.zeros_like(down), jnp.zeros_like(up)
        for c in range(3):
            spot = c * group
            turned = roll(V[c, 1, pl.ds(base, depth), :], spot + 1)
            own_down = jnp.where(here // 2 == spot // 2, turned, own_down)
            spot = c * group + 2 * (cells + 1)
            turned = roll(V[c, cells + 2, pl.ds(base, depth), :], spot + 1)
            own_up = jnp.where(here // 2 == spot // 2, turned, own_up)
        own = own_down + own_up
        own = jnp.where(evens, ahead(own), behind(own))
        mirrored = jnp.where(evens, low_end, high_end) == 1
        cell = lax.rem(here, group) // 2 - 1
        in_fields = here < 3 * group
        centre = jnp.where(
            in_fields & (cell == -1),
            jnp.where(mirrored, own, down),
            jnp.where(in_fields & (cell == cells), jnp.where(mirrored, own, up), centre),
        )
        return centre, outer, inner

    def ghost_rates(centre, outer, inner, depth, top):
        here = lane_iota(depth)
        evens = here % 2 == 0
        which = here // group
        ups = {n: roll(centre, n * group) for n in (-2, -1, 1, 2)}
        of = lambda d: jnp.where(
            which == d,
            centre,
            jnp.where(
                which == (d + 1) % 3,
                ups[1] if d < 2 else ups[-2],
                ups[2] if d == 0 else ups[-1],
            ),
        )
        c0, c1, c2 = of(0), of(1), of(2)
        tu, td = roll(centre, -2), roll(centre, 2)
        sub = row_iota(depth)
        ru, rd = roll(centre, -1, 0), roll(centre, 1, 0)
        rd = jnp.where(sub == 0, -centre, rd)
        if top is not None:
            ru = jnp.where(sub == depth - 1, top, ru)
        su, sd = jnp.where(evens, inner, outer), jnp.where(evens, outer, inner)
        return combine(centre, c0, c1, c2, tu, td, ru, rd, su, sd)

    def combine(centre, c0, c1, c2, tu, td, ru, rd, su, sd):
        laplace = (tu + td) + (ru + rd) + (su + sd) - 6.0 * centre
        advect = c0 * (tu - td) + c1 * (ru - rd) + c2 * (su - sd)
        return NU_DT * laplace - (0.5 * ADV_DT) * advect

    def beside(centre, edge, at):
        left_end, right_end = lane_iota(8) == 0, lane_iota(8) == LANES - 1
        turned = roll(edge, lax.rem(2 * LANES - 1 - at, LANES))
        up = roll(jnp.where(left_end, turned, centre), -1)
        down = roll(jnp.where(right_end, turned, centre), 1)
        return up, down

    for copy in near_copies + theta_copies[:2]:
        copy.wait_recv()
    centre, outer, inner = ghosts([near[n] for n in range(6)], high8, low8, 8, None)
    edge1 = centre
    edge2 = centre + ghost_rates(centre, outer, inner, 8, None)

    def wall_rates(field, lift, i, edge, fields):
        here = [field(c, i) for c in range(3)]
        rates = []
        for c in range(fields):
            centre = here[c]
            su, sd = beside(centre, edge, c * group + 2 * (i + 1))
            ru = roll(centre, -1, 0)
            rd = jnp.where(row8 == 0, -centre, roll(centre, 1, 0))
            rates.append(
                combine(
                    centre, here[0], here[1], here[2], field(c, i + 1), field(c, i - 1), ru, rd, su, sd
                )
            )
        return here, rates

    @pl.loop(0, (cells + 2) // 6)
    def _(block):
        for n in range(6):
            n = block * 6 + n
            here, rates = wall_rates(
                lambda c, i: V[c, i + 2, pl.ds(base, 8), :], None, n - 1, edge1, 3
            )
            for c in range(3):
                W[c, n] = here[c] + rates[c]

    def wall_block(block, sums):
        for n in range(8):
            sums = wall_sum(block * 8 + n, sums)
        return sums

    def wall_sum(i, sums):
        x, y = sums
        here, rates = wall_rates(lambda c, i: W[c, i + 1], None, i, edge2, 2)
        fresh = [
            0.5 * (V[c, i + 2, pl.ds(base, 8), :] + here[c] + rates[c]) for c in range(2)
        ]
        wc, ws = coef[0, pl.ds(i + 1, 1), :], coef[1, pl.ds(i + 1, 1), :]
        return (
            x + 2.0 * WALL_NU * (fresh[1] * wc - fresh[0] * ws),
            y + 2.0 * WALL_NU * (fresh[1] * ws + fresh[0] * wc),
        )

    zero8 = jnp.zeros((8, LANES), jnp.float32)
    fx, fy = lax.fori_loop(0, cells // 8, wall_block, (zero8, zero8))
    FB[s] = jnp.concatenate([fx[0:1], fy[0:1]], axis=0)

    @pl.loop(1, ring)
    def _(d):
        remote(FB.at[s], FB.at[s], send_sem.at[17], force_sem, k, lax.rem(s + d, ring)).start()

    finish(ring_rounds)
    begin(ring_rounds + 1)

    for copy in full_copies + theta_copies[2:]:
        copy.wait_recv()
    centre, outer, inner = ghosts([full[n] for n in range(6)], TR[...], TL[...], rows, None)
    PG[...] = centre
    cur_lo = jnp.sum(
        jnp.where(lane == 3 * group, centre[0:1], 0.0), axis=1, keepdims=True
    )
    cur_hi = jnp.sum(
        jnp.where(lane == 3 * group + 1, centre[0:1], 0.0), axis=1, keepdims=True
    )
    cur_side = jnp.where(lane % 2 == 0, cur_lo, cur_hi)
    top = jnp.where(
        lane // group == 0,
        -cur_side * lane_sin,
        jnp.where(lane // group == 1, cur_side * lane_cos, 0.0),
    )
    UG[...] = centre + ghost_rates(centre, outer, inner, rows, top)

    def outer_rows(i):
        return coef[2, pl.ds(i + 1, 1), :], coef[3, pl.ds(i + 1, 1), :], jnp.zeros((1, LANES), jnp.float32)

    @pl.loop(0, cells + 2)
    def _(n):
        for c, value in enumerate(outer_rows(n - 1)):
            V[c, n + 1, pl.ds(base + rows, 1), :] = value
            V[c, n + 1, pl.ds(base - 1, 1), :] = -V[c, n + 1, pl.ds(base, 1), :]

    def bulk_rates(field, edge, i, t):
        start = base + 8 * t
        here = [field(c, i, start) for c in range(3)]
        rates = []
        for c in range(3):
            su, sd = beside(here[c], edge[pl.ds(8 * t, 8), :], c * group + 2 * (i + 1))
            rates.append(
                combine(
                    here[c],
                    here[0],
                    here[1],
                    here[2],
                    field(c, i + 1, start),
                    field(c, i - 1, start),
                    field(c, i, start + 1),
                    field(c, i, start - 1),
                    su,
                    sd,
                )
            )
        return here, rates

    @pl.loop(0, cells + 2)
    def _(n):
        for t in range(tiles):
            here, rates = bulk_rates(
                lambda c, i, start: V[c, i + 2, pl.ds(start, 8), :], PG, n - 1, t
            )
            for c in range(3):
                fresh = here[c] + rates[c]
                U[c, n, pl.ds(base + 8 * t, 8), :] = fresh
                if t == 0:
                    U[c, n, pl.ds(base - 1, 1), :] = -fresh[0:1]
        for c, value in enumerate(outer_rows(n - 1)):
            U[c, n, pl.ds(base + rows, 1), :] = value

    finish(ring_rounds + 1)
    everyone(KB, send_sem.at[16], stiff_sem)

    arrivals = ring - 1
    pltpu.make_async_copy(
        FB.at[pl.ds(0, arrivals)], FB.at[pl.ds(0, arrivals)], force_sem
    ).wait()
    force = FB[0]
    for n in range(1, ring):
        force = force + FB[n]
    force_out[...] = force
    load = force * LANES ** (-1.5) + mass * (disp[...] + rate[...])
    load8 = wide_loads(load)
    RB[pl.ds(k, 1), 0, :] = end_loads(answers, load8)

    everyone(RB, send_sem.at[18], load_sem)

    @pl.loop(0, cells)
    def _(i):
        for t in range(tiles):
            here, rates = bulk_rates(
                lambda c, i, start: U[c, i + 1, pl.ds(start, 8), :], UG, i, t
            )
            for c in range(3):
                out[c, i, pl.ds(8 * t, 8), :] = 0.5 * (
                    V[c, i + 2, pl.ds(base + 8 * t, 8), :] + here[c] + rates[c]
                )

    others = count - 1
    pltpu.make_async_copy(KB.at[pl.ds(0, others)], KB.at[pl.ds(0, others)], stiff_sem).wait()
    spare = jnp.zeros((LANES - count, LANES), jnp.float32)
    numbers = jnp.concatenate([KB[:, 0, :], spare], axis=0).T
    blocks = chain_response(numbers, count, k, mass)
    blocks.append(jnp.zeros((LANES - 32, LANES), jnp.float32))
    response = jnp.concatenate(blocks, axis=0).T[0:count]
    rest = inner_deflection(steps, inverse, load8)

    pltpu.make_async_copy(RB.at[pl.ds(0, others)], RB.at[pl.ds(0, others)], load_sem).wait()
    ends = ends_solved(response, RB[:, 0, :])
    moved = ends * answers
    for direction in range(2):
        mine = jnp.sum(jnp.where(row8 % 2 == direction, moved, 0.0), axis=0, keepdims=True)
        defl_out[pl.ds(direction, 1), :] = rest[direction : direction + 1] + mine

    for copy in near_copies + full_copies + theta_copies:
        copy.wait_send()
    for sent, size, buffer in ((16, others, KB), (17, arrivals, FB), (18, others, RB)):
        pltpu.make_async_copy(
            buffer.at[pl.ds(0, size)], buffer.at[pl.ds(0, size)], send_sem.at[sent]
        ).wait()


def hand_over(fresh, force, defl, fresh_out, force_out, defl_out, sem):
    copies = [
        pltpu.make_async_copy(src, dst, sem.at[n])
        for n, (src, dst) in enumerate(
            ((fresh, fresh_out), (force, force_out), (defl, defl_out))
        )
    ]
    for copy in copies:
        copy.start()
    for copy in copies:
        copy.wait()


def solution(mesh):
    count, ring = mesh.shape["span"], mesh.shape["sector"]

    def local(velocity, speed, cbin, face, weight, tension, displacement, beam_rate):
        cells, rows, sections = velocity.shape[1:]
        far = pl.BlockSpec(memory_space=pltpu.HBM)
        vmem = pl.BlockSpec(memory_space=pltpu.VMEM)
        tall = rows + 16
        f32 = jnp.float32
        shapes = (
            jax.ShapeDtypeStruct(velocity.shape, f32),
            jax.ShapeDtypeStruct((2, sections), f32),
            jax.ShapeDtypeStruct((2, sections), f32),
        )
        results = pl.pallas_call(
            lambda *refs: kernel(count, ring, *refs),
            out_shape=shapes,
            in_specs=[far] * 8,
            out_specs=(vmem,) * 3,
            scratch_shapes=[
                pltpu.VMEM((3, cells + 4, tall, LANES), f32),
                pltpu.VMEM((3, cells + 2, tall, LANES), f32),
                pltpu.VMEM((3, cells + 2, 8, LANES), f32),
                pltpu.VMEM((rows, LANES), f32),
                pltpu.VMEM((rows, LANES), f32),
                pltpu.VMEM((8, LANES), f32),
                pltpu.VMEM((8, LANES), f32),
                pltpu.VMEM((6, 8, LANES), f32),
                pltpu.VMEM((6, rows, LANES), f32),
                pltpu.VMEM((rows, LANES), f32),
                pltpu.VMEM((rows, LANES), f32),
                pltpu.VMEM((ring, 2, LANES), f32),
                pltpu.VMEM((count, 1, LANES), f32),
                pltpu.VMEM((count, 1, LANES), f32),
                pltpu.VMEM((4, 24, LANES), f32),
                pltpu.SMEM(speed.shape, f32),
                pltpu.VMEM((1, sections), jnp.int32),
                pltpu.SMEM(face.shape, jnp.int32),
                pltpu.SMEM(weight.shape, f32),
                pltpu.VMEM((1, sections), f32),
                pltpu.VMEM((2, sections), f32),
                pltpu.VMEM((2, sections), f32),
                pltpu.SemaphoreType.DMA((2,)),
                pltpu.SemaphoreType.DMA((7,)),
                pltpu.SemaphoreType.DMA((19,)),
                pltpu.SemaphoreType.DMA((4,)),
                pltpu.SemaphoreType.DMA((6,)),
                pltpu.SemaphoreType.DMA((6,)),
                pltpu.SemaphoreType.DMA,
                pltpu.SemaphoreType.DMA,
                pltpu.SemaphoreType.DMA,
                pltpu.SemaphoreType.REGULAR((6,)),
            ],
            compiler_params=pltpu.CompilerParams(
                collective_id=0, has_side_effects=True, vmem_limit_bytes=24 << 20
            ),
            name="riser",
        )(
            *[pltpu.with_memory_space_constraint(x, pltpu.HBM) for x in (velocity,
            speed,
            cbin.reshape(1, sections),
            face,
            weight,
            tension.reshape(1, sections),
            displacement,
            beam_rate)],
        )
        return pl.pallas_call(
            hand_over,
            out_shape=shapes,
            in_specs=[vmem] * 3,
            out_specs=(far,) * 3,
            scratch_shapes=[pltpu.SemaphoreType.DMA((3,))],
            name="results",
        )(*[pltpu.with_memory_space_constraint(x, pltpu.VMEM) for x in results])

    return jax.shard_map(
        local,
        mesh=mesh,
        in_specs=(
            P(None, "sector", None, "span"),
            P(),
            P("span"),
            P("sector"),
            P("sector"),
            P("span"),
            P(None, "span"),
            P(None, "span"),
        ),
        out_specs=(P(None, "sector", None, "span"), P(None, "span"), P(None, "span")),
        check_vma=False,
    )
```

```python
import math

import jax
import jax.numpy as jnp
from jax import lax
from jax.experimental import pallas as pl
from jax.experimental.pallas import tpu as pltpu
from jax.sharding import PartitionSpec as P

MESH = pl.DeviceIdType.MESH
NU_DT = 0.15
ADV_DT = 0.1
WALL_NU = 0.5
BEAM_EI = 0.5
BEAM_MASS = 0.4
LANES = 128
CUTS = (3, 9)


def roll(x, shift, axis=1):
    size = x.shape[axis]
    return pltpu.roll(x, shift % size if isinstance(shift, int) else shift, axis)


def lane_iota(rows):
    return lax.broadcasted_iota(jnp.int32, (rows, LANES), 1)


def row_iota(rows):
    return lax.broadcasted_iota(jnp.int32, (rows, LANES), 0)


def reduce_chain(A, D, F, rho_of, strides):
    A00, A01, A10, A11 = A
    D00, D01, D11 = D
    Fw, Fs = F
    steps = []
    for s in strides:
        inv = 1.0 / (D00 * D11 - D01 * D01)
        I00, I01, I11 = D11 * inv, -D01 * inv, D00 * inv
        P00 = I00 * A00 + I01 * A10
        P01 = I00 * A01 + I01 * A11
        P10 = I01 * A00 + I11 * A10
        P11 = I01 * A01 + I11 * A11
        E11 = A01 * P01 + A11 * P11
        I00m, I01m, I11m = roll(I00, s), roll(I01, s), roll(I11, s)
        al00 = A00 * I00m + A01 * I01m
        al01 = A00 * I01m + A01 * I11m
        al10 = A10 * I00m + A11 * I01m
        al11 = A10 * I01m + A11 * I11m
        ga00, ga01, ga10, ga11 = roll(P00, -s), roll(P10, -s), roll(P01, -s), roll(P11, -s)
        steps.append((al00, al01, al10, al11, ga00, ga01, ga10, ga11))
        P00m, P01m, P10m, P11m = roll(P00, s), roll(P01, s), roll(P10, s), roll(P11, s)
        D11 = D11 - (al10 * A10 + al11 * A11) - roll(E11, -s)
        Fw, Fs = reduce_load(steps[-1], Fw, Fs, s)
        A00, A01, A10, A11 = (
            -(A00 * P00m + A01 * P10m),
            -(A00 * P01m + A01 * P11m),
            -(A10 * P00m + A11 * P10m),
            -(A10 * P01m + A11 * P11m),
        )
        rw, rs = rho_of(Fw, Fs)
        D00 = rw - A00 - roll(A00, -2 * s)
        D01 = rs - A10 - roll(A01, -2 * s)
    inv = 1.0 / (D00 * D11 - D01 * D01)
    last = (D11 * inv, -D01 * inv, D00 * inv)
    return last[0] * Fw + last[1] * Fs, last[1] * Fw + last[2] * Fs, steps, last


def reduce_load(step, Fw, Fs, s):
    al00, al01, al10, al11, ga00, ga01, ga10, ga11 = step
    Fwm, Fsm, Fwp, Fsp = roll(Fw, s), roll(Fs, s), roll(Fw, -s), roll(Fs, -s)
    return (
        Fw - (al00 * Fwm + al01 * Fsm) - (ga00 * Fwp + ga01 * Fsp),
        Fs - (al10 * Fwm + al11 * Fsm) - (ga10 * Fwp + ga11 * Fsp),
    )


def slab_system(t, mass):
    lane = lane_iota(1)
    g = t / 30.0
    gn = roll(g, -1)
    a00, a01, a10, a11 = (
        -12.0 * BEAM_EI - 36.0 * g,
        -6.0 * BEAM_EI - 3.0 * g,
        6.0 * BEAM_EI + 3.0 * g,
        2.0 * BEAM_EI - g,
    )
    n00, n01, n10, n11 = roll(a00, -1), roll(a01, -1), roll(a10, -1), roll(a11, -1)
    d00 = (12.0 * BEAM_EI + 36.0 * g) + (12.0 * BEAM_EI + 36.0 * gn) + mass
    d01 = (-6.0 * BEAM_EI - 3.0 * g) + (6.0 * BEAM_EI + 3.0 * gn)
    d11 = (4.0 * BEAM_EI + 4.0 * g) + (4.0 * BEAM_EI + 4.0 * gn)
    inside = lane < LANES - 1
    rho_w = jnp.where(inside, (d00 - jnp.maximum(-a00, -n00)) - jnp.minimum(-a00, -n00), 0.0)
    rho_s = jnp.where(inside, (d01 + a10) + n01, 0.0)
    first, last, end = lane == 0, lane == LANES - 2, lane == LANES - 1
    zero = jnp.zeros_like(t)
    row = row_iota(8)

    def stack(rows):
        out = jnp.zeros((8, LANES), jnp.float32)
        for index, value in enumerate(rows):
            out = jnp.where(row == index, value, out)
        return out

    Fw = stack(
        [
            rho_w,
            jnp.where(first, -a00, zero),
            jnp.where(first, -a01, zero),
            jnp.where(last, -n00, jnp.where(end, 1.0, zero)),
            jnp.where(last, -n10, zero),
        ]
    )
    Fs = stack(
        [
            rho_s,
            jnp.where(first, -a10, zero),
            jnp.where(first, -a11, zero),
            jnp.where(last, -n01, zero),
            jnp.where(last, -n11, jnp.where(end, 1.0, zero)),
        ]
    )
    coupled = jnp.logical_and(lane > 0, inside)
    A = tuple(jnp.where(coupled, x, 0.0) for x in (a00, a01, a10, a11))
    D = (jnp.where(inside, d00, 1.0), jnp.where(inside, d01, 0.0), jnp.where(inside, d11, 1.0))

    def rho_of(Fw, Fs):
        return Fw[0:1] + Fw[1:2] + Fw[3:4], Fs[0:1] + Fs[1:2] + Fs[3:4]

    Zw, Zs, steps, inverse = reduce_chain(A, D, (Fw, Fs), rho_of, [1 << b for b in range(7)])
    yw, ys = Zw[0:1], Zs[0:1]
    xa1w, xa1s = Zw[2:3], Zs[2:3]
    xb0w, xb0s, xb1w, xb1s = Zw[3:4], Zs[3:4], Zw[4:5], Zs[4:5]
    numbers = [
        (0, xb0w * a00 + xb0s * a10),
        (0, xb0w * a01 + xb0s * a11),
        (0, xb1w * a00 + xb1s * a10),
        (0, xb1w * a01 + xb1s * a11),
        (0, -(a00 * yw + a10 * ys)),
        (0, -(a01 * yw + a11 * ys)),
        (0, (4.0 * BEAM_EI + 4.0 * g) + (a01 * xa1w + a11 * xa1s)),
        (LANES - 2, -(n00 * yw + n01 * ys)),
        (LANES - 2, -(n10 * yw + n11 * ys)),
        (LANES - 2, (4.0 * BEAM_EI + 4.0 * gn) + (n10 * xb1w + n11 * xb1s)),
    ]
    row16 = row_iota(16)
    table = jnp.zeros((16, LANES), jnp.float32)
    for index, (spot, value) in enumerate(numbers):
        table = jnp.where((row16 == index) & (lane == spot), value, table)
    column = jnp.sum(table, axis=1, keepdims=True)
    message = jnp.sum(jnp.where(lane_iota(16) == row16, column, 0.0), axis=0, keepdims=True)
    answers = jnp.zeros((8, LANES), jnp.float32)
    for u in range(4):
        answers = jnp.where(row // 2 == u, Zw[u + 1 : u + 2], answers)
    return message, answers, steps, inverse


def chain_response(numbers, count, place, mass):
    lane = lane_iota(1)
    valid = lane < count
    row = row_iota(8)
    pick = lambda n: jnp.where(valid, numbers[n : n + 1], 0.0)
    a00, a01, a10, a11 = pick(0), pick(1), pick(2), pick(3)
    raw, ras, ka11, rbw, rbs, kb11 = [pick(n) for n in range(4, 10)]
    above = lambda x: jnp.where(lane < count - 1, roll(x, -1), 0.0)
    first = lane == 0
    rw = rbw + above(raw) + mass - jnp.where(first, a00, 0.0)
    rs = rbs + above(ras) - jnp.where(first, a10, 0.0)
    rw = jnp.where(valid, rw, 1.0)
    rs = jnp.where(valid, rs, 0.0)
    d11 = jnp.where(valid, kb11 + above(ka11), 1.0)
    A = tuple(jnp.where(first, 0.0, x) for x in (a00, a01, a10, a11))
    d00 = rw - A[0] - roll(A[0], -1)
    d01 = rs - A[2] - roll(A[1], -1)
    lane8 = lane_iota(8)
    mine = lane8 == place
    before = lane8 == place - 1
    Fw = jnp.where((before & (row == 0)) | (mine & (row == 2)), 1.0, 0.0)
    Fs = jnp.where((before & (row == 1)) | (mine & (row == 3)), 1.0, 0.0)
    Fw = jnp.where(row == 4, rw, Fw)
    Fs = jnp.where(row == 4, rs, Fs)
    strides = []
    while (1 << len(strides)) < count:
        strides.append(1 << len(strides))
    Gw, Gs, _, _ = reduce_chain(
        A, (d00, d01, d11), (Fw, Fs), lambda w, s: (w[4:5], s[4:5]), strides
    )
    Hw, Hs = roll(Gw, 1), roll(Gs, 1)
    blocks = []
    for u in range(4):
        block = jnp.where(row // 2 == 0, Hw[u : u + 1], 0.0)
        block = jnp.where(row // 2 == 1, Hs[u : u + 1], block)
        block = jnp.where(row // 2 == 2, Gw[u : u + 1], block)
        blocks.append(jnp.where(row // 2 == 3, Gs[u : u + 1], block))
    return blocks


def wide_loads(load):
    row = row_iota(8)
    return jnp.where(row % 2 == 0, load[0:1], load[1:2])


def end_loads(answers, load8):
    total = jnp.sum(answers * load8, axis=1, keepdims=True)
    lane = lane_iota(8)
    keep = (lane % 8 == row_iota(8)) & (lane < 32)
    return jnp.sum(jnp.where(keep, total, 0.0), axis=0, keepdims=True)


def ends_solved(response, loads):
    total = jnp.sum(response * loads, axis=0, keepdims=True)
    lane, row = lane_iota(8), row_iota(8)
    keep = (lane // 8 == row // 2) & (lane % 2 == row % 2) & (lane < 32)
    return jnp.sum(jnp.where(keep, total, 0.0), axis=1, keepdims=True)


def inner_deflection(steps, inverse, load8):
    inside = lane_iota(8) < LANES - 1
    Fw, Fs = jnp.where(inside, load8, 0.0), jnp.zeros((8, LANES), jnp.float32)
    for b in range(7):
        Fw, Fs = reduce_load(steps[b], Fw, Fs, 1 << b)
    return inverse[0] * Fw + inverse[1] * Fs


def kernel(
    count,
    ring,
    vel_hbm,
    speed_hbm,
    cbin_hbm,
    face_hbm,
    weight_hbm,
    tens_hbm,
    disp_hbm,
    rate_hbm,
    out,
    force_out,
    defl_out,
    V,
    U,
    W,
    TR,
    TL,
    TRw,
    TLw,
    near,
    full,
    PG,
    UG,
    FB,
    KB,
    RB,
    coef,
    speed,
    cbin,
    face,
    weight,
    tens,
    disp,
    rate,
    own_sem,
    small_sem,
    send_sem,
    theta_sem,
    near_sem,
    full_sem,
    force_sem,
    stiff_sem,
    load_sem,
    round_sem,
    shifts,
):
    vel = vel_hbm
    cells, rows = vel.shape[1], vel.shape[2]
    tiles = rows // 8
    base = 8
    k = lax.axis_index("span")
    s = lax.axis_index("sector")
    left, right = lax.rem(k + count - 1, count), lax.rem(k + 1, count)
    turn = lambda d: lax.rem(s + d + ring, ring)
    lower, upper = turn(-1), turn(1)
    ny = 4 if count >= 32 else 2
    nz = count // ny
    y, z = k // nz, lax.rem(k, nz)

    def torus(dy, dz):
        return lax.rem(y + dy + ny, ny) * nz + lax.rem(z + dz + nz, nz)

    low_end = jnp.where(k == 0, 1, 0)
    high_end = jnp.where(k == count - 1, 1, 0)
    mass = BEAM_MASS / LANES**2
    stride = cells + 2
    group = 2 * stride

    barrier = pltpu.get_barrier_semaphore()

    def signal(semaphore, span, sector):
        pl.semaphore_signal(
            semaphore, inc=1, device_id={"span": span, "sector": sector}, device_id_type=MESH
        )

    close = [(side, way) for side in (left, right) for way in (lower, upper)]
    close += [(left, s), (right, s)] + [(k, turn(d)) for d in range(1, ring)]
    close += [(torus(1, 0), s), (torus(-1, 0), s), (torus(0, 1), s), (torus(0, -1), s)]
    own_wall = pltpu.make_async_copy(
        vel.at[:, :, pl.ds(0, 8), :],
        V.at[:, pl.ds(2, cells), pl.ds(base, 8), :],
        own_sem.at[0],
    )
    own_bulk = pltpu.make_async_copy(
        vel.at[:, :, pl.ds(8, rows - 8), :],
        V.at[:, pl.ds(2, cells), pl.ds(base + 8, rows - 8), :],
        own_sem.at[1],
    )
    small = [
        pltpu.make_async_copy(src, dst, small_sem.at[n])
        for n, (src, dst) in enumerate(
            (
                (speed_hbm, speed),
                (cbin_hbm, cbin),
                (face_hbm, face),
                (weight_hbm, weight),
                (tens_hbm, tens),
                (disp_hbm, disp),
                (rate_hbm, rate),
            )
        )
    ]
    own_wall.start()
    for copy in small:
        copy.start()
    own_bulk.start()


    for span, sector in close:
        signal(barrier, span, sector)

    rounds = []
    known = 1
    while known < nz // 2:
        rounds.append([(torus(0, known), s), (torus(0, -known), s)])
        known *= 2
    rounds += [[(torus(1, 0), s), (torus(-1, 0), s)]] * 2

    def begin(n):
        for span, sector in rounds[n]:
            signal(round_sem.at[n], span, sector)

    def finish(n):
        pl.semaphore_wait(round_sem.at[n], len(rounds[n]))

    lane = lane_iota(1)
    row8 = row_iota(8)
    total_cells = cells * ring

    def angle_of(index):
        whole = lax.rem(s * cells + index + total_cells, total_cells)
        return 2.0 * math.pi * (whole.astype(jnp.float32) + 0.5) / total_cells

    ring_angle = angle_of(row_iota(24) - 1)
    ring_sin, ring_cos = jnp.sin(ring_angle), jnp.cos(ring_angle)
    lane_cell = lax.rem(lane, group) // 2 - 1
    lane_angle = angle_of(lane_cell)
    lane_sin, lane_cos = jnp.sin(lane_angle), jnp.cos(lane_angle)

    from_lane = lax.broadcasted_iota(jnp.int32, (LANES, 2 * LANES), 0)
    to_lane = lax.broadcasted_iota(jnp.int32, (LANES, 2 * LANES), 1)
    source = jnp.where(to_lane < LANES, to_lane + 1, to_lane - LANES - 1)
    source = jnp.where(to_lane == LANES - 1, -1, source)
    shifts[...] = jnp.where(from_lane == source, 1.0, 0.0).astype(jnp.bfloat16)

    own_wall.wait()
    lane8 = lane_iota(8)
    highs, lows = [], []
    for c in range(3):
        high = jnp.zeros((8, LANES), jnp.float32)
        low = high
        for i in range(cells):
            spot = c * group + 2 * (i + 1)
            turned = roll(V[c, i + 2, pl.ds(base, 8), :], spot + 2)
            high = jnp.where(lane8 // 2 == spot // 2, turned, high)
            low = jnp.where(lane8 // 2 == spot // 2 + 1, turned, low)
        highs.append(high)
        lows.append(low)
    high8 = highs[0] + highs[1] + highs[2]
    low8 = roll(lows[0] + lows[1] + lows[2], -2)
    TRw[...] = high8
    TLw[...] = low8

    def remote(src, dst, sent, arrived, span, sector):
        return pltpu.make_async_remote_copy(
            src_ref=src,
            dst_ref=dst,
            send_sem=sent,
            recv_sem=arrived,
            device_id={"span": span, "sector": sector},
            device_id_type=MESH,
        )

    spread = [
        (0, 0, right, s),
        (1, 1, left, s),
        (0, 2, right, upper),
        (1, 3, left, upper),
        (0, 4, right, lower),
        (1, 5, left, lower),
    ]
    near_copies = [
        remote(
            (TRw, TLw)[which], near.at[slot], send_sem.at[slot], near_sem.at[slot], span, sector
        )
        for which, slot, span, sector in spread
    ]
    full_copies = [
        remote(
            (TR, TL)[which], full.at[slot], send_sem.at[6 + slot], full_sem.at[slot], span, sector
        )
        for which, slot, span, sector in spread
    ]
    theta_copies = []
    for part, (start, size) in enumerate(((0, 8), (8, rows - 8))):
        theta_copies.append(
            remote(
                vel.at[:, pl.ds(0, 2), pl.ds(start, size), :],
                V.at[:, pl.ds(cells + 2, 2), pl.ds(base + start, size), :],
                send_sem.at[12 + 2 * part],
                theta_sem.at[2 * part],
                k,
                lower,
            )
        )
        theta_copies.append(
            remote(
                vel.at[:, pl.ds(cells - 2, 2), pl.ds(start, size), :],
                V.at[:, pl.ds(0, 2), pl.ds(base + start, size), :],
                send_sem.at[13 + 2 * part],
                theta_sem.at[1 + 2 * part],
                k,
                upper,
            )
        )

    for copy in small:
        copy.wait()
    current = jnp.zeros((1, LANES), jnp.float32)
    for b in range(speed.shape[0]):
        current = current + jnp.where(cbin[...] == b, speed[b], 0.0)
    face_row = row_iota(24) - 1
    face_weight = jnp.zeros((24, LANES), jnp.float32)
    for q in range(weight.shape[0]):
        face_weight = face_weight + jnp.where(face_row == face[q], weight[q], 0.0)
    coef[0] = face_weight * ring_cos
    coef[1] = face_weight * ring_sin
    coef[2] = -current * ring_sin
    coef[3] = current * ring_cos
    cur_high = jnp.sum(jnp.where(lane == LANES - 1, current, 0.0), axis=1, keepdims=True)
    cur_low = jnp.sum(jnp.where(lane == 0, current, 0.0), axis=1, keepdims=True)
    wide = lane_iota(rows)
    TR[...] = jnp.where(wide == 3 * group + 1, cur_high, 0.0)
    TL[...] = jnp.where(wide == 3 * group + 2, cur_low, 0.0)
    own_bulk.wait()

    @pl.loop(0, cells)
    def _(i):
        high, low = TR[...], TL[...]
        for c in range(3):
            spot = c * group + 2 * (i + 1)
            turned = roll(V[c, i + 2, pl.ds(base, rows), :], spot + 2)
            high = jnp.where(wide // 2 == spot // 2, turned, high)
            low = jnp.where(wide // 2 == spot // 2 + 1, turned, low)
        TR[...] = high
        TL[...] = low

    TL[...] = roll(TL[...], -2)
    pl.semaphore_wait(barrier, len(close))
    for copy in near_copies[2:] + near_copies[:2] + theta_copies[:2]:
        copy.start()
    begin(0)
    for copy in full_copies[2:] + full_copies[:2] + theta_copies[2:]:
        copy.start()

    message, answers, steps, inverse = slab_system(tens[...], mass)
    KB[pl.ds(k, 1), 0, :] = message
    advance = iter(range(len(rounds)))

    def next_round():
        n = next(advance, None)
        if n is not None:
            finish(n)
            if n + 1 < len(rounds):
                begin(n + 1)

    for _ in range(len(rounds) - 2):
        next_round()

    def everyone(buffer, sent, arrived):
        far = [(dy, dz) for dy in range(ny) for dz in range(nz) if (dy, dz) != (0, 0)]
        far.sort(key=lambda d: -(min(d[0], ny - d[0]) + min(d[1], nz - d[1])))
        for dy, dz in far:
            remote(buffer.at[k], buffer.at[k], sent, arrived, torus(dy, dz), s).start()

    def ghosts(boxes, high, low, depth, store):
        here = lane_iota(depth)
        evens = here % 2 == 0
        at_low = here * 0 + low_end == 1
        at_high = here * 0 + high_end == 1
        ahead = lambda x: roll(x, -1)
        behind = lambda x: roll(x, 1)
        centre = jnp.where(
            evens,
            jnp.where(at_low, low, ahead(boxes[0])),
            jnp.where(at_high, high, behind(boxes[1])),
        )
        outer = jnp.where(
            evens, jnp.where(at_low, low, boxes[0]), jnp.where(at_high, high, boxes[1])
        )
        inner = jnp.where(
            evens, jnp.where(at_low, ahead(low), low), jnp.where(at_high, behind(high), high)
        )
        down = roll(jnp.where(evens, ahead(boxes[2]), behind(boxes[3])), -2 * cells)
        up = roll(jnp.where(evens, ahead(boxes[4]), behind(boxes[5])), 2 * cells)
        own_down, own_up = jnp.zeros_like(down), jnp.zeros_like(up)
        for c in range(3):
            spot = c * group
            turned = roll(V[c, 1, pl.ds(base, depth), :], spot + 1)
            own_down = jnp.where(here // 2 == spot // 2, turned, own_down)
            spot = c * group + 2 * (cells + 1)
            turned = roll(V[c, cells + 2, pl.ds(base, depth), :], spot + 1)
            own_up = jnp.where(here // 2 == spot // 2, turned, own_up)
        own = own_down + own_up
        own = jnp.where(evens, ahead(own), behind(own))
        mirrored = jnp.where(evens, low_end, high_end) == 1
        cell = lax.rem(here, group) // 2 - 1
        in_fields = here < 3 * group
        centre = jnp.where(
            in_fields & (cell == -1),
            jnp.where(mirrored, own, down),
            jnp.where(in_fields & (cell == cells), jnp.where(mirrored, own, up), centre),
        )
        return centre, outer, inner

    def ghost_rates(centre, outer, inner, depth, top):
        here = lane_iota(depth)
        evens = here % 2 == 0
        which = here // group
        ups = {n: roll(centre, n * group) for n in (-2, -1, 1, 2)}
        of = lambda d: jnp.where(
            which == d,
            centre,
            jnp.where(
                which == (d + 1) % 3,
                ups[1] if d < 2 else ups[-2],
                ups[2] if d == 0 else ups[-1],
            ),
        )
        c0, c1, c2 = of(0), of(1), of(2)
        tu, td = roll(centre, -2), roll(centre, 2)
        sub = row_iota(depth)
        ru, rd = roll(centre, -1, 0), roll(centre, 1, 0)
        rd = jnp.where(sub == 0, -centre, rd)
        if top is not None:
            ru = jnp.where(sub == depth - 1, top, ru)
        su, sd = jnp.where(evens, inner, outer), jnp.where(evens, outer, inner)
        return combine(centre, c0, c1, c2, tu, td, ru, rd, su, sd)

    def combine(centre, c0, c1, c2, tu, td, ru, rd, su, sd):
        laplace = (tu + td) + (ru + rd) + (su + sd) - 6.0 * centre
        advect = c0 * (tu - td) + c1 * (ru - rd) + c2 * (su - sd)
        return NU_DT * laplace - (0.5 * ADV_DT) * advect

    def beside(centre, edge, at):
        left_end, right_end = lane_iota(8) == 0, lane_iota(8) == LANES - 1
        turned = roll(edge, lax.rem(2 * LANES - 1 - at, LANES))
        up = roll(jnp.where(left_end, turned, centre), -1)
        down = roll(jnp.where(right_end, turned, centre), 1)
        return up, down

    for copy in near_copies + theta_copies[:2]:
        copy.wait_recv()
    centre, outer, inner = ghosts([near[n] for n in range(6)], high8, low8, 8, None)
    edge1 = centre
    edge2 = centre + ghost_rates(centre, outer, inner, 8, None)

    def wall_rates(field, lift, i, edge, fields):
        here = [field(c, i) for c in range(3)]
        rates = []
        for c in range(fields):
            centre = here[c]
            su, sd = beside(centre, edge, c * group + 2 * (i + 1))
            ru = roll(centre, -1, 0)
            rd = jnp.where(row8 == 0, -centre, roll(centre, 1, 0))
            rates.append(
                combine(
                    centre, here[0], here[1], here[2], field(c, i + 1), field(c, i - 1), ru, rd, su, sd
                )
            )
        return here, rates

    @pl.loop(0, (cells + 2) // 6)
    def _(block):
        for n in range(6):
            n = block * 6 + n
            here, rates = wall_rates(
                lambda c, i: V[c, i + 2, pl.ds(base, 8), :], None, n - 1, edge1, 3
            )
            for c in range(3):
                W[c, n] = here[c] + rates[c]

    def wall_block(block, sums):
        for n in range(8):
            sums = wall_sum(block * 8 + n, sums)
        return sums

    def wall_sum(i, sums):
        x, y = sums
        here, rates = wall_rates(lambda c, i: W[c, i + 1], None, i, edge2, 2)
        fresh = [
            0.5 * (V[c, i + 2, pl.ds(base, 8), :] + here[c] + rates[c]) for c in range(2)
        ]
        wc, ws = coef[0, pl.ds(i + 1, 1), :], coef[1, pl.ds(i + 1, 1), :]
        return (
            x + 2.0 * WALL_NU * (fresh[1] * wc - fresh[0] * ws),
            y + 2.0 * WALL_NU * (fresh[1] * ws + fresh[0] * wc),
        )

    zero8 = jnp.zeros((8, LANES), jnp.float32)
    fx, fy = lax.fori_loop(0, cells // 8, wall_block, (zero8, zero8))
    FB[s] = jnp.concatenate([fx[0:1], fy[0:1]], axis=0)

    @pl.loop(1, ring)
    def _(d):
        remote(FB.at[s], FB.at[s], send_sem.at[17], force_sem, k, lax.rem(s + d, ring)).start()

    next_round()

    for copy in full_copies + theta_copies[2:]:
        copy.wait_recv()
    centre, outer, inner = ghosts([full[n] for n in range(6)], TR[...], TL[...], rows, None)
    swap = lambda x: jnp.where(lane_iota(rows) % 2 == 0, roll(x, -1), roll(x, 1))
    PG[...] = swap(centre)
    cur_lo = jnp.sum(
        jnp.where(lane == 3 * group, centre[0:1], 0.0), axis=1, keepdims=True
    )
    cur_hi = jnp.sum(
        jnp.where(lane == 3 * group + 1, centre[0:1], 0.0), axis=1, keepdims=True
    )
    cur_side = jnp.where(lane % 2 == 0, cur_lo, cur_hi)
    top = jnp.where(
        lane // group == 0,
        -cur_side * lane_sin,
        jnp.where(lane // group == 1, cur_side * lane_cos, 0.0),
    )
    UG[...] = swap(centre + ghost_rates(centre, outer, inner, rows, top))

    def outer_rows(i):
        return coef[2, pl.ds(i + 1, 1), :], coef[3, pl.ds(i + 1, 1), :], jnp.zeros((1, LANES), jnp.float32)

    @pl.loop(0, cells + 2)
    def _(n):
        for c, value in enumerate(outer_rows(n - 1)):
            V[c, n + 1, pl.ds(base + rows, 1), :] = value
            V[c, n + 1, pl.ds(base - 1, 1), :] = -V[c, n + 1, pl.ds(base, 1), :]

    first_lane, last_lane = lane_iota(8) == 0, lane_iota(8) == LANES - 1

    def advanced(field, edge, i, scale, store):
        here = [[field(c, i, base + 8 * t) for t in range(tiles)] for c in range(3)]
        column = jnp.concatenate([tile for own in here for tile in own], axis=0)
        moved = jnp.dot(
            column.astype(jnp.bfloat16), shifts[...], preferred_element_type=jnp.float32
        )
        for t in range(tiles):
            start = base + 8 * t
            weights = []
            for d in range(3):
                half = (0.5 * ADV_DT * scale) * here[d][t]
                weights.append((NU_DT * scale - half, NU_DT * scale + half))
            for c in range(3):
                line = (c * tiles + t) * 8
                at = c * group + 2 * (i + 1)
                ghost = roll(edge[pl.ds(8 * t, 8), :], lax.rem(2 * LANES - 1 - at, LANES))
                su = jnp.where(last_lane, ghost, moved[line : line + 8, :LANES])
                sd = jnp.where(first_lane, ghost, moved[line : line + 8, LANES:])
                total = weights[2][0] * su + weights[2][1] * sd
                total += weights[0][0] * field(c, i + 1, start)
                total += weights[0][1] * field(c, i - 1, start)
                total += weights[1][0] * field(c, i, start + 1)
                total += weights[1][1] * field(c, i, start - 1)
                store(c, t, total + (scale * (1.0 - 6.0 * NU_DT)) * here[c][t])

    def first_stage(pair):
        for n in (2 * pair, 2 * pair + 1):

            def store(c, t, fresh, n=n):
                U[c, n, pl.ds(base + 8 * t, 8), :] = fresh
                if t == 0:
                    U[c, n, pl.ds(base - 1, 1), :] = -fresh[0:1]

            advanced(
                lambda c, i, start: V[c, i + 2, pl.ds(start, 8), :], PG, n - 1, 1.0, store
            )
            for c, value in enumerate(outer_rows(n - 1)):
                U[c, n, pl.ds(base + rows, 1), :] = value

    pl.loop(0, CUTS[0])(first_stage)
    next_round()
    everyone(KB, send_sem.at[16], stiff_sem)
    pl.loop(CUTS[0], CUTS[1])(first_stage)

    arrivals = ring - 1
    pltpu.make_async_copy(
        FB.at[pl.ds(0, arrivals)], FB.at[pl.ds(0, arrivals)], force_sem
    ).wait()
    force = FB[0]
    for n in range(1, ring):
        force = force + FB[n]
    force_out[...] = force
    load = force * LANES ** (-1.5) + mass * (disp[...] + rate[...])
    load8 = wide_loads(load)
    RB[pl.ds(k, 1), 0, :] = end_loads(answers, load8)

    everyone(RB, send_sem.at[18], load_sem)

    pl.loop(CUTS[1], cells // 2 + 1)(first_stage)

    @pl.loop(0, cells // 2)
    def _(pair):
        for i in (2 * pair, 2 * pair + 1):

            def store(c, t, value, i=i):
                out[c, i, pl.ds(8 * t, 8), :] = (
                    0.5 * V[c, i + 2, pl.ds(base + 8 * t, 8), :] + value
                )

            advanced(lambda c, i, start: U[c, i + 1, pl.ds(start, 8), :], UG, i, 0.5, store)

    others = count - 1
    pltpu.make_async_copy(KB.at[pl.ds(0, others)], KB.at[pl.ds(0, others)], stiff_sem).wait()
    spare = jnp.zeros((LANES - count, LANES), jnp.float32)
    numbers = jnp.concatenate([KB[:, 0, :], spare], axis=0).T
    blocks = chain_response(numbers, count, k, mass)
    blocks.append(jnp.zeros((LANES - 32, LANES), jnp.float32))
    response = jnp.concatenate(blocks, axis=0).T[0:count]
    rest = inner_deflection(steps, inverse, load8)

    pltpu.make_async_copy(RB.at[pl.ds(0, others)], RB.at[pl.ds(0, others)], load_sem).wait()
    ends = ends_solved(response, RB[:, 0, :])
    moved = ends * answers
    for direction in range(2):
        mine = jnp.sum(jnp.where(row8 % 2 == direction, moved, 0.0), axis=0, keepdims=True)
        defl_out[pl.ds(direction, 1), :] = rest[direction : direction + 1] + mine

    for copy in near_copies + full_copies + theta_copies:
        copy.wait_send()
    for sent, size, buffer in ((16, others, KB), (17, arrivals, FB), (18, others, RB)):
        pltpu.make_async_copy(
            buffer.at[pl.ds(0, size)], buffer.at[pl.ds(0, size)], send_sem.at[sent]
        ).wait()


def hand_over(fresh, force, defl, fresh_out, force_out, defl_out, sem):
    copies = [
        pltpu.make_async_copy(src, dst, sem.at[n])
        for n, (src, dst) in enumerate(
            ((fresh, fresh_out), (force, force_out), (defl, defl_out))
        )
    ]
    for copy in copies:
        copy.start()
    for copy in copies:
        copy.wait()


def solution(mesh):
    count, ring = mesh.shape["span"], mesh.shape["sector"]

    def local(velocity, speed, cbin, face, weight, tension, displacement, beam_rate):
        cells, rows, sections = velocity.shape[1:]
        far = pl.BlockSpec(memory_space=pltpu.HBM)
        vmem = pl.BlockSpec(memory_space=pltpu.VMEM)
        tall = rows + 16
        f32 = jnp.float32
        shapes = (
            jax.ShapeDtypeStruct(velocity.shape, f32),
            jax.ShapeDtypeStruct((2, sections), f32),
            jax.ShapeDtypeStruct((2, sections), f32),
        )
        results = pl.pallas_call(
            lambda *refs: kernel(count, ring, *refs),
            out_shape=shapes,
            in_specs=[far] * 8,
            out_specs=(vmem,) * 3,
            scratch_shapes=[
                pltpu.VMEM((3, cells + 4, tall, LANES), f32),
                pltpu.VMEM((3, cells + 2, tall, LANES), f32),
                pltpu.VMEM((3, cells + 2, 8, LANES), f32),
                pltpu.VMEM((rows, LANES), f32),
                pltpu.VMEM((rows, LANES), f32),
                pltpu.VMEM((8, LANES), f32),
                pltpu.VMEM((8, LANES), f32),
                pltpu.VMEM((6, 8, LANES), f32),
                pltpu.VMEM((6, rows, LANES), f32),
                pltpu.VMEM((rows, LANES), f32),
                pltpu.VMEM((rows, LANES), f32),
                pltpu.VMEM((ring, 2, LANES), f32),
                pltpu.VMEM((count, 1, LANES), f32),
                pltpu.VMEM((count, 1, LANES), f32),
                pltpu.VMEM((4, 24, LANES), f32),
                pltpu.SMEM(speed.shape, f32),
                pltpu.VMEM((1, sections), jnp.int32),
                pltpu.SMEM(face.shape, jnp.int32),
                pltpu.SMEM(weight.shape, f32),
                pltpu.VMEM((1, sections), f32),
                pltpu.VMEM((2, sections), f32),
                pltpu.VMEM((2, sections), f32),
                pltpu.SemaphoreType.DMA((2,)),
                pltpu.SemaphoreType.DMA((7,)),
                pltpu.SemaphoreType.DMA((19,)),
                pltpu.SemaphoreType.DMA((4,)),
                pltpu.SemaphoreType.DMA((6,)),
                pltpu.SemaphoreType.DMA((6,)),
                pltpu.SemaphoreType.DMA,
                pltpu.SemaphoreType.DMA,
                pltpu.SemaphoreType.DMA,
                pltpu.SemaphoreType.REGULAR((6,)),
                pltpu.VMEM((LANES, 2 * LANES), jnp.bfloat16),
            ],
            compiler_params=pltpu.CompilerParams(
                collective_id=0, has_side_effects=True, vmem_limit_bytes=24 << 20
            ),
            name="riser",
        )(
            *[pltpu.with_memory_space_constraint(x, pltpu.HBM) for x in (velocity,
            speed,
            cbin.reshape(1, sections),
            face,
            weight,
            tension.reshape(1, sections),
            displacement,
            beam_rate)],
        )
        return pl.pallas_call(
            hand_over,
            out_shape=shapes,
            in_specs=[vmem] * 3,
            out_specs=(far,) * 3,
            scratch_shapes=[pltpu.SemaphoreType.DMA((3,))],
            name="results",
        )(*[pltpu.with_memory_space_constraint(x, pltpu.VMEM) for x in results])

    return jax.shard_map(
        local,
        mesh=mesh,
        in_specs=(
            P(None, "sector", None, "span"),
            P(),
            P("span"),
            P("sector"),
            P("sector"),
            P("span"),
            P(None, "span"),
            P(None, "span"),
        ),
        out_specs=(P(None, "sector", None, "span"), P(None, "span"), P(None, "span")),
        check_vma=False,
    )
```

```python
import math

import jax
import jax.numpy as jnp
from jax import lax
from jax.experimental import pallas as pl
from jax.experimental.pallas import tpu as pltpu
from jax.sharding import PartitionSpec as P

MESH = pl.DeviceIdType.MESH
NU_DT = 0.15
ADV_DT = 0.1
WALL_NU = 0.5
BEAM_EI = 0.5
BEAM_MASS = 0.4
LANES = 128
CUTS = (6, 9)


def roll(x, shift, axis=1):
    size = x.shape[axis]
    return pltpu.roll(x, shift % size if isinstance(shift, int) else shift, axis)


def lane_iota(rows):
    return lax.broadcasted_iota(jnp.int32, (rows, LANES), 1)


def row_iota(rows):
    return lax.broadcasted_iota(jnp.int32, (rows, LANES), 0)


def reduce_chain(A, D, F, rho_of, strides):
    A00, A01, A10, A11 = A
    D00, D01, D11 = D
    Fw, Fs = F
    steps = []
    for s in strides:
        inv = 1.0 / (D00 * D11 - D01 * D01)
        I00, I01, I11 = D11 * inv, -D01 * inv, D00 * inv
        P00 = I00 * A00 + I01 * A10
        P01 = I00 * A01 + I01 * A11
        P10 = I01 * A00 + I11 * A10
        P11 = I01 * A01 + I11 * A11
        E11 = A01 * P01 + A11 * P11
        I00m, I01m, I11m = roll(I00, s), roll(I01, s), roll(I11, s)
        al00 = A00 * I00m + A01 * I01m
        al01 = A00 * I01m + A01 * I11m
        al10 = A10 * I00m + A11 * I01m
        al11 = A10 * I01m + A11 * I11m
        ga00, ga01, ga10, ga11 = roll(P00, -s), roll(P10, -s), roll(P01, -s), roll(P11, -s)
        steps.append((al00, al01, al10, al11, ga00, ga01, ga10, ga11))
        P00m, P01m, P10m, P11m = roll(P00, s), roll(P01, s), roll(P10, s), roll(P11, s)
        D11 = D11 - (al10 * A10 + al11 * A11) - roll(E11, -s)
        Fw, Fs = reduce_load(steps[-1], Fw, Fs, s)
        A00, A01, A10, A11 = (
            -(A00 * P00m + A01 * P10m),
            -(A00 * P01m + A01 * P11m),
            -(A10 * P00m + A11 * P10m),
            -(A10 * P01m + A11 * P11m),
        )
        rw, rs = rho_of(Fw, Fs)
        D00 = rw - A00 - roll(A00, -2 * s)
        D01 = rs - A10 - roll(A01, -2 * s)
    inv = 1.0 / (D00 * D11 - D01 * D01)
    last = (D11 * inv, -D01 * inv, D00 * inv)
    return last[0] * Fw + last[1] * Fs, last[1] * Fw + last[2] * Fs, steps, last


def reduce_load(step, Fw, Fs, s):
    al00, al01, al10, al11, ga00, ga01, ga10, ga11 = step
    Fwm, Fsm, Fwp, Fsp = roll(Fw, s), roll(Fs, s), roll(Fw, -s), roll(Fs, -s)
    return (
        Fw - (al00 * Fwm + al01 * Fsm) - (ga00 * Fwp + ga01 * Fsp),
        Fs - (al10 * Fwm + al11 * Fsm) - (ga10 * Fwp + ga11 * Fsp),
    )


def slab_system(t, mass):
    lane = lane_iota(1)
    g = t / 30.0
    gn = roll(g, -1)
    a00, a01, a10, a11 = (
        -12.0 * BEAM_EI - 36.0 * g,
        -6.0 * BEAM_EI - 3.0 * g,
        6.0 * BEAM_EI + 3.0 * g,
        2.0 * BEAM_EI - g,
    )
    n00, n01, n10, n11 = roll(a00, -1), roll(a01, -1), roll(a10, -1), roll(a11, -1)
    d00 = (12.0 * BEAM_EI + 36.0 * g) + (12.0 * BEAM_EI + 36.0 * gn) + mass
    d01 = (-6.0 * BEAM_EI - 3.0 * g) + (6.0 * BEAM_EI + 3.0 * gn)
    d11 = (4.0 * BEAM_EI + 4.0 * g) + (4.0 * BEAM_EI + 4.0 * gn)
    inside = lane < LANES - 1
    rho_w = jnp.where(inside, (d00 - jnp.maximum(-a00, -n00)) - jnp.minimum(-a00, -n00), 0.0)
    rho_s = jnp.where(inside, (d01 + a10) + n01, 0.0)
    first, last, end = lane == 0, lane == LANES - 2, lane == LANES - 1
    zero = jnp.zeros_like(t)
    row = row_iota(8)

    def stack(rows):
        out = jnp.zeros((8, LANES), jnp.float32)
        for index, value in enumerate(rows):
            out = jnp.where(row == index, value, out)
        return out

    Fw = stack(
        [
            rho_w,
            jnp.where(first, -a00, zero),
            jnp.where(first, -a01, zero),
            jnp.where(last, -n00, jnp.where(end, 1.0, zero)),
            jnp.where(last, -n10, zero),
        ]
    )
    Fs = stack(
        [
            rho_s,
            jnp.where(first, -a10, zero),
            jnp.where(first, -a11, zero),
            jnp.where(last, -n01, zero),
            jnp.where(last, -n11, jnp.where(end, 1.0, zero)),
        ]
    )
    coupled = jnp.logical_and(lane > 0, inside)
    A = tuple(jnp.where(coupled, x, 0.0) for x in (a00, a01, a10, a11))
    D = (jnp.where(inside, d00, 1.0), jnp.where(inside, d01, 0.0), jnp.where(inside, d11, 1.0))

    def rho_of(Fw, Fs):
        return Fw[0:1] + Fw[1:2] + Fw[3:4], Fs[0:1] + Fs[1:2] + Fs[3:4]

    Zw, Zs, steps, inverse = reduce_chain(A, D, (Fw, Fs), rho_of, [1 << b for b in range(7)])
    yw, ys = Zw[0:1], Zs[0:1]
    xa1w, xa1s = Zw[2:3], Zs[2:3]
    xb0w, xb0s, xb1w, xb1s = Zw[3:4], Zs[3:4], Zw[4:5], Zs[4:5]
    numbers = [
        (0, xb0w * a00 + xb0s * a10),
        (0, xb0w * a01 + xb0s * a11),
        (0, xb1w * a00 + xb1s * a10),
        (0, xb1w * a01 + xb1s * a11),
        (0, -(a00 * yw + a10 * ys)),
        (0, -(a01 * yw + a11 * ys)),
        (0, (4.0 * BEAM_EI + 4.0 * g) + (a01 * xa1w + a11 * xa1s)),
        (LANES - 2, -(n00 * yw + n01 * ys)),
        (LANES - 2, -(n10 * yw + n11 * ys)),
        (LANES - 2, (4.0 * BEAM_EI + 4.0 * gn) + (n10 * xb1w + n11 * xb1s)),
    ]
    row16 = row_iota(16)
    table = jnp.zeros((16, LANES), jnp.float32)
    for index, (spot, value) in enumerate(numbers):
        table = jnp.where((row16 == index) & (lane == spot), value, table)
    column = jnp.sum(table, axis=1, keepdims=True)
    message = jnp.sum(jnp.where(lane_iota(16) == row16, column, 0.0), axis=0, keepdims=True)
    answers = jnp.zeros((8, LANES), jnp.float32)
    for u in range(4):
        answers = jnp.where(row // 2 == u, Zw[u + 1 : u + 2], answers)
    return message, answers, steps, inverse


def chain_response(numbers, count, place, mass):
    lane = lane_iota(1)
    valid = lane < count
    row = row_iota(8)
    pick = lambda n: jnp.where(valid, numbers[n : n + 1], 0.0)
    a00, a01, a10, a11 = pick(0), pick(1), pick(2), pick(3)
    raw, ras, ka11, rbw, rbs, kb11 = [pick(n) for n in range(4, 10)]
    above = lambda x: jnp.where(lane < count - 1, roll(x, -1), 0.0)
    first = lane == 0
    rw = rbw + above(raw) + mass - jnp.where(first, a00, 0.0)
    rs = rbs + above(ras) - jnp.where(first, a10, 0.0)
    rw = jnp.where(valid, rw, 1.0)
    rs = jnp.where(valid, rs, 0.0)
    d11 = jnp.where(valid, kb11 + above(ka11), 1.0)
    A = tuple(jnp.where(first, 0.0, x) for x in (a00, a01, a10, a11))
    d00 = rw - A[0] - roll(A[0], -1)
    d01 = rs - A[2] - roll(A[1], -1)
    lane8 = lane_iota(8)
    mine = lane8 == place
    before = lane8 == place - 1
    Fw = jnp.where((before & (row == 0)) | (mine & (row == 2)), 1.0, 0.0)
    Fs = jnp.where((before & (row == 1)) | (mine & (row == 3)), 1.0, 0.0)
    Fw = jnp.where(row == 4, rw, Fw)
    Fs = jnp.where(row == 4, rs, Fs)
    strides = []
    while (1 << len(strides)) < count:
        strides.append(1 << len(strides))
    Gw, Gs, _, _ = reduce_chain(
        A, (d00, d01, d11), (Fw, Fs), lambda w, s: (w[4:5], s[4:5]), strides
    )
    Hw, Hs = roll(Gw, 1), roll(Gs, 1)
    blocks = []
    for u in range(4):
        block = jnp.where(row // 2 == 0, Hw[u : u + 1], 0.0)
        block = jnp.where(row // 2 == 1, Hs[u : u + 1], block)
        block = jnp.where(row // 2 == 2, Gw[u : u + 1], block)
        blocks.append(jnp.where(row // 2 == 3, Gs[u : u + 1], block))
    return blocks


def wide_loads(load):
    row = row_iota(8)
    return jnp.where(row % 2 == 0, load[0:1], load[1:2])


def end_loads(answers, load8):
    total = jnp.sum(answers * load8, axis=1, keepdims=True)
    lane = lane_iota(8)
    keep = (lane % 8 == row_iota(8)) & (lane < 32)
    return jnp.sum(jnp.where(keep, total, 0.0), axis=0, keepdims=True)


def ends_solved(response, loads):
    total = jnp.sum(response * loads, axis=0, keepdims=True)
    lane, row = lane_iota(8), row_iota(8)
    keep = (lane // 8 == row // 2) & (lane % 2 == row % 2) & (lane < 32)
    return jnp.sum(jnp.where(keep, total, 0.0), axis=1, keepdims=True)


def inner_deflection(steps, inverse, load8):
    inside = lane_iota(8) < LANES - 1
    Fw, Fs = jnp.where(inside, load8, 0.0), jnp.zeros((8, LANES), jnp.float32)
    for b in range(7):
        Fw, Fs = reduce_load(steps[b], Fw, Fs, 1 << b)
    return inverse[0] * Fw + inverse[1] * Fs


def kernel(
    count,
    ring,
    vel_hbm,
    speed_hbm,
    cbin_hbm,
    face_hbm,
    weight_hbm,
    tens_hbm,
    disp_hbm,
    rate_hbm,
    out,
    force_out,
    defl_out,
    V,
    U,
    W,
    TR,
    TL,
    TRw,
    TLw,
    near,
    full,
    PG,
    UG,
    FB,
    KB,
    RB,
    coef,
    speed,
    cbin,
    face,
    weight,
    tens,
    disp,
    rate,
    own_sem,
    small_sem,
    send_sem,
    theta_sem,
    near_sem,
    full_sem,
    force_sem,
    stiff_sem,
    load_sem,
    round_sem,
    T,
    wall_next,
    shifts,
    shift_a,
    shift_b,
):
    vel = vel_hbm
    cells, rows = vel.shape[1], vel.shape[2]
    tiles = rows // 8
    base = 8
    k = lax.axis_index("span")
    s = lax.axis_index("sector")
    left, right = lax.rem(k + count - 1, count), lax.rem(k + 1, count)
    turn = lambda d: lax.rem(s + d + ring, ring)
    lower, upper = turn(-1), turn(1)
    ny = 4 if count >= 32 else 2
    nz = count // ny
    y, z = k // nz, lax.rem(k, nz)

    def torus(dy, dz):
        return lax.rem(y + dy + ny, ny) * nz + lax.rem(z + dz + nz, nz)

    low_end = jnp.where(k == 0, 1, 0)
    high_end = jnp.where(k == count - 1, 1, 0)
    mass = BEAM_MASS / LANES**2
    stride = cells + 2
    group = 2 * stride

    barrier = pltpu.get_barrier_semaphore()

    def signal(semaphore, span, sector):
        pl.semaphore_signal(
            semaphore, inc=1, device_id={"span": span, "sector": sector}, device_id_type=MESH
        )

    close = [(side, way) for side in (left, right) for way in (lower, upper)]
    close += [(left, s), (right, s)] + [(k, turn(d)) for d in range(1, ring)]
    close += [(torus(1, 0), s), (torus(-1, 0), s), (torus(0, 1), s), (torus(0, -1), s)]
    own_wall = pltpu.make_async_copy(
        vel.at[:, :, pl.ds(0, 8), :],
        V.at[:, pl.ds(2, cells), pl.ds(base, 8), :],
        own_sem.at[0],
    )
    own_bulk = pltpu.make_async_copy(
        vel.at[:, :, pl.ds(8, rows - 8), :],
        V.at[:, pl.ds(2, cells), pl.ds(base + 8, rows - 8), :],
        own_sem.at[1],
    )
    small = [
        pltpu.make_async_copy(src, dst, small_sem.at[n])
        for n, (src, dst) in enumerate(
            (
                (speed_hbm, speed),
                (cbin_hbm, cbin),
                (face_hbm, face),
                (weight_hbm, weight),
                (tens_hbm, tens),
                (disp_hbm, disp),
                (rate_hbm, rate),
            )
        )
    ]
    own_wall.start()
    for copy in small:
        copy.start()
    own_bulk.start()


    for span, sector in close:
        signal(barrier, span, sector)

    rounds = []
    known = 1
    while known < nz // 2:
        rounds.append([(torus(0, known), s), (torus(0, -known), s)])
        known *= 2
    rounds += [[(torus(1, 0), s), (torus(-1, 0), s)]] * 2

    def begin(n):
        for span, sector in rounds[n]:
            signal(round_sem.at[n], span, sector)

    def finish(n):
        pl.semaphore_wait(round_sem.at[n], len(rounds[n]))

    lane = lane_iota(1)
    row8 = row_iota(8)
    total_cells = cells * ring

    def angle_of(index):
        whole = lax.rem(s * cells + index + total_cells, total_cells)
        return 2.0 * math.pi * (whole.astype(jnp.float32) + 0.5) / total_cells

    ring_angle = angle_of(row_iota(24) - 1)
    ring_sin, ring_cos = jnp.sin(ring_angle), jnp.cos(ring_angle)
    lane_cell = lax.rem(lane, group) // 2 - 1
    lane_angle = angle_of(lane_cell)
    lane_sin, lane_cos = jnp.sin(lane_angle), jnp.cos(lane_angle)

    from_lane = lax.broadcasted_iota(jnp.int32, (LANES, 2 * LANES), 0)
    to_lane = lax.broadcasted_iota(jnp.int32, (LANES, 2 * LANES), 1)
    source = jnp.where(to_lane < LANES, to_lane + 1, to_lane - LANES - 1)
    source = jnp.where(to_lane == LANES - 1, -1, source)
    shifts[...] = jnp.where(from_lane == source, 1.0, 0.0).astype(jnp.bfloat16)

    own_wall.wait()
    TRw[...] = jnp.zeros((24, LANES), jnp.float32)
    TLw[...] = jnp.zeros((24, LANES), jnp.float32)
    lanes = lane_iota(cells)
    high = jnp.zeros((cells, LANES), jnp.float32)
    low = high
    for c in range(3):
        for j in range(3):
            own = V[c, pl.ds(2, cells), base + j, :]
            T[c, j, pl.ds(2, cells), :] = own
            spot = c * 3 + j
            turned = roll(own, 2 * spot + 2)
            high = jnp.where(lanes // 2 == spot, turned, high)
            low = jnp.where(lanes // 2 == spot + 1, turned, low)
    TRw[pl.ds(1, cells), :] = high
    TLw[pl.ds(1, cells), :] = roll(low, -2)

    def remote(src, dst, sent, arrived, span, sector):
        return pltpu.make_async_remote_copy(
            src_ref=src,
            dst_ref=dst,
            send_sem=sent,
            recv_sem=arrived,
            device_id={"span": span, "sector": sector},
            device_id_type=MESH,
        )

    spread = [
        (0, 0, right, s),
        (1, 1, left, s),
        (0, 2, right, upper),
        (1, 3, left, upper),
        (0, 4, right, lower),
        (1, 5, left, lower),
    ]
    near_copies = [
        remote(
            (TRw, TLw)[which], near.at[slot], send_sem.at[slot], near_sem.at[slot], span, sector
        )
        for which, slot, span, sector in spread
    ]
    full_copies = [
        remote(
            (TR, TL)[which], full.at[slot], send_sem.at[6 + slot], full_sem.at[slot], span, sector
        )
        for which, slot, span, sector in spread
    ]
    theta_copies = []
    for part, (start, size) in enumerate(((0, 8), (8, rows - 8))):
        theta_copies.append(
            remote(
                vel.at[:, pl.ds(0, 2), pl.ds(start, size), :],
                V.at[:, pl.ds(cells + 2, 2), pl.ds(base + start, size), :],
                send_sem.at[12 + 2 * part],
                theta_sem.at[2 * part],
                k,
                lower,
            )
        )
        theta_copies.append(
            remote(
                vel.at[:, pl.ds(cells - 2, 2), pl.ds(start, size), :],
                V.at[:, pl.ds(0, 2), pl.ds(base + start, size), :],
                send_sem.at[13 + 2 * part],
                theta_sem.at[1 + 2 * part],
                k,
                upper,
            )
        )

    for copy in small:
        copy.wait()
    current = jnp.zeros((1, LANES), jnp.float32)
    for b in range(speed.shape[0]):
        current = current + jnp.where(cbin[...] == b, speed[b], 0.0)
    face_row = row_iota(24) - 1
    face_weight = jnp.zeros((24, LANES), jnp.float32)
    for q in range(weight.shape[0]):
        face_weight = face_weight + jnp.where(face_row == face[q], weight[q], 0.0)
    coef[0] = face_weight * ring_cos
    coef[1] = face_weight * ring_sin
    coef[2] = -current * ring_sin
    coef[3] = current * ring_cos
    cur_high = jnp.sum(jnp.where(lane == LANES - 1, current, 0.0), axis=1, keepdims=True)
    cur_low = jnp.sum(jnp.where(lane == 0, current, 0.0), axis=1, keepdims=True)
    wide = lane_iota(rows)
    TR[...] = jnp.where(wide == 3 * group + 1, cur_high, 0.0)
    TL[...] = jnp.where(wide == 3 * group + 2, cur_low, 0.0)
    own_bulk.wait()

    def outer_rows(i):
        return (
            coef[2, pl.ds(i + 1, 1), :],
            coef[3, pl.ds(i + 1, 1), :],
            jnp.zeros((1, LANES), jnp.float32),
        )

    def ghost_rows(i):
        for c, value in enumerate(outer_rows(i)):
            V[c, i + 2, pl.ds(base + rows, 1), :] = value
            V[c, i + 2, pl.ds(base - 1, 1), :] = -V[c, i + 2, pl.ds(base, 1), :]

    @pl.loop(0, cells)
    def _(i):
        high, low = TR[...], TL[...]
        for c in range(3):
            spot = c * group + 2 * (i + 1)
            turned = roll(V[c, i + 2, pl.ds(base, rows), :], spot + 2)
            high = jnp.where(wide // 2 == spot // 2, turned, high)
            low = jnp.where(wide // 2 == spot // 2 + 1, turned, low)
        TR[...] = high
        TL[...] = low
        ghost_rows(i)

    TL[...] = roll(TL[...], -2)
    pl.semaphore_wait(barrier, len(close))
    for copy in near_copies[2:] + near_copies[:2] + theta_copies[:2]:
        copy.start()
    begin(0)
    for copy in full_copies[2:] + full_copies[:2] + theta_copies[2:]:
        copy.start()

    message, answers, steps, inverse = slab_system(tens[...], mass)
    KB[pl.ds(k, 1), 0, :] = message
    advance = iter(range(len(rounds)))

    def next_round():
        n = next(advance, None)
        if n is not None:
            finish(n)
            if n + 1 < len(rounds):
                begin(n + 1)

    for _ in range(len(rounds) - 2):
        next_round()

    def everyone(buffer, sent, arrived):
        far = [(dy, dz) for dy in range(ny) for dz in range(nz) if (dy, dz) != (0, 0)]
        far.sort(key=lambda d: -(min(d[0], ny - d[0]) + min(d[1], nz - d[1])))
        for dy, dz in far:
            remote(buffer.at[k], buffer.at[k], sent, arrived, torus(dy, dz), s).start()

    def ghosts(boxes, high, low, depth):
        here = lane_iota(depth)
        evens = here % 2 == 0
        at_low = here * 0 + low_end == 1
        at_high = here * 0 + high_end == 1
        ahead = lambda x: roll(x, -1)
        behind = lambda x: roll(x, 1)
        centre = jnp.where(
            evens,
            jnp.where(at_low, low, ahead(boxes[0])),
            jnp.where(at_high, high, behind(boxes[1])),
        )
        outer = jnp.where(
            evens, jnp.where(at_low, low, boxes[0]), jnp.where(at_high, high, boxes[1])
        )
        inner = jnp.where(
            evens, jnp.where(at_low, ahead(low), low), jnp.where(at_high, behind(high), high)
        )
        return centre, outer, inner

    def with_corners(centre, boxes, depth):
        here = lane_iota(depth)
        evens = here % 2 == 0
        ahead = lambda x: roll(x, -1)
        behind = lambda x: roll(x, 1)
        down = roll(jnp.where(evens, ahead(boxes[2]), behind(boxes[3])), -2 * cells)
        up = roll(jnp.where(evens, ahead(boxes[4]), behind(boxes[5])), 2 * cells)
        own_down, own_up = jnp.zeros_like(down), jnp.zeros_like(up)
        for c in range(3):
            spot = c * group
            turned = roll(V[c, 1, pl.ds(base, depth), :], spot + 1)
            own_down = jnp.where(here // 2 == spot // 2, turned, own_down)
            spot = c * group + 2 * (cells + 1)
            turned = roll(V[c, cells + 2, pl.ds(base, depth), :], spot + 1)
            own_up = jnp.where(here // 2 == spot // 2, turned, own_up)
        own = own_down + own_up
        own = jnp.where(evens, ahead(own), behind(own))
        mirrored = jnp.where(evens, low_end, high_end) == 1
        cell = lax.rem(here, group) // 2 - 1
        in_fields = here < 3 * group
        centre = jnp.where(
            in_fields & (cell == -1),
            jnp.where(mirrored, own, down),
            jnp.where(in_fields & (cell == cells), jnp.where(mirrored, own, up), centre),
        )
        return centre

    def ghost_rates(centre, outer, inner, depth, top):
        here = lane_iota(depth)
        evens = here % 2 == 0
        which = here // group
        ups = {n: roll(centre, n * group) for n in (-2, -1, 1, 2)}
        of = lambda d: jnp.where(
            which == d,
            centre,
            jnp.where(
                which == (d + 1) % 3,
                ups[1] if d < 2 else ups[-2],
                ups[2] if d == 0 else ups[-1],
            ),
        )
        c0, c1, c2 = of(0), of(1), of(2)
        tu, td = roll(centre, -2), roll(centre, 2)
        sub = row_iota(depth)
        ru, rd = roll(centre, -1, 0), roll(centre, 1, 0)
        rd = jnp.where(sub == 0, -centre, rd)
        if top is not None:
            ru = jnp.where(sub == depth - 1, top, ru)
        su, sd = jnp.where(evens, inner, outer), jnp.where(evens, outer, inner)
        return combine(centre, c0, c1, c2, tu, td, ru, rd, su, sd)

    def combine(centre, c0, c1, c2, tu, td, ru, rd, su, sd):
        laplace = (tu + td) + (ru + rd) + (su + sd) - 6.0 * centre
        advect = c0 * (tu - td) + c1 * (ru - rd) + c2 * (su - sd)
        return NU_DT * laplace - (0.5 * ADV_DT) * advect

    for copy in near_copies + theta_copies[:2]:
        copy.wait_recv()
    for c in range(3):
        for j in range(3):
            T[c, j, pl.ds(0, 2), :] = V[c, pl.ds(0, 2), base + j, :]
            T[c, j, pl.ds(cells + 2, 2), :] = V[c, pl.ds(cells + 2, 2), base + j, :]
    wall_edge, outer, inner = ghosts([near[0], near[1]], TRw[...], TLw[...], 24)
    here, sub = lane_iota(24), row_iota(24)
    evens = here % 2 == 0
    own_first, own_last = jnp.zeros((8, LANES), jnp.float32), jnp.zeros((8, LANES), jnp.float32)
    lane8 = lane_iota(8)
    for c in range(3):
        for j in range(3):
            spot = c * 3 + j
            keep = lane8 // 2 == spot
            own_first = jnp.where(keep, roll(T[c, j, pl.ds(1, 8), :], 2 * spot + 1), own_first)
            own_last = jnp.where(keep, roll(T[c, j, pl.ds(17, 8), :], 2 * spot + 1), own_last)
    own = jnp.concatenate([own_first, own_first, own_last], axis=0)
    own = jnp.where(evens, roll(own, -1), roll(own, 1))
    down = roll(jnp.where(evens, roll(near[2], -1), roll(near[3], 1)), 24 - cells, 0)
    up = roll(jnp.where(evens, roll(near[4], -1), roll(near[5], 1)), cells, 0)
    mirrored = jnp.where(evens, low_end, high_end) == 1
    wall_edge = jnp.where(
        sub == 0,
        jnp.where(mirrored, own, down),
        jnp.where(sub == cells + 1, jnp.where(mirrored, own, up), wall_edge),
    )

    def wall_beside(centre, edge, spot, depth):
        turned = roll(edge, -(2 * spot + 1))
        places = lane_iota(depth)
        return (
            roll(jnp.where(places == 0, turned, centre), -1),
            roll(jnp.where(places == LANES - 1, turned, centre), 1),
        )

    which = here // 6
    turns = {n: roll(wall_edge, 6 * n) for n in (-2, -1, 1, 2)}
    parts = [
        jnp.where(which == 0, wall_edge, jnp.where(which == 1, turns[1], turns[2])),
        jnp.where(which == 1, wall_edge, jnp.where(which == 2, turns[1], turns[-1])),
        jnp.where(which == 2, wall_edge, jnp.where(which == 1, turns[-1], turns[-2])),
    ]
    wall_next[...] = wall_edge + combine(
        wall_edge,
        *parts,
        roll(wall_edge, -1, 0),
        roll(wall_edge, 1, 0),
        roll(wall_edge, -2),
        jnp.where(here // 2 % 3 == 0, -wall_edge, roll(wall_edge, 2)),
        jnp.where(evens, inner, outer),
        jnp.where(evens, outer, inner),
    )
    for j in range(2):
        cell = [T[c, j, pl.ds(1, 24), :] for c in range(3)]
        for c in range(3):
            su, sd = wall_beside(cell[c], wall_edge, c * 3 + j, 24)
            W[c, j] = cell[c] + combine(
                cell[c],
                *cell,
                T[c, j, pl.ds(2, 24), :],
                T[c, j, pl.ds(0, 24), :],
                T[c, j + 1, pl.ds(1, 24), :],
                T[c, j - 1, pl.ds(1, 24), :] if j > 0 else -cell[c],
                su,
                sd,
            )
    cell = [W[c, 0, pl.ds(1, cells), :] for c in range(3)]
    fresh = []
    for c in range(2):
        su, sd = wall_beside(cell[c], wall_next[pl.ds(1, cells), :], c * 3, cells)
        rates = combine(
            cell[c],
            *cell,
            W[c, 0, pl.ds(2, cells), :],
            W[c, 0, pl.ds(0, cells), :],
            W[c, 1, pl.ds(1, cells), :],
            -cell[c],
            su,
            sd,
        )
        fresh.append(0.5 * (T[c, 0, pl.ds(2, cells), :] + cell[c] + rates))
    wc, ws = coef[0, pl.ds(1, cells), :], coef[1, pl.ds(1, cells), :]
    fx = jnp.sum(2.0 * WALL_NU * (fresh[1] * wc - fresh[0] * ws), axis=0, keepdims=True)
    fy = jnp.sum(2.0 * WALL_NU * (fresh[1] * ws + fresh[0] * wc), axis=0, keepdims=True)
    FB[s] = jnp.concatenate([fx, fy], axis=0)
    for d in sorted(range(1, ring), key=lambda d: -min(d, ring - d)):
        remote(FB.at[s], FB.at[s], send_sem.at[17], force_sem, k, turn(d)).start()

    next_round()
    for copy in full_copies + theta_copies[2:]:
        copy.wait_recv()
    boxes = [full[n] for n in range(6)]
    centre, outer, inner = ghosts(boxes, TR[...], TL[...], rows)
    centre = with_corners(centre, boxes, rows)
    swap = lambda x: jnp.where(lane_iota(rows) % 2 == 0, roll(x, -1), roll(x, 1))
    PG[...] = swap(centre)
    cur_lo = jnp.sum(
        jnp.where(lane == 3 * group, centre[0:1], 0.0), axis=1, keepdims=True
    )
    cur_hi = jnp.sum(
        jnp.where(lane == 3 * group + 1, centre[0:1], 0.0), axis=1, keepdims=True
    )
    cur_side = jnp.where(lane % 2 == 0, cur_lo, cur_hi)
    top = jnp.where(
        lane // group == 0,
        -cur_side * lane_sin,
        jnp.where(lane // group == 1, cur_side * lane_cos, 0.0),
    )
    UG[...] = swap(centre + ghost_rates(centre, outer, inner, rows, top))

    ghost_rows(-1)
    ghost_rows(cells)
    first_lane, last_lane = lane_iota(8) == 0, lane_iota(8) == LANES - 1

    def shift(field, i, moved):
        column = jnp.concatenate(
            [field(c, i, base + 8 * t) for c in range(3) for t in range(tiles)], axis=0
        )
        moved[...] = jnp.dot(
            column.astype(jnp.bfloat16), shifts[...], preferred_element_type=jnp.float32
        )

    def advanced(field, edge, i, scale, moved, store):
        for t in range(tiles):
            start = base + 8 * t
            here = [field(c, i, start) for c in range(3)]
            weights = []
            for d in range(3):
                half = (0.5 * ADV_DT * scale) * here[d]
                weights.append((NU_DT * scale - half, NU_DT * scale + half))
            for c in range(3):
                line = pl.ds((c * tiles + t) * 8, 8)
                at = c * group + 2 * (i + 1)
                ghost = roll(edge[pl.ds(8 * t, 8), :], lax.rem(2 * LANES - 1 - at, LANES))
                su = jnp.where(last_lane, ghost, moved[line, pl.ds(0, LANES)])
                sd = jnp.where(first_lane, ghost, moved[line, pl.ds(LANES, LANES)])
                total = weights[2][0] * su + weights[2][1] * sd
                total += weights[0][0] * field(c, i + 1, start)
                total += weights[0][1] * field(c, i - 1, start)
                total += weights[1][0] * field(c, i, start + 1)
                total += weights[1][1] * field(c, i, start - 1)
                store(c, t, total + (scale * (1.0 - 6.0 * NU_DT)) * here[c])

    def from_first(c, i, start):
        return V[c, i + 2, pl.ds(start, 8), :]

    def first_stage(pair):
        for n, ready, later in ((2 * pair, shift_a, shift_b), (2 * pair + 1, shift_b, shift_a)):

            def store(c, t, fresh, n=n):
                U[c, n, pl.ds(base + 8 * t, 8), :] = fresh
                if t == 0:
                    U[c, n, pl.ds(base - 1, 1), :] = -fresh[0:1]

            shift(from_first, n, later)
            advanced(from_first, PG, n - 1, 1.0, ready, store)
            for c, value in enumerate(outer_rows(n - 1)):
                U[c, n, pl.ds(base + rows, 1), :] = value

    shift(from_first, -1, shift_a)
    pl.loop(0, CUTS[0])(first_stage)
    next_round()
    everyone(KB, send_sem.at[16], stiff_sem)
    pl.loop(CUTS[0], CUTS[1])(first_stage)

    arrivals = ring - 1
    pltpu.make_async_copy(
        FB.at[pl.ds(0, arrivals)], FB.at[pl.ds(0, arrivals)], force_sem
    ).wait()
    force = FB[0]
    for n in range(1, ring):
        force = force + FB[n]
    force_out[...] = force
    load = force * LANES ** (-1.5) + mass * (disp[...] + rate[...])
    load8 = wide_loads(load)
    RB[pl.ds(k, 1), 0, :] = end_loads(answers, load8)

    everyone(RB, send_sem.at[18], load_sem)

    pl.loop(CUTS[1], cells // 2 + 1)(first_stage)

    def from_second(c, i, start):
        return U[c, i + 1, pl.ds(start, 8), :]

    shift(from_second, 0, shift_a)

    @pl.loop(0, cells // 2)
    def _(pair):
        for i, ready, later in ((2 * pair, shift_a, shift_b), (2 * pair + 1, shift_b, shift_a)):

            def store(c, t, value, i=i):
                out[c, i, pl.ds(8 * t, 8), :] = (
                    0.5 * V[c, i + 2, pl.ds(base + 8 * t, 8), :] + value
                )

            shift(from_second, i + 1, later)
            advanced(from_second, UG, i, 0.5, ready, store)

    others = count - 1
    pltpu.make_async_copy(KB.at[pl.ds(0, others)], KB.at[pl.ds(0, others)], stiff_sem).wait()
    spare = jnp.zeros((LANES - count, LANES), jnp.float32)
    numbers = jnp.concatenate([KB[:, 0, :], spare], axis=0).T
    blocks = chain_response(numbers, count, k, mass)
    blocks.append(jnp.zeros((LANES - 32, LANES), jnp.float32))
    response = jnp.concatenate(blocks, axis=0).T[0:count]
    rest = inner_deflection(steps, inverse, load8)

    pltpu.make_async_copy(RB.at[pl.ds(0, others)], RB.at[pl.ds(0, others)], load_sem).wait()
    ends = ends_solved(response, RB[:, 0, :])
    moved = ends * answers
    for direction in range(2):
        mine = jnp.sum(jnp.where(row8 % 2 == direction, moved, 0.0), axis=0, keepdims=True)
        defl_out[pl.ds(direction, 1), :] = rest[direction : direction + 1] + mine

    for copy in near_copies + full_copies + theta_copies:
        copy.wait_send()
    for sent, size, buffer in ((16, others, KB), (17, arrivals, FB), (18, others, RB)):
        pltpu.make_async_copy(
            buffer.at[pl.ds(0, size)], buffer.at[pl.ds(0, size)], send_sem.at[sent]
        ).wait()


def hand_over(fresh, force, defl, fresh_out, force_out, defl_out, sem):
    copies = [
        pltpu.make_async_copy(src, dst, sem.at[n])
        for n, (src, dst) in enumerate(
            ((fresh, fresh_out), (force, force_out), (defl, defl_out))
        )
    ]
    for copy in copies:
        copy.start()
    for copy in copies:
        copy.wait()


def solution(mesh):
    count, ring = mesh.shape["span"], mesh.shape["sector"]

    def local(velocity, speed, cbin, face, weight, tension, displacement, beam_rate):
        cells, rows, sections = velocity.shape[1:]
        far = pl.BlockSpec(memory_space=pltpu.HBM)
        vmem = pl.BlockSpec(memory_space=pltpu.VMEM)
        tall = rows + 16
        f32 = jnp.float32
        shapes = (
            jax.ShapeDtypeStruct(velocity.shape, f32),
            jax.ShapeDtypeStruct((2, sections), f32),
            jax.ShapeDtypeStruct((2, sections), f32),
        )
        results = pl.pallas_call(
            lambda *refs: kernel(count, ring, *refs),
            out_shape=shapes,
            in_specs=[far] * 8,
            out_specs=(vmem,) * 3,
            scratch_shapes=[
                pltpu.VMEM((3, cells + 4, tall, LANES), f32),
                pltpu.VMEM((3, cells + 2, tall, LANES), f32),
                pltpu.VMEM((3, 2, 24, LANES), f32),
                pltpu.VMEM((rows, LANES), f32),
                pltpu.VMEM((rows, LANES), f32),
                pltpu.VMEM((24, LANES), f32),
                pltpu.VMEM((24, LANES), f32),
                pltpu.VMEM((6, 24, LANES), f32),
                pltpu.VMEM((6, rows, LANES), f32),
                pltpu.VMEM((rows, LANES), f32),
                pltpu.VMEM((rows, LANES), f32),
                pltpu.VMEM((ring, 2, LANES), f32),
                pltpu.VMEM((count, 1, LANES), f32),
                pltpu.VMEM((count, 1, LANES), f32),
                pltpu.VMEM((4, 24, LANES), f32),
                pltpu.SMEM(speed.shape, f32),
                pltpu.VMEM((1, sections), jnp.int32),
                pltpu.SMEM(face.shape, jnp.int32),
                pltpu.SMEM(weight.shape, f32),
                pltpu.VMEM((1, sections), f32),
                pltpu.VMEM((2, sections), f32),
                pltpu.VMEM((2, sections), f32),
                pltpu.SemaphoreType.DMA((2,)),
                pltpu.SemaphoreType.DMA((7,)),
                pltpu.SemaphoreType.DMA((19,)),
                pltpu.SemaphoreType.DMA((4,)),
                pltpu.SemaphoreType.DMA((6,)),
                pltpu.SemaphoreType.DMA((6,)),
                pltpu.SemaphoreType.DMA,
                pltpu.SemaphoreType.DMA,
                pltpu.SemaphoreType.DMA,
                pltpu.SemaphoreType.REGULAR((6,)),
                pltpu.VMEM((3, 3, 32, LANES), f32),
                pltpu.VMEM((24, LANES), f32),
                pltpu.VMEM((LANES, 2 * LANES), jnp.bfloat16),
                pltpu.VMEM((3 * rows, 2 * LANES), f32),
                pltpu.VMEM((3 * rows, 2 * LANES), f32),
            ],
            compiler_params=pltpu.CompilerParams(
                collective_id=0, has_side_effects=True, vmem_limit_bytes=24 << 20
            ),
            name="riser",
        )(
            *[pltpu.with_memory_space_constraint(x, pltpu.HBM) for x in (velocity,
            speed,
            cbin.reshape(1, sections),
            face,
            weight,
            tension.reshape(1, sections),
            displacement,
            beam_rate)],
        )
        return pl.pallas_call(
            hand_over,
            out_shape=shapes,
            in_specs=[vmem] * 3,
            out_specs=(far,) * 3,
            scratch_shapes=[pltpu.SemaphoreType.DMA((3,))],
            name="results",
        )(*[pltpu.with_memory_space_constraint(x, pltpu.VMEM) for x in results])

    return jax.shard_map(
        local,
        mesh=mesh,
        in_specs=(
            P(None, "sector", None, "span"),
            P(),
            P("span"),
            P("sector"),
            P("sector"),
            P("span"),
            P(None, "span"),
            P(None, "span"),
        ),
        out_specs=(P(None, "sector", None, "span"), P(None, "span"), P(None, "span")),
        check_vma=False,
    )
```

```python
import math

import jax
import jax.numpy as jnp
from jax import lax
from jax.experimental import pallas as pl
from jax.experimental.pallas import tpu as pltpu
from jax.sharding import PartitionSpec as P

MESH = pl.DeviceIdType.MESH
NU_DT = 0.15
ADV_DT = 0.1
WALL_NU = 0.5
BEAM_EI = 0.5
BEAM_MASS = 0.4
LANES = 128
CUTS = (5, 7)


def roll(x, shift, axis=1):
    size = x.shape[axis]
    return pltpu.roll(x, shift % size if isinstance(shift, int) else shift, axis)


def lane_iota(rows):
    return lax.broadcasted_iota(jnp.int32, (rows, LANES), 1)


def row_iota(rows):
    return lax.broadcasted_iota(jnp.int32, (rows, LANES), 0)


def reduce_chain(A, D, F, rho_of, strides):
    A00, A01, A10, A11 = A
    D00, D01, D11 = D
    Fw, Fs = F
    steps = []
    for s in strides:
        inv = 1.0 / (D00 * D11 - D01 * D01)
        I00, I01, I11 = D11 * inv, -D01 * inv, D00 * inv
        P00 = I00 * A00 + I01 * A10
        P01 = I00 * A01 + I01 * A11
        P10 = I01 * A00 + I11 * A10
        P11 = I01 * A01 + I11 * A11
        E11 = A01 * P01 + A11 * P11
        I00m, I01m, I11m = roll(I00, s), roll(I01, s), roll(I11, s)
        al00 = A00 * I00m + A01 * I01m
        al01 = A00 * I01m + A01 * I11m
        al10 = A10 * I00m + A11 * I01m
        al11 = A10 * I01m + A11 * I11m
        ga00, ga01, ga10, ga11 = roll(P00, -s), roll(P10, -s), roll(P01, -s), roll(P11, -s)
        steps.append((al00, al01, al10, al11, ga00, ga01, ga10, ga11))
        P00m, P01m, P10m, P11m = roll(P00, s), roll(P01, s), roll(P10, s), roll(P11, s)
        D11 = D11 - (al10 * A10 + al11 * A11) - roll(E11, -s)
        Fw, Fs = reduce_load(steps[-1], Fw, Fs, s)
        A00, A01, A10, A11 = (
            -(A00 * P00m + A01 * P10m),
            -(A00 * P01m + A01 * P11m),
            -(A10 * P00m + A11 * P10m),
            -(A10 * P01m + A11 * P11m),
        )
        rw, rs = rho_of(Fw, Fs)
        D00 = rw - A00 - roll(A00, -2 * s)
        D01 = rs - A10 - roll(A01, -2 * s)
    inv = 1.0 / (D00 * D11 - D01 * D01)
    last = (D11 * inv, -D01 * inv, D00 * inv)
    return last[0] * Fw + last[1] * Fs, last[1] * Fw + last[2] * Fs, steps, last


def reduce_load(step, Fw, Fs, s):
    al00, al01, al10, al11, ga00, ga01, ga10, ga11 = step
    Fwm, Fsm, Fwp, Fsp = roll(Fw, s), roll(Fs, s), roll(Fw, -s), roll(Fs, -s)
    return (
        Fw - (al00 * Fwm + al01 * Fsm) - (ga00 * Fwp + ga01 * Fsp),
        Fs - (al10 * Fwm + al11 * Fsm) - (ga10 * Fwp + ga11 * Fsp),
    )


def slab_system(t, mass):
    lane = lane_iota(1)
    g = t / 30.0
    gn = roll(g, -1)
    a00, a01, a10, a11 = (
        -12.0 * BEAM_EI - 36.0 * g,
        -6.0 * BEAM_EI - 3.0 * g,
        6.0 * BEAM_EI + 3.0 * g,
        2.0 * BEAM_EI - g,
    )
    n00, n01, n10, n11 = roll(a00, -1), roll(a01, -1), roll(a10, -1), roll(a11, -1)
    d00 = (12.0 * BEAM_EI + 36.0 * g) + (12.0 * BEAM_EI + 36.0 * gn) + mass
    d01 = (-6.0 * BEAM_EI - 3.0 * g) + (6.0 * BEAM_EI + 3.0 * gn)
    d11 = (4.0 * BEAM_EI + 4.0 * g) + (4.0 * BEAM_EI + 4.0 * gn)
    inside = lane < LANES - 1
    rho_w = jnp.where(inside, (d00 - jnp.maximum(-a00, -n00)) - jnp.minimum(-a00, -n00), 0.0)
    rho_s = jnp.where(inside, (d01 + a10) + n01, 0.0)
    first, last, end = lane == 0, lane == LANES - 2, lane == LANES - 1
    zero = jnp.zeros_like(t)
    row = row_iota(8)

    def stack(rows):
        out = jnp.zeros((8, LANES), jnp.float32)
        for index, value in enumerate(rows):
            out = jnp.where(row == index, value, out)
        return out

    Fw = stack(
        [
            rho_w,
            jnp.where(first, -a00, zero),
            jnp.where(first, -a01, zero),
            jnp.where(last, -n00, jnp.where(end, 1.0, zero)),
            jnp.where(last, -n10, zero),
        ]
    )
    Fs = stack(
        [
            rho_s,
            jnp.where(first, -a10, zero),
            jnp.where(first, -a11, zero),
            jnp.where(last, -n01, zero),
            jnp.where(last, -n11, jnp.where(end, 1.0, zero)),
        ]
    )
    coupled = jnp.logical_and(lane > 0, inside)
    A = tuple(jnp.where(coupled, x, 0.0) for x in (a00, a01, a10, a11))
    D = (jnp.where(inside, d00, 1.0), jnp.where(inside, d01, 0.0), jnp.where(inside, d11, 1.0))

    def rho_of(Fw, Fs):
        return Fw[0:1] + Fw[1:2] + Fw[3:4], Fs[0:1] + Fs[1:2] + Fs[3:4]

    Zw, Zs, steps, inverse = reduce_chain(A, D, (Fw, Fs), rho_of, [1 << b for b in range(7)])
    yw, ys = Zw[0:1], Zs[0:1]
    xa1w, xa1s = Zw[2:3], Zs[2:3]
    xb0w, xb0s, xb1w, xb1s = Zw[3:4], Zs[3:4], Zw[4:5], Zs[4:5]
    numbers = [
        (0, xb0w * a00 + xb0s * a10),
        (0, xb0w * a01 + xb0s * a11),
        (0, xb1w * a00 + xb1s * a10),
        (0, xb1w * a01 + xb1s * a11),
        (0, -(a00 * yw + a10 * ys)),
        (0, -(a01 * yw + a11 * ys)),
        (0, (4.0 * BEAM_EI + 4.0 * g) + (a01 * xa1w + a11 * xa1s)),
        (LANES - 2, -(n00 * yw + n01 * ys)),
        (LANES - 2, -(n10 * yw + n11 * ys)),
        (LANES - 2, (4.0 * BEAM_EI + 4.0 * gn) + (n10 * xb1w + n11 * xb1s)),
    ]
    row16 = row_iota(16)
    table = jnp.zeros((16, LANES), jnp.float32)
    for index, (spot, value) in enumerate(numbers):
        table = jnp.where((row16 == index) & (lane == spot), value, table)
    column = jnp.sum(table, axis=1, keepdims=True)
    message = jnp.sum(jnp.where(lane_iota(16) == row16, column, 0.0), axis=0, keepdims=True)
    answers = jnp.zeros((8, LANES), jnp.float32)
    for u in range(4):
        answers = jnp.where(row // 2 == u, Zw[u + 1 : u + 2], answers)
    return message, answers, steps, inverse


def chain_response(numbers, count, place, mass):
    lane = lane_iota(1)
    valid = lane < count
    row = row_iota(8)
    pick = lambda n: jnp.where(valid, numbers[n : n + 1], 0.0)
    a00, a01, a10, a11 = pick(0), pick(1), pick(2), pick(3)
    raw, ras, ka11, rbw, rbs, kb11 = [pick(n) for n in range(4, 10)]
    above = lambda x: jnp.where(lane < count - 1, roll(x, -1), 0.0)
    first = lane == 0
    rw = rbw + above(raw) + mass - jnp.where(first, a00, 0.0)
    rs = rbs + above(ras) - jnp.where(first, a10, 0.0)
    rw = jnp.where(valid, rw, 1.0)
    rs = jnp.where(valid, rs, 0.0)
    d11 = jnp.where(valid, kb11 + above(ka11), 1.0)
    A = tuple(jnp.where(first, 0.0, x) for x in (a00, a01, a10, a11))
    d00 = rw - A[0] - roll(A[0], -1)
    d01 = rs - A[2] - roll(A[1], -1)
    lane8 = lane_iota(8)
    mine = lane8 == place
    before = lane8 == place - 1
    Fw = jnp.where((before & (row == 0)) | (mine & (row == 2)), 1.0, 0.0)
    Fs = jnp.where((before & (row == 1)) | (mine & (row == 3)), 1.0, 0.0)
    Fw = jnp.where(row == 4, rw, Fw)
    Fs = jnp.where(row == 4, rs, Fs)
    strides = []
    while (1 << len(strides)) < count:
        strides.append(1 << len(strides))
    Gw, Gs, _, _ = reduce_chain(
        A, (d00, d01, d11), (Fw, Fs), lambda w, s: (w[4:5], s[4:5]), strides
    )
    Hw, Hs = roll(Gw, 1), roll(Gs, 1)
    blocks = []
    for u in range(4):
        block = jnp.where(row // 2 == 0, Hw[u : u + 1], 0.0)
        block = jnp.where(row // 2 == 1, Hs[u : u + 1], block)
        block = jnp.where(row // 2 == 2, Gw[u : u + 1], block)
        blocks.append(jnp.where(row // 2 == 3, Gs[u : u + 1], block))
    return blocks


def wide_loads(load):
    row = row_iota(8)
    return jnp.where(row % 2 == 0, load[0:1], load[1:2])


def end_loads(answers, load8):
    total = jnp.sum(answers * load8, axis=1, keepdims=True)
    lane = lane_iota(8)
    keep = (lane % 8 == row_iota(8)) & (lane < 32)
    return jnp.sum(jnp.where(keep, total, 0.0), axis=0, keepdims=True)


def ends_solved(response, loads):
    total = jnp.sum(response * loads, axis=0, keepdims=True)
    lane, row = lane_iota(8), row_iota(8)
    keep = (lane // 8 == row // 2) & (lane % 2 == row % 2) & (lane < 32)
    return jnp.sum(jnp.where(keep, total, 0.0), axis=1, keepdims=True)


def inner_deflection(steps, inverse, load8):
    inside = lane_iota(8) < LANES - 1
    Fw, Fs = jnp.where(inside, load8, 0.0), jnp.zeros((8, LANES), jnp.float32)
    for b in range(7):
        Fw, Fs = reduce_load(steps[b], Fw, Fs, 1 << b)
    return inverse[0] * Fw + inverse[1] * Fs


def kernel(
    count,
    ring,
    vel_hbm,
    speed_hbm,
    cbin_hbm,
    face_hbm,
    weight_hbm,
    tens_hbm,
    disp_hbm,
    rate_hbm,
    out,
    force_out,
    defl_out,
    V,
    U,
    W,
    TR,
    TL,
    TRw,
    TLw,
    near,
    full,
    PG,
    UG,
    FB,
    KB,
    RB,
    coef,
    speed,
    cbin,
    face,
    weight,
    tens,
    disp,
    rate,
    own_sem,
    small_sem,
    send_sem,
    theta_sem,
    near_sem,
    full_sem,
    force_sem,
    stiff_sem,
    load_sem,
    round_sem,
    corner,
    T,
    wall_next,
    shifts,
    shift_a,
    shift_b,
):
    vel = vel_hbm
    cells, rows = vel.shape[1], vel.shape[2]
    tiles = rows // 8
    base = 8
    k = lax.axis_index("span")
    s = lax.axis_index("sector")
    left, right = lax.rem(k + count - 1, count), lax.rem(k + 1, count)
    turn = lambda d: lax.rem(s + d + ring, ring)
    lower, upper = turn(-1), turn(1)
    ny = 4 if count >= 32 else 2
    nz = count // ny
    y, z = k // nz, lax.rem(k, nz)

    def torus(dy, dz):
        return lax.rem(y + dy + ny, ny) * nz + lax.rem(z + dz + nz, nz)

    low_end = jnp.where(k == 0, 1, 0)
    high_end = jnp.where(k == count - 1, 1, 0)
    mass = BEAM_MASS / LANES**2
    stride = cells + 2
    group = 2 * stride

    barrier = pltpu.get_barrier_semaphore()

    def signal(semaphore, span, sector):
        pl.semaphore_signal(
            semaphore, inc=1, device_id={"span": span, "sector": sector}, device_id_type=MESH
        )

    close = [(side, way) for side in (left, right) for way in (lower, upper)]
    close += [(left, s), (right, s)] + [(k, turn(d)) for d in range(1, ring)]
    close += [(torus(1, 0), s), (torus(-1, 0), s), (torus(0, 1), s), (torus(0, -1), s)]
    own_wall = pltpu.make_async_copy(
        vel.at[:, :, pl.ds(0, 8), :],
        V.at[:, pl.ds(2, cells), pl.ds(base, 8), :],
        own_sem.at[0],
    )
    for span, sector in close[:6]:
        signal(barrier, span, sector)
    own_wall.start()
    for span, sector in close[6:]:
        signal(barrier, span, sector)

    own_bulk = pltpu.make_async_copy(
        vel.at[:, :, pl.ds(8, rows - 8), :],
        V.at[:, pl.ds(2, cells), pl.ds(base + 8, rows - 8), :],
        own_sem.at[1],
    )
    small = [
        pltpu.make_async_copy(src, dst, small_sem.at[n])
        for n, (src, dst) in enumerate(
            (
                (speed_hbm, speed),
                (cbin_hbm, cbin),
                (face_hbm, face),
                (weight_hbm, weight),
                (tens_hbm, tens),
                (disp_hbm, disp),
                (rate_hbm, rate),
            )
        )
    ]
    for copy in small:
        copy.start()
    own_bulk.start()


    rounds = []
    known = 1
    while known < nz // 2:
        rounds.append([(torus(0, known), s), (torus(0, -known), s)])
        known *= 2
    rounds += [[(torus(1, 0), s), (torus(-1, 0), s)]] * 2

    def begin(n):
        for span, sector in rounds[n]:
            signal(round_sem.at[n], span, sector)

    def finish(n):
        pl.semaphore_wait(round_sem.at[n], len(rounds[n]))

    lane = lane_iota(1)
    row8 = row_iota(8)
    total_cells = cells * ring

    def angle_of(index):
        whole = lax.rem(s * cells + index + total_cells, total_cells)
        return 2.0 * math.pi * (whole.astype(jnp.float32) + 0.5) / total_cells

    ring_angle = angle_of(row_iota(24) - 1)
    ring_sin, ring_cos = jnp.sin(ring_angle), jnp.cos(ring_angle)
    lane_cell = lax.rem(lane, group) // 2 - 1
    lane_angle = angle_of(lane_cell)
    lane_sin, lane_cos = jnp.sin(lane_angle), jnp.cos(lane_angle)

    from_lane = lax.broadcasted_iota(jnp.int32, (LANES, 2 * LANES), 0)
    to_lane = lax.broadcasted_iota(jnp.int32, (LANES, 2 * LANES), 1)
    source = jnp.where(to_lane < LANES, to_lane + 1, to_lane - LANES - 1)
    source = jnp.where(to_lane == LANES - 1, -1, source)
    shifts[...] = jnp.where(from_lane == source, 1.0, 0.0).astype(jnp.bfloat16)

    own_wall.wait()
    TRw[...] = jnp.zeros((24, LANES), jnp.float32)
    TLw[...] = jnp.zeros((24, LANES), jnp.float32)
    lanes = lane_iota(cells)
    high = jnp.zeros((cells, LANES), jnp.float32)
    low = high
    for c in range(3):
        for j in range(3):
            own = V[c, pl.ds(2, cells), base + j, :]
            T[c, j, pl.ds(2, cells), :] = own
            spot = c * 3 + j
            turned = roll(own, 2 * spot + 2)
            high = jnp.where(lanes // 2 == spot, turned, high)
            low = jnp.where(lanes // 2 == spot + 1, turned, low)
    TRw[pl.ds(1, cells), :] = high
    TLw[pl.ds(1, cells), :] = roll(low, -2)

    def remote(src, dst, sent, arrived, span, sector):
        return pltpu.make_async_remote_copy(
            src_ref=src,
            dst_ref=dst,
            send_sem=sent,
            recv_sem=arrived,
            device_id={"span": span, "sector": sector},
            device_id_type=MESH,
        )

    spread = [
        (0, 0, right, s),
        (1, 1, left, s),
        (0, 2, right, upper),
        (1, 3, left, upper),
        (0, 4, right, lower),
        (1, 5, left, lower),
    ]
    near_copies = []
    for which, slot, span, sector in spread:
        src, dst = (TRw, TLw)[which], near.at[slot] if slot < 2 else corner.at[slot - 2]
        if slot >= 2:
            src = src.at[pl.ds(cells if slot < 4 else 0, 8), :]
        near_copies.append(remote(src, dst, send_sem.at[slot], near_sem.at[slot], span, sector))
    full_copies = [
        remote(
            (TR, TL)[which], full.at[slot], send_sem.at[6 + slot], full_sem.at[slot], span, sector
        )
        for which, slot, span, sector in spread
    ]
    theta_copies = []
    for part, (start, size) in enumerate(((0, 8), (8, rows - 8))):
        theta_copies.append(
            remote(
                vel.at[:, pl.ds(0, 2), pl.ds(start, size), :],
                V.at[:, pl.ds(cells + 2, 2), pl.ds(base + start, size), :],
                send_sem.at[12 + 2 * part],
                theta_sem.at[2 * part],
                k,
                lower,
            )
        )
        theta_copies.append(
            remote(
                vel.at[:, pl.ds(cells - 2, 2), pl.ds(start, size), :],
                V.at[:, pl.ds(0, 2), pl.ds(base + start, size), :],
                send_sem.at[13 + 2 * part],
                theta_sem.at[1 + 2 * part],
                k,
                upper,
            )
        )

    for copy in small:
        copy.wait()
    current = jnp.zeros((1, LANES), jnp.float32)
    for b in range(speed.shape[0]):
        current = current + jnp.where(cbin[...] == b, speed[b], 0.0)
    face_row = row_iota(24) - 1
    face_weight = jnp.zeros((24, LANES), jnp.float32)
    for q in range(weight.shape[0]):
        face_weight = face_weight + jnp.where(face_row == face[q], weight[q], 0.0)
    coef[0] = face_weight * ring_cos
    coef[1] = face_weight * ring_sin
    coef[2] = -current * ring_sin
    coef[3] = current * ring_cos
    cur_high = jnp.sum(jnp.where(lane == LANES - 1, current, 0.0), axis=1, keepdims=True)
    cur_low = jnp.sum(jnp.where(lane == 0, current, 0.0), axis=1, keepdims=True)
    wide = lane_iota(rows)
    TR[...] = jnp.where(wide == 3 * group + 1, cur_high, 0.0)
    TL[...] = jnp.where(wide == 3 * group + 2, cur_low, 0.0)
    own_bulk.wait()

    def outer_rows(i):
        return (
            coef[2, pl.ds(i + 1, 1), :],
            coef[3, pl.ds(i + 1, 1), :],
            jnp.zeros((1, LANES), jnp.float32),
        )

    def ghost_rows(i):
        for c, value in enumerate(outer_rows(i)):
            V[c, i + 2, pl.ds(base + rows, 1), :] = value
            V[c, i + 2, pl.ds(base - 1, 1), :] = -V[c, i + 2, pl.ds(base, 1), :]

    @pl.loop(0, cells)
    def _(i):
        high, low = TR[...], TL[...]
        for c in range(3):
            spot = c * group + 2 * (i + 1)
            turned = roll(V[c, i + 2, pl.ds(base, rows), :], spot + 2)
            high = jnp.where(wide // 2 == spot // 2, turned, high)
            low = jnp.where(wide // 2 == spot // 2 + 1, turned, low)
        TR[...] = high
        TL[...] = low
        ghost_rows(i)

    TL[...] = roll(TL[...], -2)
    pl.semaphore_wait(barrier, len(close))
    for copy in near_copies[2:] + near_copies[:2] + theta_copies[:2]:
        copy.start()
    begin(0)
    for copy in full_copies[2:] + full_copies[:2] + theta_copies[2:]:
        copy.start()

    message, answers, steps, inverse = slab_system(tens[...], mass)
    KB[pl.ds(k, 1), 0, :] = message
    advance = iter(range(len(rounds)))

    def next_round():
        n = next(advance, None)
        if n is not None:
            finish(n)
            if n + 1 < len(rounds):
                begin(n + 1)

    for _ in range(len(rounds) - 2):
        next_round()

    def everyone(buffer, sent, arrived):
        far = [(dy, dz) for dy in range(ny) for dz in range(nz) if (dy, dz) != (0, 0)]
        far.sort(key=lambda d: -(min(d[0], ny - d[0]) + min(d[1], nz - d[1])))
        for dy, dz in far:
            remote(buffer.at[k], buffer.at[k], sent, arrived, torus(dy, dz), s).start()

    def ghosts(boxes, high, low, depth):
        here = lane_iota(depth)
        evens = here % 2 == 0
        at_low = here * 0 + low_end == 1
        at_high = here * 0 + high_end == 1
        ahead = lambda x: roll(x, -1)
        behind = lambda x: roll(x, 1)
        centre = jnp.where(
            evens,
            jnp.where(at_low, low, ahead(boxes[0])),
            jnp.where(at_high, high, behind(boxes[1])),
        )
        outer = jnp.where(
            evens, jnp.where(at_low, low, boxes[0]), jnp.where(at_high, high, boxes[1])
        )
        inner = jnp.where(
            evens, jnp.where(at_low, ahead(low), low), jnp.where(at_high, behind(high), high)
        )
        return centre, outer, inner

    def with_corners(centre, boxes, depth):
        here = lane_iota(depth)
        evens = here % 2 == 0
        ahead = lambda x: roll(x, -1)
        behind = lambda x: roll(x, 1)
        down = roll(jnp.where(evens, ahead(boxes[2]), behind(boxes[3])), -2 * cells)
        up = roll(jnp.where(evens, ahead(boxes[4]), behind(boxes[5])), 2 * cells)
        own_down, own_up = jnp.zeros_like(down), jnp.zeros_like(up)
        for c in range(3):
            spot = c * group
            turned = roll(V[c, 1, pl.ds(base, depth), :], spot + 1)
            own_down = jnp.where(here // 2 == spot // 2, turned, own_down)
            spot = c * group + 2 * (cells + 1)
            turned = roll(V[c, cells + 2, pl.ds(base, depth), :], spot + 1)
            own_up = jnp.where(here // 2 == spot // 2, turned, own_up)
        own = own_down + own_up
        own = jnp.where(evens, ahead(own), behind(own))
        mirrored = jnp.where(evens, low_end, high_end) == 1
        cell = lax.rem(here, group) // 2 - 1
        in_fields = here < 3 * group
        centre = jnp.where(
            in_fields & (cell == -1),
            jnp.where(mirrored, own, down),
            jnp.where(in_fields & (cell == cells), jnp.where(mirrored, own, up), centre),
        )
        return centre

    def ghost_rates(centre, outer, inner, depth, top):
        here = lane_iota(depth)
        evens = here % 2 == 0
        which = here // group
        ups = {n: roll(centre, n * group) for n in (-2, -1, 1, 2)}
        of = lambda d: jnp.where(
            which == d,
            centre,
            jnp.where(
                which == (d + 1) % 3,
                ups[1] if d < 2 else ups[-2],
                ups[2] if d == 0 else ups[-1],
            ),
        )
        c0, c1, c2 = of(0), of(1), of(2)
        tu, td = roll(centre, -2), roll(centre, 2)
        sub = row_iota(depth)
        ru, rd = roll(centre, -1, 0), roll(centre, 1, 0)
        rd = jnp.where(sub == 0, -centre, rd)
        if top is not None:
            ru = jnp.where(sub == depth - 1, top, ru)
        su, sd = jnp.where(evens, inner, outer), jnp.where(evens, outer, inner)
        return combine(centre, c0, c1, c2, tu, td, ru, rd, su, sd)

    def combine(centre, c0, c1, c2, tu, td, ru, rd, su, sd):
        laplace = (tu + td) + (ru + rd) + (su + sd) - 6.0 * centre
        advect = c0 * (tu - td) + c1 * (ru - rd) + c2 * (su - sd)
        return NU_DT * laplace - (0.5 * ADV_DT) * advect

    for copy in near_copies + theta_copies[:2]:
        copy.wait_recv()
    for c in range(3):
        for j in range(3):
            T[c, j, pl.ds(0, 2), :] = V[c, pl.ds(0, 2), base + j, :]
            T[c, j, pl.ds(cells + 2, 2), :] = V[c, pl.ds(cells + 2, 2), base + j, :]
    wall_edge, outer, inner = ghosts([near[0], near[1]], TRw[...], TLw[...], 24)
    here, sub = lane_iota(24), row_iota(24)
    evens = here % 2 == 0
    own_first, own_last = jnp.zeros((8, LANES), jnp.float32), jnp.zeros((8, LANES), jnp.float32)
    lane8 = lane_iota(8)
    for c in range(3):
        for j in range(3):
            spot = c * 3 + j
            keep = lane8 // 2 == spot
            own_first = jnp.where(keep, roll(T[c, j, pl.ds(1, 8), :], 2 * spot + 1), own_first)
            own_last = jnp.where(keep, roll(T[c, j, pl.ds(17, 8), :], 2 * spot + 1), own_last)
    even8 = lane8 % 2 == 0
    mirrored = jnp.where(even8, low_end, high_end) == 1
    ends = []
    for own, left_box, right_box in (
        (own_first, corner[0], corner[1]),
        (own_last, corner[2], corner[3]),
    ):
        own = jnp.where(even8, roll(own, -1), roll(own, 1))
        sent = jnp.where(even8, roll(left_box, -1), roll(right_box, 1))
        ends.append(jnp.where(mirrored, own, sent))
    ends = jnp.concatenate([ends[0], ends[0], ends[1]], axis=0)
    wall_edge = jnp.where((sub == 0) | (sub == cells + 1), ends, wall_edge)

    def wall_beside(centre, edge, spot, depth):
        turned = roll(edge, -(2 * spot + 1))
        places = lane_iota(depth)
        return (
            roll(jnp.where(places == 0, turned, centre), -1),
            roll(jnp.where(places == LANES - 1, turned, centre), 1),
        )

    which = here // 6
    turns = {n: roll(wall_edge, 6 * n) for n in (-2, -1, 1, 2)}
    parts = [
        jnp.where(which == 0, wall_edge, jnp.where(which == 1, turns[1], turns[2])),
        jnp.where(which == 1, wall_edge, jnp.where(which == 2, turns[1], turns[-1])),
        jnp.where(which == 2, wall_edge, jnp.where(which == 1, turns[-1], turns[-2])),
    ]
    wall_next[...] = wall_edge + combine(
        wall_edge,
        *parts,
        roll(wall_edge, -1, 0),
        roll(wall_edge, 1, 0),
        roll(wall_edge, -2),
        jnp.where(here // 2 % 3 == 0, -wall_edge, roll(wall_edge, 2)),
        jnp.where(evens, inner, outer),
        jnp.where(evens, outer, inner),
    )
    for j in range(2):
        cell = [T[c, j, pl.ds(1, 24), :] for c in range(3)]
        for c in range(3):
            su, sd = wall_beside(cell[c], wall_edge, c * 3 + j, 24)
            W[c, j] = cell[c] + combine(
                cell[c],
                *cell,
                T[c, j, pl.ds(2, 24), :],
                T[c, j, pl.ds(0, 24), :],
                T[c, j + 1, pl.ds(1, 24), :],
                T[c, j - 1, pl.ds(1, 24), :] if j > 0 else -cell[c],
                su,
                sd,
            )
    cell = [W[c, 0, pl.ds(1, cells), :] for c in range(3)]
    fresh = []
    for c in range(2):
        su, sd = wall_beside(cell[c], wall_next[pl.ds(1, cells), :], c * 3, cells)
        rates = combine(
            cell[c],
            *cell,
            W[c, 0, pl.ds(2, cells), :],
            W[c, 0, pl.ds(0, cells), :],
            W[c, 1, pl.ds(1, cells), :],
            -cell[c],
            su,
            sd,
        )
        fresh.append(0.5 * (T[c, 0, pl.ds(2, cells), :] + cell[c] + rates))
    wc, ws = coef[0, pl.ds(1, cells), :], coef[1, pl.ds(1, cells), :]
    fx = jnp.sum(2.0 * WALL_NU * (fresh[1] * wc - fresh[0] * ws), axis=0, keepdims=True)
    fy = jnp.sum(2.0 * WALL_NU * (fresh[1] * ws + fresh[0] * wc), axis=0, keepdims=True)
    FB[s] = jnp.concatenate([fx, fy], axis=0)
    for d in sorted(range(1, ring), key=lambda d: -min(d, ring - d)):
        remote(FB.at[s], FB.at[s], send_sem.at[17], force_sem, k, turn(d)).start()

    next_round()
    for copy in full_copies + theta_copies[2:]:
        copy.wait_recv()
    boxes = [full[n] for n in range(6)]
    centre, outer, inner = ghosts(boxes, TR[...], TL[...], rows)
    centre = with_corners(centre, boxes, rows)
    swap = lambda x: jnp.where(lane_iota(rows) % 2 == 0, roll(x, -1), roll(x, 1))
    PG[...] = swap(centre)
    cur_lo = jnp.sum(
        jnp.where(lane == 3 * group, centre[0:1], 0.0), axis=1, keepdims=True
    )
    cur_hi = jnp.sum(
        jnp.where(lane == 3 * group + 1, centre[0:1], 0.0), axis=1, keepdims=True
    )
    cur_side = jnp.where(lane % 2 == 0, cur_lo, cur_hi)
    top = jnp.where(
        lane // group == 0,
        -cur_side * lane_sin,
        jnp.where(lane // group == 1, cur_side * lane_cos, 0.0),
    )
    UG[...] = swap(centre + ghost_rates(centre, outer, inner, rows, top))

    ghost_rows(-1)
    ghost_rows(cells)
    first_lane, last_lane = lane_iota(8) == 0, lane_iota(8) == LANES - 1

    def shift(field, i, moved):
        column = jnp.concatenate(
            [field(c, i, base + 8 * t) for c in range(3) for t in range(tiles)], axis=0
        )
        moved[...] = jnp.dot(
            column.astype(jnp.bfloat16), shifts[...], preferred_element_type=jnp.float32
        )

    def advanced(field, edge, i, scale, moved, store):
        for t in range(tiles):
            start = base + 8 * t
            here = [field(c, i, start) for c in range(3)]
            weights = []
            for d in range(3):
                half = (0.5 * ADV_DT * scale) * here[d]
                weights.append((NU_DT * scale - half, NU_DT * scale + half))
            for c in range(3):
                line = pl.ds((c * tiles + t) * 8, 8)
                at = c * group + 2 * (i + 1)
                ghost = roll(edge[pl.ds(8 * t, 8), :], lax.rem(2 * LANES - 1 - at, LANES))
                su = jnp.where(last_lane, ghost, moved[line, pl.ds(0, LANES)])
                sd = jnp.where(first_lane, ghost, moved[line, pl.ds(LANES, LANES)])
                total = weights[2][0] * su + weights[2][1] * sd
                total += weights[0][0] * field(c, i + 1, start)
                total += weights[0][1] * field(c, i - 1, start)
                total += weights[1][0] * field(c, i, start + 1)
                total += weights[1][1] * field(c, i, start - 1)
                store(c, t, total + (scale * (1.0 - 6.0 * NU_DT)) * here[c])

    def from_first(c, i, start):
        return V[c, i + 2, pl.ds(start, 8), :]

    def first_stage(pair):
        for n, ready, later in ((2 * pair, shift_a, shift_b), (2 * pair + 1, shift_b, shift_a)):

            def store(c, t, fresh, n=n):
                U[c, n, pl.ds(base + 8 * t, 8), :] = fresh
                if t == 0:
                    U[c, n, pl.ds(base - 1, 1), :] = -fresh[0:1]

            shift(from_first, n, later)
            advanced(from_first, PG, n - 1, 1.0, ready, store)
            for c, value in enumerate(outer_rows(n - 1)):
                U[c, n, pl.ds(base + rows, 1), :] = value

    shift(from_first, -1, shift_a)
    pl.loop(0, CUTS[0])(first_stage)
    next_round()
    everyone(KB, send_sem.at[16], stiff_sem)
    pl.loop(CUTS[0], CUTS[1])(first_stage)

    arrivals = ring - 1
    pltpu.make_async_copy(
        FB.at[pl.ds(0, arrivals)], FB.at[pl.ds(0, arrivals)], force_sem
    ).wait()
    force = FB[0]
    for n in range(1, ring):
        force = force + FB[n]
    force_out[...] = force
    load = force * LANES ** (-1.5) + mass * (disp[...] + rate[...])
    load8 = wide_loads(load)
    RB[pl.ds(k, 1), 0, :] = end_loads(answers, load8)

    everyone(RB, send_sem.at[18], load_sem)

    pl.loop(CUTS[1], cells // 2 + 1)(first_stage)

    def from_second(c, i, start):
        return U[c, i + 1, pl.ds(start, 8), :]

    shift(from_second, 0, shift_a)

    @pl.loop(0, cells // 2)
    def _(pair):
        for i, ready, later in ((2 * pair, shift_a, shift_b), (2 * pair + 1, shift_b, shift_a)):

            def store(c, t, value, i=i):
                out[c, i, pl.ds(8 * t, 8), :] = (
                    0.5 * V[c, i + 2, pl.ds(base + 8 * t, 8), :] + value
                )

            shift(from_second, i + 1, later)
            advanced(from_second, UG, i, 0.5, ready, store)

    others = count - 1
    pltpu.make_async_copy(KB.at[pl.ds(0, others)], KB.at[pl.ds(0, others)], stiff_sem).wait()
    spare = jnp.zeros((LANES - count, LANES), jnp.float32)
    numbers = jnp.concatenate([KB[:, 0, :], spare], axis=0).T
    blocks = chain_response(numbers, count, k, mass)
    blocks.append(jnp.zeros((LANES - 32, LANES), jnp.float32))
    response = jnp.concatenate(blocks, axis=0).T[0:count]
    rest = inner_deflection(steps, inverse, load8)

    pltpu.make_async_copy(RB.at[pl.ds(0, others)], RB.at[pl.ds(0, others)], load_sem).wait()
    ends = ends_solved(response, RB[:, 0, :])
    moved = ends * answers
    for direction in range(2):
        mine = jnp.sum(jnp.where(row8 % 2 == direction, moved, 0.0), axis=0, keepdims=True)
        defl_out[pl.ds(direction, 1), :] = rest[direction : direction + 1] + mine

    for copy in near_copies + full_copies + theta_copies:
        copy.wait_send()
    for sent, size, buffer in ((16, others, KB), (17, arrivals, FB), (18, others, RB)):
        pltpu.make_async_copy(
            buffer.at[pl.ds(0, size)], buffer.at[pl.ds(0, size)], send_sem.at[sent]
        ).wait()


def hand_over(fresh, force, defl, fresh_out, force_out, defl_out, sem):
    copies = [
        pltpu.make_async_copy(src, dst, sem.at[n])
        for n, (src, dst) in enumerate(
            ((fresh, fresh_out), (force, force_out), (defl, defl_out))
        )
    ]
    for copy in copies:
        copy.start()
    for copy in copies:
        copy.wait()


def solution(mesh):
    count, ring = mesh.shape["span"], mesh.shape["sector"]

    def local(velocity, speed, cbin, face, weight, tension, displacement, beam_rate):
        cells, rows, sections = velocity.shape[1:]
        far = pl.BlockSpec(memory_space=pltpu.HBM)
        vmem = pl.BlockSpec(memory_space=pltpu.VMEM)
        tall = rows + 16
        f32 = jnp.float32
        shapes = (
            jax.ShapeDtypeStruct(velocity.shape, f32),
            jax.ShapeDtypeStruct((2, sections), f32),
            jax.ShapeDtypeStruct((2, sections), f32),
        )
        results = pl.pallas_call(
            lambda *refs: kernel(count, ring, *refs),
            out_shape=shapes,
            in_specs=[far] * 8,
            out_specs=(vmem,) * 3,
            scratch_shapes=[
                pltpu.VMEM((3, cells + 4, tall, LANES), f32),
                pltpu.VMEM((3, cells + 2, tall, LANES), f32),
                pltpu.VMEM((3, 2, 24, LANES), f32),
                pltpu.VMEM((rows, LANES), f32),
                pltpu.VMEM((rows, LANES), f32),
                pltpu.VMEM((24, LANES), f32),
                pltpu.VMEM((24, LANES), f32),
                pltpu.VMEM((2, 24, LANES), f32),
                pltpu.VMEM((6, rows, LANES), f32),
                pltpu.VMEM((rows, LANES), f32),
                pltpu.VMEM((rows, LANES), f32),
                pltpu.VMEM((ring, 2, LANES), f32),
                pltpu.VMEM((count, 1, LANES), f32),
                pltpu.VMEM((count, 1, LANES), f32),
                pltpu.VMEM((4, 24, LANES), f32),
                pltpu.SMEM(speed.shape, f32),
                pltpu.VMEM((1, sections), jnp.int32),
                pltpu.SMEM(face.shape, jnp.int32),
                pltpu.SMEM(weight.shape, f32),
                pltpu.VMEM((1, sections), f32),
                pltpu.VMEM((2, sections), f32),
                pltpu.VMEM((2, sections), f32),
                pltpu.SemaphoreType.DMA((2,)),
                pltpu.SemaphoreType.DMA((7,)),
                pltpu.SemaphoreType.DMA((19,)),
                pltpu.SemaphoreType.DMA((4,)),
                pltpu.SemaphoreType.DMA((6,)),
                pltpu.SemaphoreType.DMA((6,)),
                pltpu.SemaphoreType.DMA,
                pltpu.SemaphoreType.DMA,
                pltpu.SemaphoreType.DMA,
                pltpu.SemaphoreType.REGULAR((6,)),
                pltpu.VMEM((4, 8, LANES), f32),
                pltpu.VMEM((3, 3, 32, LANES), f32),
                pltpu.VMEM((24, LANES), f32),
                pltpu.VMEM((LANES, 2 * LANES), jnp.bfloat16),
                pltpu.VMEM((3 * rows, 2 * LANES), f32),
                pltpu.VMEM((3 * rows, 2 * LANES), f32),
            ],
            compiler_params=pltpu.CompilerParams(
                collective_id=0, has_side_effects=True, vmem_limit_bytes=24 << 20
            ),
            name="riser",
        )(
            *[pltpu.with_memory_space_constraint(x, pltpu.HBM) for x in (velocity,
            speed,
            cbin.reshape(1, sections),
            face,
            weight,
            tension.reshape(1, sections),
            displacement,
            beam_rate)],
        )
        return pl.pallas_call(
            hand_over,
            out_shape=shapes,
            in_specs=[vmem] * 3,
            out_specs=(far,) * 3,
            scratch_shapes=[pltpu.SemaphoreType.DMA((3,))],
            name="results",
        )(*[pltpu.with_memory_space_constraint(x, pltpu.VMEM) for x in results])

    return jax.shard_map(
        local,
        mesh=mesh,
        in_specs=(
            P(None, "sector", None, "span"),
            P(),
            P("span"),
            P("sector"),
            P("sector"),
            P("span"),
            P(None, "span"),
            P(None, "span"),
        ),
        out_specs=(P(None, "sector", None, "span"), P(None, "span"), P(None, "span")),
        check_vma=False,
    )
```

```python
import math

import jax
import jax.numpy as jnp
from jax import lax
from jax.experimental import pallas as pl
from jax.experimental.pallas import tpu as pltpu
from jax.sharding import PartitionSpec as P

MESH = pl.DeviceIdType.MESH
NU_DT = 0.15
ADV_DT = 0.1
WALL_NU = 0.5
BEAM_EI = 0.5
BEAM_MASS = 0.4
LANES = 128
CUTS = (2, 7)


def roll(x, shift, axis=1):
    size = x.shape[axis]
    return pltpu.roll(x, shift % size if isinstance(shift, int) else shift, axis)


def lane_iota(rows):
    return lax.broadcasted_iota(jnp.int32, (rows, LANES), 1)


def row_iota(rows):
    return lax.broadcasted_iota(jnp.int32, (rows, LANES), 0)


def reduce_chain(A, D, F, rho_of, strides):
    A00, A01, A10, A11 = A
    D00, D01, D11 = D
    Fw, Fs = F
    steps = []
    for s in strides:
        inv = 1.0 / (D00 * D11 - D01 * D01)
        I00, I01, I11 = D11 * inv, -D01 * inv, D00 * inv
        P00 = I00 * A00 + I01 * A10
        P01 = I00 * A01 + I01 * A11
        P10 = I01 * A00 + I11 * A10
        P11 = I01 * A01 + I11 * A11
        E11 = A01 * P01 + A11 * P11
        I00m, I01m, I11m = roll(I00, s), roll(I01, s), roll(I11, s)
        al00 = A00 * I00m + A01 * I01m
        al01 = A00 * I01m + A01 * I11m
        al10 = A10 * I00m + A11 * I01m
        al11 = A10 * I01m + A11 * I11m
        ga00, ga01, ga10, ga11 = roll(P00, -s), roll(P10, -s), roll(P01, -s), roll(P11, -s)
        steps.append((al00, al01, al10, al11, ga00, ga01, ga10, ga11))
        P00m, P01m, P10m, P11m = roll(P00, s), roll(P01, s), roll(P10, s), roll(P11, s)
        D11 = D11 - (al10 * A10 + al11 * A11) - roll(E11, -s)
        Fw, Fs = reduce_load(steps[-1], Fw, Fs, s)
        A00, A01, A10, A11 = (
            -(A00 * P00m + A01 * P10m),
            -(A00 * P01m + A01 * P11m),
            -(A10 * P00m + A11 * P10m),
            -(A10 * P01m + A11 * P11m),
        )
        rw, rs = rho_of(Fw, Fs)
        D00 = rw - A00 - roll(A00, -2 * s)
        D01 = rs - A10 - roll(A01, -2 * s)
    inv = 1.0 / (D00 * D11 - D01 * D01)
    last = (D11 * inv, -D01 * inv, D00 * inv)
    return last[0] * Fw + last[1] * Fs, last[1] * Fw + last[2] * Fs, steps, last


def reduce_load(step, Fw, Fs, s):
    al00, al01, al10, al11, ga00, ga01, ga10, ga11 = step
    Fwm, Fsm, Fwp, Fsp = roll(Fw, s), roll(Fs, s), roll(Fw, -s), roll(Fs, -s)
    return (
        Fw - (al00 * Fwm + al01 * Fsm) - (ga00 * Fwp + ga01 * Fsp),
        Fs - (al10 * Fwm + al11 * Fsm) - (ga10 * Fwp + ga11 * Fsp),
    )


def slab_system(t, mass):
    lane = lane_iota(1)
    g = t / 30.0
    gn = roll(g, -1)
    a00, a01, a10, a11 = (
        -12.0 * BEAM_EI - 36.0 * g,
        -6.0 * BEAM_EI - 3.0 * g,
        6.0 * BEAM_EI + 3.0 * g,
        2.0 * BEAM_EI - g,
    )
    n00, n01, n10, n11 = roll(a00, -1), roll(a01, -1), roll(a10, -1), roll(a11, -1)
    d00 = (12.0 * BEAM_EI + 36.0 * g) + (12.0 * BEAM_EI + 36.0 * gn) + mass
    d01 = (-6.0 * BEAM_EI - 3.0 * g) + (6.0 * BEAM_EI + 3.0 * gn)
    d11 = (4.0 * BEAM_EI + 4.0 * g) + (4.0 * BEAM_EI + 4.0 * gn)
    inside = lane < LANES - 1
    rho_w = jnp.where(inside, (d00 - jnp.maximum(-a00, -n00)) - jnp.minimum(-a00, -n00), 0.0)
    rho_s = jnp.where(inside, (d01 + a10) + n01, 0.0)
    first, last, end = lane == 0, lane == LANES - 2, lane == LANES - 1
    zero = jnp.zeros_like(t)
    row = row_iota(8)

    def stack(rows):
        out = jnp.zeros((8, LANES), jnp.float32)
        for index, value in enumerate(rows):
            out = jnp.where(row == index, value, out)
        return out

    Fw = stack(
        [
            rho_w,
            jnp.where(first, -a00, zero),
            jnp.where(first, -a01, zero),
            jnp.where(last, -n00, jnp.where(end, 1.0, zero)),
            jnp.where(last, -n10, zero),
        ]
    )
    Fs = stack(
        [
            rho_s,
            jnp.where(first, -a10, zero),
            jnp.where(first, -a11, zero),
            jnp.where(last, -n01, zero),
            jnp.where(last, -n11, jnp.where(end, 1.0, zero)),
        ]
    )
    coupled = jnp.logical_and(lane > 0, inside)
    A = tuple(jnp.where(coupled, x, 0.0) for x in (a00, a01, a10, a11))
    D = (jnp.where(inside, d00, 1.0), jnp.where(inside, d01, 0.0), jnp.where(inside, d11, 1.0))

    def rho_of(Fw, Fs):
        return Fw[0:1] + Fw[1:2] + Fw[3:4], Fs[0:1] + Fs[1:2] + Fs[3:4]

    Zw, Zs, steps, inverse = reduce_chain(A, D, (Fw, Fs), rho_of, [1 << b for b in range(7)])
    yw, ys = Zw[0:1], Zs[0:1]
    xa1w, xa1s = Zw[2:3], Zs[2:3]
    xb0w, xb0s, xb1w, xb1s = Zw[3:4], Zs[3:4], Zw[4:5], Zs[4:5]
    numbers = [
        (0, xb0w * a00 + xb0s * a10),
        (0, xb0w * a01 + xb0s * a11),
        (0, xb1w * a00 + xb1s * a10),
        (0, xb1w * a01 + xb1s * a11),
        (0, -(a00 * yw + a10 * ys)),
        (0, -(a01 * yw + a11 * ys)),
        (0, (4.0 * BEAM_EI + 4.0 * g) + (a01 * xa1w + a11 * xa1s)),
        (LANES - 2, -(n00 * yw + n01 * ys)),
        (LANES - 2, -(n10 * yw + n11 * ys)),
        (LANES - 2, (4.0 * BEAM_EI + 4.0 * gn) + (n10 * xb1w + n11 * xb1s)),
    ]
    row16 = row_iota(16)
    table = jnp.zeros((16, LANES), jnp.float32)
    for index, (spot, value) in enumerate(numbers):
        table = jnp.where((row16 == index) & (lane == spot), value, table)
    column = jnp.sum(table, axis=1, keepdims=True)
    message = jnp.sum(jnp.where(lane_iota(16) == row16, column, 0.0), axis=0, keepdims=True)
    answers = jnp.zeros((8, LANES), jnp.float32)
    for u in range(4):
        answers = jnp.where(row // 2 == u, Zw[u + 1 : u + 2], answers)
    return message, answers, steps, inverse


def chain_response(numbers, count, place, mass):
    lane = lane_iota(1)
    valid = lane < count
    row = row_iota(8)
    pick = lambda n: jnp.where(valid, numbers[n : n + 1], 0.0)
    a00, a01, a10, a11 = pick(0), pick(1), pick(2), pick(3)
    raw, ras, ka11, rbw, rbs, kb11 = [pick(n) for n in range(4, 10)]
    above = lambda x: jnp.where(lane < count - 1, roll(x, -1), 0.0)
    first = lane == 0
    rw = rbw + above(raw) + mass - jnp.where(first, a00, 0.0)
    rs = rbs + above(ras) - jnp.where(first, a10, 0.0)
    rw = jnp.where(valid, rw, 1.0)
    rs = jnp.where(valid, rs, 0.0)
    d11 = jnp.where(valid, kb11 + above(ka11), 1.0)
    A = tuple(jnp.where(first, 0.0, x) for x in (a00, a01, a10, a11))
    d00 = rw - A[0] - roll(A[0], -1)
    d01 = rs - A[2] - roll(A[1], -1)
    lane8 = lane_iota(8)
    mine = lane8 == place
    before = lane8 == place - 1
    Fw = jnp.where((before & (row == 0)) | (mine & (row == 2)), 1.0, 0.0)
    Fs = jnp.where((before & (row == 1)) | (mine & (row == 3)), 1.0, 0.0)
    Fw = jnp.where(row == 4, rw, Fw)
    Fs = jnp.where(row == 4, rs, Fs)
    strides = []
    while (1 << len(strides)) < count:
        strides.append(1 << len(strides))
    Gw, Gs, _, _ = reduce_chain(
        A, (d00, d01, d11), (Fw, Fs), lambda w, s: (w[4:5], s[4:5]), strides
    )
    Hw, Hs = roll(Gw, 1), roll(Gs, 1)
    blocks = []
    for u in range(4):
        block = jnp.where(row // 2 == 0, Hw[u : u + 1], 0.0)
        block = jnp.where(row // 2 == 1, Hs[u : u + 1], block)
        block = jnp.where(row // 2 == 2, Gw[u : u + 1], block)
        blocks.append(jnp.where(row // 2 == 3, Gs[u : u + 1], block))
    return blocks


def wide_loads(load):
    row = row_iota(8)
    return jnp.where(row % 2 == 0, load[0:1], load[1:2])


def end_loads(answers, load8):
    total = jnp.sum(answers * load8, axis=1, keepdims=True)
    lane = lane_iota(8)
    keep = (lane % 8 == row_iota(8)) & (lane < 32)
    return jnp.sum(jnp.where(keep, total, 0.0), axis=0, keepdims=True)


def ends_solved(response, loads):
    total = jnp.sum(response * loads, axis=0, keepdims=True)
    lane, row = lane_iota(8), row_iota(8)
    keep = (lane // 8 == row // 2) & (lane % 2 == row % 2) & (lane < 32)
    return jnp.sum(jnp.where(keep, total, 0.0), axis=1, keepdims=True)


def inner_deflection(steps, inverse, load8):
    inside = lane_iota(8) < LANES - 1
    Fw, Fs = jnp.where(inside, load8, 0.0), jnp.zeros((8, LANES), jnp.float32)
    for b in range(7):
        Fw, Fs = reduce_load(steps[b], Fw, Fs, 1 << b)
    return inverse[0] * Fw + inverse[1] * Fs


def kernel(
    count,
    ring,
    vel_hbm,
    speed_hbm,
    cbin_hbm,
    face_hbm,
    weight_hbm,
    tens_hbm,
    disp_hbm,
    rate_hbm,
    out,
    force_out,
    defl_out,
    V,
    U,
    W,
    TR,
    TL,
    TRw,
    TLw,
    near,
    full,
    PG,
    UG,
    FB,
    KB,
    RB,
    coef,
    speed,
    cbin,
    face,
    weight,
    tens,
    disp,
    rate,
    own_sem,
    small_sem,
    send_sem,
    theta_sem,
    near_sem,
    full_sem,
    force_sem,
    stiff_sem,
    load_sem,
    round_sem,
    corner,
    T,
    wall_next,
    shifts,
    shift_a,
    shift_b,
):
    vel = vel_hbm
    cells, rows = vel.shape[1], vel.shape[2]
    tiles = rows // 8
    base = 8
    k = lax.axis_index("span")
    s = lax.axis_index("sector")
    left, right = lax.rem(k + count - 1, count), lax.rem(k + 1, count)
    turn = lambda d: lax.rem(s + d + ring, ring)
    lower, upper = turn(-1), turn(1)
    ny = 4 if count >= 32 else 2
    nz = count // ny
    y, z = k // nz, lax.rem(k, nz)

    def torus(dy, dz):
        return lax.rem(y + dy + ny, ny) * nz + lax.rem(z + dz + nz, nz)

    low_end = jnp.where(k == 0, 1, 0)
    high_end = jnp.where(k == count - 1, 1, 0)
    mass = BEAM_MASS / LANES**2
    stride = cells + 2
    group = 2 * stride

    barrier = pltpu.get_barrier_semaphore()

    def signal(semaphore, span, sector):
        pl.semaphore_signal(
            semaphore, inc=1, device_id={"span": span, "sector": sector}, device_id_type=MESH
        )

    close = [(side, way) for side in (left, right) for way in (lower, upper)]
    close += [(left, s), (right, s)] + [(k, turn(d)) for d in range(1, ring)]
    close += [(torus(0, 1), s), (torus(0, -1), s)] + [(torus(d, 0), s) for d in range(1, ny)]
    own_wall = pltpu.make_async_copy(
        vel.at[:, :, pl.ds(0, 8), :],
        V.at[:, pl.ds(2, cells), pl.ds(base, 8), :],
        own_sem.at[0],
    )
    for span, sector in close[:6]:
        signal(barrier, span, sector)
    own_wall.start()
    for span, sector in close[6:]:
        signal(barrier, span, sector)

    own_bulk = pltpu.make_async_copy(
        vel.at[:, :, pl.ds(8, rows - 8), :],
        V.at[:, pl.ds(2, cells), pl.ds(base + 8, rows - 8), :],
        own_sem.at[1],
    )
    small = [
        pltpu.make_async_copy(src, dst, small_sem.at[n])
        for n, (src, dst) in enumerate(
            (
                (speed_hbm, speed),
                (cbin_hbm, cbin),
                (face_hbm, face),
                (weight_hbm, weight),
                (tens_hbm, tens),
                (disp_hbm, disp),
                (rate_hbm, rate),
            )
        )
    ]
    for copy in small:
        copy.start()
    own_bulk.start()


    rounds = [[(torus(0, 1), s), (torus(0, -1), s)]]
    known = 1
    while known < nz // 2:
        reach = min(known + 1, nz // 2 - known)
        rounds.append([(torus(0, reach), s), (torus(0, -reach), s)])
        known += reach

    def begin(n):
        for span, sector in rounds[n]:
            signal(round_sem.at[n], span, sector)

    def finish(n):
        pl.semaphore_wait(round_sem.at[n], len(rounds[n]))

    lane = lane_iota(1)
    row8 = row_iota(8)
    total_cells = cells * ring

    def angle_of(index):
        whole = lax.rem(s * cells + index + total_cells, total_cells)
        return 2.0 * math.pi * (whole.astype(jnp.float32) + 0.5) / total_cells

    ring_angle = angle_of(row_iota(24) - 1)
    ring_sin, ring_cos = jnp.sin(ring_angle), jnp.cos(ring_angle)
    lane_cell = lax.rem(lane, group) // 2 - 1
    lane_angle = angle_of(lane_cell)
    lane_sin, lane_cos = jnp.sin(lane_angle), jnp.cos(lane_angle)

    from_lane = lax.broadcasted_iota(jnp.int32, (LANES, 2 * LANES), 0)
    to_lane = lax.broadcasted_iota(jnp.int32, (LANES, 2 * LANES), 1)
    source = jnp.where(to_lane < LANES, to_lane + 1, to_lane - LANES - 1)
    source = jnp.where(to_lane == LANES - 1, -1, source)
    shifts[...] = jnp.where(from_lane == source, 1.0, 0.0).astype(jnp.bfloat16)

    own_wall.wait()
    TRw[...] = jnp.zeros((24, LANES), jnp.float32)
    TLw[...] = jnp.zeros((24, LANES), jnp.float32)
    lanes = lane_iota(cells)
    high = jnp.zeros((cells, LANES), jnp.float32)
    low = high
    for c in range(3):
        for j in range(3):
            own = V[c, pl.ds(2, cells), base + j, :]
            T[c, j, pl.ds(2, cells), :] = own
            spot = c * 3 + j
            turned = roll(own, 2 * spot + 2)
            high = jnp.where(lanes // 2 == spot, turned, high)
            low = jnp.where(lanes // 2 == spot + 1, turned, low)
    TRw[pl.ds(1, cells), :] = high
    TLw[pl.ds(1, cells), :] = roll(low, -2)

    def remote(src, dst, sent, arrived, span, sector):
        return pltpu.make_async_remote_copy(
            src_ref=src,
            dst_ref=dst,
            send_sem=sent,
            recv_sem=arrived,
            device_id={"span": span, "sector": sector},
            device_id_type=MESH,
        )

    spread = [
        (0, 0, right, s),
        (1, 1, left, s),
        (0, 2, right, upper),
        (1, 3, left, upper),
        (0, 4, right, lower),
        (1, 5, left, lower),
    ]
    near_copies = []
    for which, slot, span, sector in spread:
        src, dst = (TRw, TLw)[which], near.at[slot] if slot < 2 else corner.at[slot - 2]
        if slot >= 2:
            src = src.at[pl.ds(cells if slot < 4 else 0, 8), :]
        near_copies.append(remote(src, dst, send_sem.at[slot], near_sem.at[slot], span, sector))
    full_copies = [
        remote(
            (TR, TL)[which], full.at[slot], send_sem.at[6 + slot], full_sem.at[slot], span, sector
        )
        for which, slot, span, sector in spread
    ]
    theta_copies = []
    for part, (start, size) in enumerate(((0, 8), (8, rows - 8))):
        theta_copies.append(
            remote(
                vel.at[:, pl.ds(0, 2), pl.ds(start, size), :],
                V.at[:, pl.ds(cells + 2, 2), pl.ds(base + start, size), :],
                send_sem.at[12 + 2 * part],
                theta_sem.at[2 * part],
                k,
                lower,
            )
        )
        theta_copies.append(
            remote(
                vel.at[:, pl.ds(cells - 2, 2), pl.ds(start, size), :],
                V.at[:, pl.ds(0, 2), pl.ds(base + start, size), :],
                send_sem.at[13 + 2 * part],
                theta_sem.at[1 + 2 * part],
                k,
                upper,
            )
        )

    for copy in small:
        copy.wait()
    current = jnp.zeros((1, LANES), jnp.float32)
    for b in range(speed.shape[0]):
        current = current + jnp.where(cbin[...] == b, speed[b], 0.0)
    face_row = row_iota(24) - 1
    face_weight = jnp.zeros((24, LANES), jnp.float32)
    for q in range(weight.shape[0]):
        face_weight = face_weight + jnp.where(face_row == face[q], weight[q], 0.0)
    coef[0] = face_weight * ring_cos
    coef[1] = face_weight * ring_sin
    coef[2] = -current * ring_sin
    coef[3] = current * ring_cos
    cur_high = jnp.sum(jnp.where(lane == LANES - 1, current, 0.0), axis=1, keepdims=True)
    cur_low = jnp.sum(jnp.where(lane == 0, current, 0.0), axis=1, keepdims=True)
    wide = lane_iota(rows)
    TR[...] = jnp.where(wide == 3 * group + 1, cur_high, 0.0)
    TL[...] = jnp.where(wide == 3 * group + 2, cur_low, 0.0)
    own_bulk.wait()

    def outer_rows(i):
        return (
            coef[2, pl.ds(i + 1, 1), :],
            coef[3, pl.ds(i + 1, 1), :],
            jnp.zeros((1, LANES), jnp.float32),
        )

    def ghost_rows(i):
        for c, value in enumerate(outer_rows(i)):
            V[c, i + 2, pl.ds(base + rows, 1), :] = value
            V[c, i + 2, pl.ds(base - 1, 1), :] = -V[c, i + 2, pl.ds(base, 1), :]

    @pl.loop(0, cells)
    def _(i):
        high, low = TR[...], TL[...]
        for c in range(3):
            spot = c * group + 2 * (i + 1)
            turned = roll(V[c, i + 2, pl.ds(base, rows), :], spot + 2)
            high = jnp.where(wide // 2 == spot // 2, turned, high)
            low = jnp.where(wide // 2 == spot // 2 + 1, turned, low)
        TR[...] = high
        TL[...] = low
        ghost_rows(i)

    TL[...] = roll(TL[...], -2)
    pl.semaphore_wait(barrier, len(close))
    for copy in near_copies[2:] + near_copies[:2] + theta_copies[:2]:
        copy.start()
    begin(0)
    for copy in full_copies[2:] + full_copies[:2] + theta_copies[2:]:
        copy.start()

    message, answers, steps, inverse = slab_system(tens[...], mass)
    KB[pl.ds(k, 1), 0, :] = message
    advance = iter(range(len(rounds)))

    def next_round():
        n = next(advance, None)
        if n is not None:
            finish(n)
            if n + 1 < len(rounds):
                begin(n + 1)

    for _ in range(len(rounds) - 1):
        next_round()

    def everyone(buffer, sent, arrived):
        far = [(dy, dz) for dy in range(ny) for dz in range(nz) if (dy, dz) != (0, 0)]
        far.sort(key=lambda d: -(min(d[0], ny - d[0]) + min(d[1], nz - d[1])))
        for dy, dz in far:
            remote(buffer.at[k], buffer.at[k], sent, arrived, torus(dy, dz), s).start()

    def ghosts(boxes, high, low, depth):
        here = lane_iota(depth)
        evens = here % 2 == 0
        at_low = here * 0 + low_end == 1
        at_high = here * 0 + high_end == 1
        ahead = lambda x: roll(x, -1)
        behind = lambda x: roll(x, 1)
        centre = jnp.where(
            evens,
            jnp.where(at_low, low, ahead(boxes[0])),
            jnp.where(at_high, high, behind(boxes[1])),
        )
        outer = jnp.where(
            evens, jnp.where(at_low, low, boxes[0]), jnp.where(at_high, high, boxes[1])
        )
        inner = jnp.where(
            evens, jnp.where(at_low, ahead(low), low), jnp.where(at_high, behind(high), high)
        )
        return centre, outer, inner

    def with_corners(centre, boxes, depth):
        here = lane_iota(depth)
        evens = here % 2 == 0
        ahead = lambda x: roll(x, -1)
        behind = lambda x: roll(x, 1)
        down = roll(jnp.where(evens, ahead(boxes[2]), behind(boxes[3])), -2 * cells)
        up = roll(jnp.where(evens, ahead(boxes[4]), behind(boxes[5])), 2 * cells)
        own_down, own_up = jnp.zeros_like(down), jnp.zeros_like(up)
        for c in range(3):
            spot = c * group
            turned = roll(V[c, 1, pl.ds(base, depth), :], spot + 1)
            own_down = jnp.where(here // 2 == spot // 2, turned, own_down)
            spot = c * group + 2 * (cells + 1)
            turned = roll(V[c, cells + 2, pl.ds(base, depth), :], spot + 1)
            own_up = jnp.where(here // 2 == spot // 2, turned, own_up)
        own = own_down + own_up
        own = jnp.where(evens, ahead(own), behind(own))
        mirrored = jnp.where(evens, low_end, high_end) == 1
        cell = lax.rem(here, group) // 2 - 1
        in_fields = here < 3 * group
        centre = jnp.where(
            in_fields & (cell == -1),
            jnp.where(mirrored, own, down),
            jnp.where(in_fields & (cell == cells), jnp.where(mirrored, own, up), centre),
        )
        return centre

    def ghost_rates(centre, outer, inner, depth, top):
        here = lane_iota(depth)
        evens = here % 2 == 0
        which = here // group
        ups = {n: roll(centre, n * group) for n in (-2, -1, 1, 2)}
        of = lambda d: jnp.where(
            which == d,
            centre,
            jnp.where(
                which == (d + 1) % 3,
                ups[1] if d < 2 else ups[-2],
                ups[2] if d == 0 else ups[-1],
            ),
        )
        c0, c1, c2 = of(0), of(1), of(2)
        tu, td = roll(centre, -2), roll(centre, 2)
        sub = row_iota(depth)
        ru, rd = roll(centre, -1, 0), roll(centre, 1, 0)
        rd = jnp.where(sub == 0, -centre, rd)
        if top is not None:
            ru = jnp.where(sub == depth - 1, top, ru)
        su, sd = jnp.where(evens, inner, outer), jnp.where(evens, outer, inner)
        return combine(centre, c0, c1, c2, tu, td, ru, rd, su, sd)

    def combine(centre, c0, c1, c2, tu, td, ru, rd, su, sd):
        laplace = (tu + td) + (ru + rd) + (su + sd) - 6.0 * centre
        advect = c0 * (tu - td) + c1 * (ru - rd) + c2 * (su - sd)
        return NU_DT * laplace - (0.5 * ADV_DT) * advect

    for copy in near_copies + theta_copies[:2]:
        copy.wait_recv()
    for c in range(3):
        for j in range(3):
            T[c, j, pl.ds(0, 2), :] = V[c, pl.ds(0, 2), base + j, :]
            T[c, j, pl.ds(cells + 2, 2), :] = V[c, pl.ds(cells + 2, 2), base + j, :]
    wall_edge, outer, inner = ghosts([near[0], near[1]], TRw[...], TLw[...], 24)
    here, sub = lane_iota(24), row_iota(24)
    evens = here % 2 == 0
    own_first, own_last = jnp.zeros((8, LANES), jnp.float32), jnp.zeros((8, LANES), jnp.float32)
    lane8 = lane_iota(8)
    for c in range(3):
        for j in range(3):
            spot = c * 3 + j
            keep = lane8 // 2 == spot
            own_first = jnp.where(keep, roll(T[c, j, pl.ds(1, 8), :], 2 * spot + 1), own_first)
            own_last = jnp.where(keep, roll(T[c, j, pl.ds(17, 8), :], 2 * spot + 1), own_last)
    even8 = lane8 % 2 == 0
    mirrored = jnp.where(even8, low_end, high_end) == 1
    ends = []
    for own, left_box, right_box in (
        (own_first, corner[0], corner[1]),
        (own_last, corner[2], corner[3]),
    ):
        own = jnp.where(even8, roll(own, -1), roll(own, 1))
        sent = jnp.where(even8, roll(left_box, -1), roll(right_box, 1))
        ends.append(jnp.where(mirrored, own, sent))
    ends = jnp.concatenate([ends[0], ends[0], ends[1]], axis=0)
    wall_edge = jnp.where((sub == 0) | (sub == cells + 1), ends, wall_edge)

    def wall_beside(centre, edge, spot, depth):
        turned = roll(edge, -(2 * spot + 1))
        places = lane_iota(depth)
        return (
            roll(jnp.where(places == 0, turned, centre), -1),
            roll(jnp.where(places == LANES - 1, turned, centre), 1),
        )

    which = here // 6
    turns = {n: roll(wall_edge, 6 * n) for n in (-2, -1, 1, 2)}
    parts = [
        jnp.where(which == 0, wall_edge, jnp.where(which == 1, turns[1], turns[2])),
        jnp.where(which == 1, wall_edge, jnp.where(which == 2, turns[1], turns[-1])),
        jnp.where(which == 2, wall_edge, jnp.where(which == 1, turns[-1], turns[-2])),
    ]
    wall_next[...] = wall_edge + combine(
        wall_edge,
        *parts,
        roll(wall_edge, -1, 0),
        roll(wall_edge, 1, 0),
        roll(wall_edge, -2),
        jnp.where(here // 2 % 3 == 0, -wall_edge, roll(wall_edge, 2)),
        jnp.where(evens, inner, outer),
        jnp.where(evens, outer, inner),
    )
    for j in range(2):
        cell = [T[c, j, pl.ds(1, 24), :] for c in range(3)]
        for c in range(3):
            su, sd = wall_beside(cell[c], wall_edge, c * 3 + j, 24)
            W[c, j] = cell[c] + combine(
                cell[c],
                *cell,
                T[c, j, pl.ds(2, 24), :],
                T[c, j, pl.ds(0, 24), :],
                T[c, j + 1, pl.ds(1, 24), :],
                T[c, j - 1, pl.ds(1, 24), :] if j > 0 else -cell[c],
                su,
                sd,
            )
    cell = [W[c, 0, pl.ds(1, cells), :] for c in range(3)]
    fresh = []
    for c in range(2):
        su, sd = wall_beside(cell[c], wall_next[pl.ds(1, cells), :], c * 3, cells)
        rates = combine(
            cell[c],
            *cell,
            W[c, 0, pl.ds(2, cells), :],
            W[c, 0, pl.ds(0, cells), :],
            W[c, 1, pl.ds(1, cells), :],
            -cell[c],
            su,
            sd,
        )
        fresh.append(0.5 * (T[c, 0, pl.ds(2, cells), :] + cell[c] + rates))
    wc, ws = coef[0, pl.ds(1, cells), :], coef[1, pl.ds(1, cells), :]
    fx = jnp.sum(2.0 * WALL_NU * (fresh[1] * wc - fresh[0] * ws), axis=0, keepdims=True)
    fy = jnp.sum(2.0 * WALL_NU * (fresh[1] * ws + fresh[0] * wc), axis=0, keepdims=True)
    FB[s] = jnp.concatenate([fx, fy], axis=0)
    for d in sorted(range(1, ring), key=lambda d: -min(d, ring - d)):
        remote(FB.at[s], FB.at[s], send_sem.at[17], force_sem, k, turn(d)).start()

    for copy in full_copies + theta_copies[2:]:
        copy.wait_recv()
    boxes = [full[n] for n in range(6)]
    centre, outer, inner = ghosts(boxes, TR[...], TL[...], rows)
    centre = with_corners(centre, boxes, rows)
    swap = lambda x: jnp.where(lane_iota(rows) % 2 == 0, roll(x, -1), roll(x, 1))
    PG[...] = swap(centre)
    cur_lo = jnp.sum(
        jnp.where(lane == 3 * group, centre[0:1], 0.0), axis=1, keepdims=True
    )
    cur_hi = jnp.sum(
        jnp.where(lane == 3 * group + 1, centre[0:1], 0.0), axis=1, keepdims=True
    )
    cur_side = jnp.where(lane % 2 == 0, cur_lo, cur_hi)
    top = jnp.where(
        lane // group == 0,
        -cur_side * lane_sin,
        jnp.where(lane // group == 1, cur_side * lane_cos, 0.0),
    )
    UG[...] = swap(centre + ghost_rates(centre, outer, inner, rows, top))

    ghost_rows(-1)
    ghost_rows(cells)
    first_lane, last_lane = lane_iota(8) == 0, lane_iota(8) == LANES - 1

    def shift(field, i, moved):
        column = jnp.concatenate(
            [field(c, i, base + 8 * t) for c in range(3) for t in range(tiles)], axis=0
        )
        moved[...] = jnp.dot(
            column.astype(jnp.bfloat16), shifts[...], preferred_element_type=jnp.float32
        )

    def advanced(field, edge, i, scale, moved, store):
        for t in range(tiles):
            start = base + 8 * t
            here = [field(c, i, start) for c in range(3)]
            weights = []
            for d in range(3):
                half = (0.5 * ADV_DT * scale) * here[d]
                weights.append((NU_DT * scale - half, NU_DT * scale + half))
            for c in range(3):
                line = pl.ds((c * tiles + t) * 8, 8)
                at = c * group + 2 * (i + 1)
                ghost = roll(edge[pl.ds(8 * t, 8), :], lax.rem(2 * LANES - 1 - at, LANES))
                su = jnp.where(last_lane, ghost, moved[line, pl.ds(0, LANES)])
                sd = jnp.where(first_lane, ghost, moved[line, pl.ds(LANES, LANES)])
                total = weights[2][0] * su + weights[2][1] * sd
                total += weights[0][0] * field(c, i + 1, start)
                total += weights[0][1] * field(c, i - 1, start)
                total += weights[1][0] * field(c, i, start + 1)
                total += weights[1][1] * field(c, i, start - 1)
                store(c, t, total + (scale * (1.0 - 6.0 * NU_DT)) * here[c])

    def from_first(c, i, start):
        return V[c, i + 2, pl.ds(start, 8), :]

    def first_stage(pair):
        for n, ready, later in ((2 * pair, shift_a, shift_b), (2 * pair + 1, shift_b, shift_a)):

            def store(c, t, fresh, n=n):
                U[c, n, pl.ds(base + 8 * t, 8), :] = fresh
                if t == 0:
                    U[c, n, pl.ds(base - 1, 1), :] = -fresh[0:1]

            shift(from_first, n, later)
            advanced(from_first, PG, n - 1, 1.0, ready, store)
            for c, value in enumerate(outer_rows(n - 1)):
                U[c, n, pl.ds(base + rows, 1), :] = value

    shift(from_first, -1, shift_a)
    pl.loop(0, CUTS[0])(first_stage)
    next_round()
    everyone(KB, send_sem.at[16], stiff_sem)
    pl.loop(CUTS[0], CUTS[1])(first_stage)

    arrivals = ring - 1
    pltpu.make_async_copy(
        FB.at[pl.ds(0, arrivals)], FB.at[pl.ds(0, arrivals)], force_sem
    ).wait()
    force = FB[0]
    for n in range(1, ring):
        force = force + FB[n]
    force_out[...] = force
    load = force * LANES ** (-1.5) + mass * (disp[...] + rate[...])
    load8 = wide_loads(load)
    RB[pl.ds(k, 1), 0, :] = end_loads(answers, load8)

    everyone(RB, send_sem.at[18], load_sem)

    pl.loop(CUTS[1], cells // 2 + 1)(first_stage)

    def from_second(c, i, start):
        return U[c, i + 1, pl.ds(start, 8), :]

    shift(from_second, 0, shift_a)

    @pl.loop(0, cells // 2)
    def _(pair):
        for i, ready, later in ((2 * pair, shift_a, shift_b), (2 * pair + 1, shift_b, shift_a)):

            def store(c, t, value, i=i):
                out[c, i, pl.ds(8 * t, 8), :] = (
                    0.5 * V[c, i + 2, pl.ds(base + 8 * t, 8), :] + value
                )

            shift(from_second, i + 1, later)
            advanced(from_second, UG, i, 0.5, ready, store)

    others = count - 1
    pltpu.make_async_copy(KB.at[pl.ds(0, others)], KB.at[pl.ds(0, others)], stiff_sem).wait()
    spare = jnp.zeros((LANES - count, LANES), jnp.float32)
    numbers = jnp.concatenate([KB[:, 0, :], spare], axis=0).T
    blocks = chain_response(numbers, count, k, mass)
    blocks.append(jnp.zeros((LANES - 32, LANES), jnp.float32))
    response = jnp.concatenate(blocks, axis=0).T[0:count]
    rest = inner_deflection(steps, inverse, load8)

    for copy in near_copies + full_copies + theta_copies:
        copy.wait_send()
    for sent, size, buffer in ((16, others, KB), (17, arrivals, FB), (18, others, RB)):
        pltpu.make_async_copy(
            buffer.at[pl.ds(0, size)], buffer.at[pl.ds(0, size)], send_sem.at[sent]
        ).wait()

    pltpu.make_async_copy(RB.at[pl.ds(0, others)], RB.at[pl.ds(0, others)], load_sem).wait()
    ends = ends_solved(response, RB[:, 0, :])
    moved = ends * answers
    for direction in range(2):
        mine = jnp.sum(jnp.where(row8 % 2 == direction, moved, 0.0), axis=0, keepdims=True)
        defl_out[pl.ds(direction, 1), :] = rest[direction : direction + 1] + mine


def hand_over(fresh, force, defl, fresh_out, force_out, defl_out, sem):
    copies = [
        pltpu.make_async_copy(src, dst, sem.at[n])
        for n, (src, dst) in enumerate(
            ((fresh, fresh_out), (force, force_out), (defl, defl_out))
        )
    ]
    for copy in copies:
        copy.start()
    for copy in copies:
        copy.wait()


def solution(mesh):
    count, ring = mesh.shape["span"], mesh.shape["sector"]

    def local(velocity, speed, cbin, face, weight, tension, displacement, beam_rate):
        cells, rows, sections = velocity.shape[1:]
        far = pl.BlockSpec(memory_space=pltpu.HBM)
        vmem = pl.BlockSpec(memory_space=pltpu.VMEM)
        tall = rows + 16
        f32 = jnp.float32
        shapes = (
            jax.ShapeDtypeStruct(velocity.shape, f32),
            jax.ShapeDtypeStruct((2, sections), f32),
            jax.ShapeDtypeStruct((2, sections), f32),
        )
        results = pl.pallas_call(
            lambda *refs: kernel(count, ring, *refs),
            out_shape=shapes,
            in_specs=[far] * 8,
            out_specs=(vmem,) * 3,
            scratch_shapes=[
                pltpu.VMEM((3, cells + 4, tall, LANES), f32),
                pltpu.VMEM((3, cells + 2, tall, LANES), f32),
                pltpu.VMEM((3, 2, 24, LANES), f32),
                pltpu.VMEM((rows, LANES), f32),
                pltpu.VMEM((rows, LANES), f32),
                pltpu.VMEM((24, LANES), f32),
                pltpu.VMEM((24, LANES), f32),
                pltpu.VMEM((2, 24, LANES), f32),
                pltpu.VMEM((6, rows, LANES), f32),
                pltpu.VMEM((rows, LANES), f32),
                pltpu.VMEM((rows, LANES), f32),
                pltpu.VMEM((ring, 2, LANES), f32),
                pltpu.VMEM((count, 1, LANES), f32),
                pltpu.VMEM((count, 1, LANES), f32),
                pltpu.VMEM((4, 24, LANES), f32),
                pltpu.SMEM(speed.shape, f32),
                pltpu.VMEM((1, sections), jnp.int32),
                pltpu.SMEM(face.shape, jnp.int32),
                pltpu.SMEM(weight.shape, f32),
                pltpu.VMEM((1, sections), f32),
                pltpu.VMEM((2, sections), f32),
                pltpu.VMEM((2, sections), f32),
                pltpu.SemaphoreType.DMA((2,)),
                pltpu.SemaphoreType.DMA((7,)),
                pltpu.SemaphoreType.DMA((19,)),
                pltpu.SemaphoreType.DMA((4,)),
                pltpu.SemaphoreType.DMA((6,)),
                pltpu.SemaphoreType.DMA((6,)),
                pltpu.SemaphoreType.DMA,
                pltpu.SemaphoreType.DMA,
                pltpu.SemaphoreType.DMA,
                pltpu.SemaphoreType.REGULAR((6,)),
                pltpu.VMEM((4, 8, LANES), f32),
                pltpu.VMEM((3, 3, 32, LANES), f32),
                pltpu.VMEM((24, LANES), f32),
                pltpu.VMEM((LANES, 2 * LANES), jnp.bfloat16),
                pltpu.VMEM((3 * rows, 2 * LANES), f32),
                pltpu.VMEM((3 * rows, 2 * LANES), f32),
            ],
            compiler_params=pltpu.CompilerParams(
                collective_id=0, has_side_effects=True, vmem_limit_bytes=24 << 20
            ),
            name="riser",
        )(
            *[pltpu.with_memory_space_constraint(x, pltpu.HBM) for x in (velocity,
            speed,
            cbin.reshape(1, sections),
            face,
            weight,
            tension.reshape(1, sections),
            displacement,
            beam_rate)],
        )
        return pl.pallas_call(
            hand_over,
            out_shape=shapes,
            in_specs=[vmem] * 3,
            out_specs=(far,) * 3,
            scratch_shapes=[pltpu.SemaphoreType.DMA((3,))],
            name="results",
        )(*[pltpu.with_memory_space_constraint(x, pltpu.VMEM) for x in results])

    return jax.shard_map(
        local,
        mesh=mesh,
        in_specs=(
            P(None, "sector", None, "span"),
            P(),
            P("span"),
            P("sector"),
            P("sector"),
            P("span"),
            P(None, "span"),
            P(None, "span"),
        ),
        out_specs=(P(None, "sector", None, "span"), P(None, "span"), P(None, "span")),
        check_vma=False,
    )
```
